32 devices in a mesh: user: 4 (over y, x), item: 8 (over z, core).
Axes of the slice: x: 2, y: 2, z: 4, core: 2. Of those that a mesh axis runs over, the one named last changes fastest.
Arguments:
- item_factors: bfloat16 [16384, 256], P('item'), may hold values from -0.125 to 0.125
- item_gram: float32 [256, 256], replicated, as said below
- tile_users: int32 [4, 8, 48], P('user', 'item'), may hold values from 0 to 3
- tile_items: int32 [4, 8, 48], P('user', 'item'), may hold values from 0 to 15, as said below
- tile_counts: int32 [4, 8], P('user', 'item'), may hold values from 12 to 48, as said below
- tile_values: bfloat16 [4, 8, 48, 128, 128], P('user', 'item'), may hold values from 0 to 8
Outputs:
- user_factors: float32 [2048, 256], P(('user', 'item'))
- item_rhs: float32 [8, 2048, 256], P('item', 'user')
The draws below stay inside these ranges and needn't reach their ends.
Inputs may be any that keep to these rules, and one draw needn't show every extreme that they name: `item_gram`: symmetric positive definite. The pairs (tile_users, tile_items) of one device's slots are all different. `tile_counts`: some device uses all 48 slots in every draw.
All inputs are finite; a program needn't handle non-finite values.
Results may differ from the reference program's by a relative error of at most 0.0032.
Values may be sent and summed in bfloat16 or wider, within the bound.
A program may use at most 64 MiB of HBM per device.

```python
import jax
import jax.numpy as jnp
from jax import lax

RANK = 256
TILE = 128
USER_BLK = 4
ITEM_BLK = 16
TILES = 48
ITERS = 3
ITEM_TOTAL = 16384
N_USER = 4
N_ITEM = 8


def draw_item_factors(key, part):
    first, second, third = jax.random.split(jax.random.fold_in(key, 53), 3)
    base = jax.random.normal(first, (ITEM_TOTAL, RANK), jnp.float32) * ITEM_TOTAL ** (-0.5)
    column_slot = jnp.exp(jax.random.uniform(second, (RANK,), jnp.float32, -1.0, 0.5))
    scale_per_row = jnp.exp(jax.random.uniform(third, (ITEM_TOTAL, 1), jnp.float32, jnp.log(0.3), jnp.log(2.0)))
    scale_factor = column_slot[None, :] * scale_per_row / 0.94
    return jnp.clip(base * scale_factor, -0.125, 0.125).astype(jnp.bfloat16)


def draw_item_gram(key, part):
    base = jax.random.normal(key, (RANK, RANK), jnp.float32)
    return 0.5 * jnp.eye(RANK, dtype=jnp.float32) + jnp.dot(base, base.T) / (2 * RANK)


def tile_pairs(key):
    base = jax.random.fold_in(key, 17)
    order = jnp.broadcast_to(jnp.arange(USER_BLK * ITEM_BLK, dtype=jnp.int32), (N_USER * N_ITEM, USER_BLK * ITEM_BLK))
    mixed = jax.random.permutation(base, order, axis=1, independent=True)[:, :TILES]
    return mixed.reshape(N_USER, N_ITEM, TILES).astype(jnp.int32)


def draw_tile_users(key, part):
    return tile_pairs(key) // ITEM_BLK


def draw_tile_items(key, part):
    return tile_pairs(key) % ITEM_BLK


def draw_tile_counts(key, part):
    first, second = jax.random.split(jax.random.fold_in(key, 29))
    ratio = jax.random.randint(first, (N_USER, N_ITEM), 1, 5)
    counts = TILES // ratio
    busiest = jax.random.randint(second, (), 0, N_USER * N_ITEM)
    places = jnp.arange(N_USER * N_ITEM, dtype=jnp.int32).reshape(N_USER, N_ITEM)
    return jnp.where(places == busiest, TILES, counts).astype(jnp.int32)


def draw_tile_values(key, part):
    shape = (N_USER, N_ITEM, TILES, TILE, TILE)
    first, second = jax.random.split(jax.random.fold_in(key, 41))
    keep = jax.random.uniform(first, shape, jnp.float32) < 0.5
    level = jnp.exp(jax.random.uniform(second, shape, jnp.float32, jnp.log(0.5), jnp.log(8.0)))
    return jnp.where(keep, level, 0.0).astype(jnp.bfloat16)


def setup_inputs(seed: int = 0) -> dict:
    arg_keys = jax.random.split(jax.random.key(seed), 7)
    item_factors = draw_item_factors(jax.random.fold_in(arg_keys[6], 71), 0)
    item_gram = draw_item_gram(jax.random.fold_in(arg_keys[6], 71), 0)
    tile_users = draw_tile_users(jax.random.fold_in(arg_keys[6], 71), 0)
    tile_items = draw_tile_items(jax.random.fold_in(arg_keys[6], 71), 0)
    tile_counts = draw_tile_counts(jax.random.fold_in(arg_keys[6], 71), 0)
    tile_values = draw_tile_values(jax.random.fold_in(arg_keys[6], 71), 0)
    return dict(item_factors=item_factors, item_gram=item_gram, tile_users=tile_users, tile_items=tile_items, tile_counts=tile_counts, tile_values=tile_values)


epsilon = 1e-6
highest = lax.Precision.HIGHEST


def confidence_of(tile_vals):
    return jnp.where(tile_vals > 0, 1.0 + tile_vals.astype(jnp.float32), 0.0).astype(jnp.bfloat16)


def chosen_of(block_ids, active, limit):
    return ((block_ids[:, None] == jnp.arange(limit, dtype=jnp.int32)[None, :]) & active[:, None]).astype(jnp.float32)


def reference(item_factors, item_gram, tile_users, tile_items, tile_counts, tile_values):
    block_grid_height = item_factors.reshape(N_ITEM, ITEM_BLK, TILE, RANK)
    active_all = jnp.arange(TILES, dtype=jnp.int32)[None, None, :] < tile_counts[:, :, None]
    group_rows = USER_BLK * TILE

    def user_side(tile_fn):
        def per_group(group):
            def per_owner(running, owner):
                return running + tile_fn(group, owner), None
            total, _ = lax.scan(per_owner, jnp.zeros((USER_BLK, TILE, RANK), jnp.float32), jnp.arange(N_ITEM, dtype=jnp.int32))
            return total
        return lax.map(per_group, jnp.arange(N_USER, dtype=jnp.int32)).reshape(N_USER * group_rows, RANK)

    def rhs_term(group, owner):
        item_rows = jnp.take(block_grid_height[owner], tile_items[group, owner], axis=0).astype(jnp.float32)
        confidence = confidence_of(tile_values[group, owner]).astype(jnp.float32)
        partial_value = jnp.einsum('tui,tir->tur', confidence, item_rows, precision=highest)
        chosen = chosen_of(tile_users[group, owner], active_all[group, owner], USER_BLK)
        return jnp.einsum('tk,tur->kur', chosen, partial_value, precision=highest)

    def apply_tiles(dir_rows):
        def term(group, owner):
            item_rows = jnp.take(block_grid_height[owner], tile_items[group, owner], axis=0).astype(jnp.float32)
            user_rows = jnp.take(dir_rows[group], tile_users[group, owner], axis=0).astype(jnp.float32)
            scores = jnp.einsum('tur,tir->tui', user_rows, item_rows, precision=highest)
            weighted = (scores * tile_values[group, owner].astype(jnp.float32)).astype(jnp.bfloat16)
            weighted = lax.optimization_barrier(weighted).astype(jnp.float32)
            returned = jnp.einsum('tui,tir->tur', weighted, item_rows, precision=highest)
            chosen = chosen_of(tile_users[group, owner], active_all[group, owner], USER_BLK)
            return jnp.einsum('tk,tur->kur', chosen, returned, precision=highest)
        return user_side(term)

    right_side = user_side(rhs_term)
    solution = jnp.zeros_like(right_side)
    residual = right_side
    direction = right_side
    norm_now = jnp.sum(residual * residual, axis=1, keepdims=True)
    for iteration in range(ITERS):
        dir_rows = direction.astype(jnp.bfloat16).reshape(N_USER, USER_BLK, TILE, RANK)
        image = jnp.dot(direction, item_gram, precision=highest) + apply_tiles(dir_rows)
        step_size = norm_now / (jnp.sum(direction * image, axis=1, keepdims=True) + epsilon)
        solution = solution + step_size * direction
        residual = residual - step_size * image
        norm_next = jnp.sum(residual * residual, axis=1, keepdims=True)
        direction = residual + norm_next / (norm_now + epsilon) * direction
        norm_now = norm_next

    closing_rows = solution.astype(jnp.bfloat16).reshape(N_USER, USER_BLK, TILE, RANK)

    def per_owner(owner):
        def per_group(running, group):
            user_rows = jnp.take(closing_rows[group], tile_users[group, owner], axis=0).astype(jnp.float32)
            confidence = confidence_of(tile_values[group, owner]).astype(jnp.float32)
            partial_value = jnp.einsum('tui,tur->tir', confidence, user_rows, precision=highest)
            chosen = chosen_of(tile_items[group, owner], active_all[group, owner], ITEM_BLK)
            return running + jnp.einsum('tk,tir->kir', chosen, partial_value, precision=highest), None
        total, _ = lax.scan(per_group, jnp.zeros((ITEM_BLK, TILE, RANK), jnp.float32), jnp.arange(N_USER, dtype=jnp.int32))
        return total

    item_rhs = lax.map(per_owner, jnp.arange(N_ITEM, dtype=jnp.int32)).reshape(N_ITEM, ITEM_BLK * TILE, RANK)
    item_rhs = item_rhs * (N_USER * group_rows) ** -0.5
    return solution, item_rhs
```

```python
import functools

import jax
import jax.numpy as jnp
from jax import lax
from jax.experimental import pallas as pl
from jax.experimental.pallas import tpu as pltpu
from jax.sharding import PartitionSpec as P

USER_BLK = 4
ITERS = 3
CHUNK = 1024
LAST_CHUNK = 512
STREAMS = 2
LANES = 128

epsilon = 1e-06
highest = lax.Precision.HIGHEST
MESH = pl.DeviceIdType.MESH
NT = (((1,), (1,)), ((), ()))


def confidence_of(w):
    w = w.astype(jnp.float32)
    return jnp.where(w > 0, 1.0 + w, 0.0).astype(jnp.bfloat16)


def kernel(
    nu, ni, scale,
    inv_ref, y_hbm, gram_hbm, tiles_hbm,
    sol_ref, item_ref,
    tiles, yv, gram, wide, ws, wx, ct, xb, pa, ra, own, sb, rb,
    d_state, r_state, x_state, n_state, i_state, a_state, sol_in,
    scal, sums, coef, x2,
    load_sem, w_send, w_recv, a_send, a_recv, y_send, y_recv, b_send, b_recv,
    z_send, z_recv, f_send, f_recv, u_send, u_recv, s_send, s_recv, o_send, o_recv,
    c_send, c_recv, p_send, p_recv,
):
    slots, side, _ = tiles_hbm.shape
    items, rank = y_hbm.shape
    group = wide.shape[0]
    half = group // 2
    rows = group // ni
    nz = ni // 2
    owners = nz // STREAMS
    low = (nz - owners) // 2
    srows = owners * rows
    cols = items // nu
    blocks = items // side
    devices = nu * ni
    per = STREAMS * rows
    g, o = lax.axis_index("user"), lax.axis_index("item")
    z, c = lax.div(o, 2), lax.rem(o, 2)
    other = 1 - c
    me = g * ni + o
    sib = {"item": z * 2 + other}
    place = lax.rem(z - low + nz, owners)
    is_owner = (z >= low) & (z < low + owners)

    def unum(j):
        return lax.rem(g + (j + nu), nu)

    def zpeer(j):
        return {"item": lax.rem(z + (j + nz), nz) * 2 + c}

    def upeer(j):
        return {"user": unum(j)}

    def peer(i):
        return {"user": lax.rem(g + lax.div(i, ni), nu), "item": lax.rem(o + lax.rem(i, ni), ni)}

    def piece(s, q, hh=0):
        at = (hh * STREAMS + s) * srows
        if isinstance(q, int):
            return pl.ds(at + q * rows, rows)
        return pl.ds(pl.multiple_of(at + q * rows, rows), rows)

    sent = []

    def rcopy(src, dst, ss, rs, dev):
        return pltpu.make_async_remote_copy(
            src_ref=src, dst_ref=dst, send_sem=ss, recv_sem=rs, device_id=dev, device_id_type=MESH
        )

    def send(*args):
        cp = rcopy(*args)
        cp.start()
        sent.append((None, cp))

    def send_if(cond, *args):
        cp = rcopy(*args)
        pl.when(cond)(cp.start)
        sent.append((cond, cp))

    def arrived(dst, ss, rs, dev):
        rcopy(dst, dst, ss, rs, dev).wait_recv()

    loads = [
        pltpu.make_async_copy(tiles_hbm, tiles.at[pl.ds(0, slots)], load_sem.at[0]),
        pltpu.make_async_copy(y_hbm, yv.at[0], load_sem.at[1]),
        pltpu.make_async_copy(gram_hbm, gram, load_sem.at[2]),
    ]
    for cp in loads:
        cp.start()

    barrier = pltpu.get_barrier_semaphore()

    def greet(i, carry):
        pl.semaphore_signal(barrier, inc=1, device_id=peer(i), device_id_type=MESH)
        return carry

    lax.fori_loop(1, devices, greet, 0)

    tiles[slots] = jnp.zeros((side, side), jnp.bfloat16)
    loads[0].wait()
    for b in range(blocks):
        for q in range(owners):
            for s in range(STREAMS):
                start = (q * STREAMS + s) * 2 * rows
                u, off = start // side, start % side
                for hh in range(2):
                    to = ((hh * STREAMS + s) * owners + q) * rows
                    at = pl.ds(pl.multiple_of(off + (c if hh == 0 else other) * rows, rows), rows)
                    wide[to : to + rows, b * side : (b + 1) * side] = tiles[
                        slots - inv_ref[u * blocks + b], at, :
                    ]
    for cp in loads[1:]:
        cp.wait()

    def wcol(gg):
        return pl.ds(pl.multiple_of(gg * cols, cols), cols)

    def turn(j):
        if j == 0:
            block = wide[:, wcol(g)]
        else:
            arrived(wx.at[j], w_send.at[j], w_recv.at[j], upeer(-j))
            block = wx[j]
        ct[j] = confidence_of(block).T

    turns = [[], [], [], []]
    for j in range(nu):
        turns[j * 4 // nu].append(j)

    def turn_all(which):
        for j in turns[which]:
            turn(j)

    def rhs_pass(hh):
        here = slice(hh * half, (hh + 1) * half)
        acc = jnp.zeros((half, rank), jnp.float32)
        for i in range(items // CHUNK):
            at = slice(i * CHUNK, (i + 1) * CHUNK)
            acc = acc + jnp.dot(
                confidence_of(wide[here, at]), yv[0, at, :], preferred_element_type=jnp.float32
            )
        return acc

    def stream_pass(k, s):
        here = slice(s * srows, (s + 1) * srows)
        acc = jnp.zeros((srows, rank), jnp.float32)
        for side_of, w_ref in enumerate((wide, ws)):
            for i in range(items // CHUNK):
                at = slice(i * CHUNK, (i + 1) * CHUNK)
                yc = yv[side_of, at, :]
                scores = lax.dot_general(xb[k - 1, 0, here, :], yc, NT, preferred_element_type=jnp.float32)
                weighted = (scores * w_ref[here, at].astype(jnp.float32)).astype(jnp.bfloat16)
                acc = acc + jnp.dot(weighted, yc, preferred_element_type=jnp.float32)
        return acc

    def last_pass():
        acc = jnp.zeros((half, LANES), jnp.float32)
        for side_of, w_ref in enumerate((wide, ws)):
            for i in range(items // LAST_CHUNK):
                at = slice(i * LAST_CHUNK, (i + 1) * LAST_CHUNK)
                scores = lax.dot_general(
                    xb[ITERS - 1, 0, 0:half, :], yv[side_of, at, :], NT, preferred_element_type=jnp.float32
                )
                weighted = (scores * w_ref[0:half, at].astype(jnp.float32)).astype(jnp.bfloat16)
                prod = weighted.astype(jnp.float32) * scores
                for j in range(LAST_CHUNK // LANES):
                    acc = acc + prod[:, j * LANES : (j + 1) * LANES]
        for q in range(owners):
            mine = [acc[(s * owners + q) * rows : (s * owners + q + 1) * rows] for s in range(STREAMS)]
            sums[me, q : q + 1, 0:per] = jnp.sum(jnp.concatenate(mine, axis=0).T, axis=0, keepdims=True)

    def reduce_start(k, s, total):
        own[s] = total
        sb[k, s] = total.astype(jnp.bfloat16)
        for q in range(owners):
            zo = q + low
            j = lax.rem(zo - z + nz, nz)
            part = sb.at[k, s, pl.ds(q * rows, rows)]
            send_if(
                z != zo, part, rb.at[k, s, j], b_send.at[k, s, q], b_recv.at[k, s, j], {"item": zo * 2 + c}
            )

    def reduce_end(k, s):
        total = own[s, pl.ds(pl.multiple_of(place * rows, rows), rows), :]
        for j in range(1, nz):
            arrived(rb.at[k, s, j], b_send.at[k, s, 0], b_recv.at[k, s, j], zpeer(-j))
            total = total + rb[k, s, j].astype(jnp.float32)
        return total

    def gather_send(k, s):
        mine = xb.at[k, 0, piece(s, place)]
        for j in range(1, nz):
            send_if(is_owner, mine, mine, z_send.at[k, s, j], z_recv.at[k, s, place], zpeer(j))

    def gather_end(k, s, pass_on):
        for q in range(owners):
            zo = q + low
            got = xb.at[k, 0, piece(s, q)]

            @pl.when(z != zo)
            def _():
                arrived(got, z_send.at[k, s, 0], z_recv.at[k, s, q], {"item": lax.rem(o + 2, ni)})

            if pass_on:
                for v in range(1, nu):
                    send(got, xb.at[k, v, piece(s, q)], u_send.at[k, v, s, q], u_recv.at[k, v, s, q], upeer(v))
                send(got, xb.at[k, 0, piece(s, q, 1)], f_send.at[k, s, q], f_recv.at[k, s, q], sib)

    mine_all, theirs_all = pl.ds(0, half), pl.ds(half, half)

    def basis_send(k):
        mine = xb.at[k, 0, mine_all]
        for v in range(1, nu):
            send(mine, xb.at[k, v, mine_all], u_send.at[k, v, 0, 0], u_recv.at[k, v, 0, 0], upeer(v))
        send(mine, xb.at[k, 0, theirs_all], f_send.at[k, 0, 0], f_recv.at[k, 0, 0], sib)

    def basis_pass(k):
        for v in range(1, nu):
            got = xb.at[k, v, mine_all]
            arrived(got, u_send.at[k, v, 0, 0], u_recv.at[k, v, 0, 0], upeer(-v))
            send(got, xb.at[k, v, theirs_all], s_send.at[k, v, 0, 0], s_recv.at[k, v, 0, 0], sib)

    def basis_end(k):
        arrived(xb.at[k, 0, theirs_all], f_send.at[k, 0, 0], f_recv.at[k, 0, 0], sib)
        for v in range(1, nu):
            arrived(xb.at[k, v, theirs_all], s_send.at[k, v, 0, 0], s_recv.at[k, v, 0, 0], sib)

    def update(k, s):
        total = reduce_end(k, s)
        if k == 0:
            r_state[s] = total
            d_state[s] = total
            n_state[s] = jnp.sum(total * total, axis=1, keepdims=True)
            xb[k, 0, piece(s, place), :] = total.astype(jnp.bfloat16)
            return
        direction = d_state[s]
        image = i_state[s] + total
        norm = n_state[s]
        alpha = norm / (jnp.sum(direction * image, axis=1, keepdims=True) + epsilon)
        residual = r_state[s] - alpha * image
        norm_next = jnp.sum(residual * residual, axis=1, keepdims=True)
        direction_next = residual + norm_next / (norm + epsilon) * direction
        xb[k, 0, piece(s, place), :] = direction_next.astype(jnp.bfloat16)
        moved = alpha * direction
        x_state[s] = moved if k == 1 else x_state[s] + moved
        a_state[k - 1, s] = alpha
        r_state[s] = residual
        d_state[s] = direction_next
        n_state[s] = norm_next

    def grams():
        for s in range(STREAMS):
            i_state[s] = jnp.dot(
                d_state[s], gram[...], precision=highest, preferred_element_type=jnp.float32
            )

    def spread(src, ss, rs):
        def body(i, carry):
            rcopy(src, src, ss.at[i], rs, peer(i)).start()
            return carry

        lax.fori_loop(1, devices, body, 0)

    def spread_end(src, ss, rs):
        def body(i, carry):
            rcopy(src, src, ss.at[i], rs, peer(i)).wait_send()
            return carry

        lax.fori_loop(1, devices, body, 0)

    my_scal = scal.at[(g * owners + place) * 2 + c]

    def tell():
        grams()
        lane = lax.broadcasted_iota(jnp.int32, (rows, LANES), 1)
        parts = []
        for s in range(STREAMS):
            turned = jnp.sum(d_state[s] * i_state[s], axis=1, keepdims=True)
            at = jnp.where(lane == 2, n_state[s], turned)
            at = jnp.where(lane == 1, a_state[1, s], at)
            parts.append(jnp.where(lane == 0, a_state[0, s], at))
        my_scal[:, 0:per] = jnp.concatenate(parts, axis=0).T[0:8]
        spread(my_scal, c_send, c_recv)

    pa[...] = rhs_pass(1)
    pl.semaphore_wait(barrier, devices - 1)
    for s in range(STREAMS):
        here = pl.ds(s * srows, srows)
        send(pa.at[here], ra.at[here], a_send.at[s], a_recv.at[s], sib)
    first = rhs_pass(0)
    for s in range(STREAMS):
        own[s] = first[s * srows : (s + 1) * srows]
    send(yv.at[0], yv.at[1], y_send.at[0], y_recv.at[0], sib)
    send(wide.at[theirs_all], ws, y_send.at[1], y_recv.at[1], sib)
    for s in range(STREAMS):
        here = pl.ds(s * srows, srows)
        arrived(ra.at[here], a_send.at[s], a_recv.at[s], sib)
        reduce_start(0, s, own[s] + ra[here, :])
    for j in range(1, nu):
        send(wide.at[:, wcol(unum(j))], wx.at[j], w_send.at[j], w_recv.at[j], upeer(j))
    turn_all(0)
    for s in range(STREAMS):
        pl.when(is_owner)(functools.partial(update, 0, s))
        gather_send(0, s)
    arrived(yv.at[1], y_send.at[0], y_recv.at[0], sib)
    arrived(ws, y_send.at[1], y_recv.at[1], sib)

    for k in range(1, ITERS):
        for s in range(STREAMS):
            gather_end(k - 1, s, False)
            reduce_start(k, s, stream_pass(k, s))
        basis_send(k - 1)
        pl.when(is_owner)(grams)
        if k == 1:
            turn_all(1)
        if k == 2:
            basis_pass(0)
        for s in range(STREAMS):
            pl.when(is_owner)(functools.partial(update, k, s))
            gather_send(k, s)

    pl.when(is_owner)(tell)
    for q in range(owners):
        for s in range(STREAMS):
            target = q * STREAMS + s
            if target != q + low:
                send_if(
                    z == q + low, x_state.at[s], sol_in, o_send.at[s], o_recv, {"item": target * 2 + c}
                )
    k = ITERS - 1
    for s in range(STREAMS):
        gather_end(k, s, True)
    last_pass()
    spread(sums.at[me], p_send, p_recv)

    basis_pass(1)
    turn_all(2)
    turn_all(3)
    known = scal.shape[0]

    @pl.when(is_owner)
    def _():
        every = scal.at[pl.ds(0, known - 1)]
        arrived(every, c_send.at[0], c_recv, sib)

    @pl.when(jnp.logical_not(is_owner))
    def _():
        arrived(scal, c_send.at[0], c_recv, sib)

    def cell(v, hh, q):
        return (v * 2 + hh) * owners + q

    def cells():
        for v in range(nu):
            for hh in range(2):
                for q in range(owners):
                    yield v, hh, q, unum(-v), (c if hh == 0 else other)

    def block(v, hh, s, q):
        at = ((hh * STREAMS + s) * owners + q) * rows
        return slice(at, at + rows)

    for v, hh, q, gv, cc in cells():
        n = cell(v, hh, q)
        coef[0:4, n, :] = scal[(gv * owners + q) * 2 + cc][0:4]
    alpha1, alpha2 = coef[0].T, coef[1].T
    for j in range(2):
        basis_end(j)
    for v, hh, q, gv, cc in cells():
        n = cell(v, hh, q)
        for s in range(STREAMS):
            at = block(v, hh, s, q)
            r = slice(s * rows, (s + 1) * rows)
            x2[v, at, :] = alpha1[r, n : n + 1] * xb[0, v, at, :].astype(jnp.float32) + alpha2[
                r, n : n + 1
            ] * xb[1, v, at, :].astype(jnp.float32)

    for v in range(1, nu):
        for s in range(STREAMS):
            for q in range(owners):
                got = xb.at[k, v, piece(s, q)]
                arrived(got, u_send.at[k, v, s, q], u_recv.at[k, v, s, q], upeer(-v))
                send(got, xb.at[k, v, piece(s, q, 1)], s_send.at[k, v, s, q], s_recv.at[k, v, s, q], sib)

    arrived(sums.at[pl.ds(0, devices - 1)], p_send.at[0], p_recv, sib)
    for v, hh, q, gv, cc in cells():
        n = cell(v, hh, q)
        total = coef[3, n : n + 1, :]
        for zz in range(nz):
            total = total + sums[gv * ni + zz * 2 + cc, q : q + 1, :]
        coef[4, n : n + 1, :] = coef[2, n : n + 1, :] / (total + epsilon)
    alpha3 = coef[4].T

    for target in range(nz):
        owner = target // STREAMS + low
        s, q = target % STREAMS, target // STREAMS

        @pl.when(z == target)
        def _():
            if owner == target:
                before = x_state[s]
            else:
                arrived(sol_in, o_send.at[0], o_recv, {"item": owner * 2 + c})
                before = sol_in[...]
            n = cell(0, 0, q)
            sol_ref[...] = before + alpha3[s * rows : (s + 1) * rows, n : n + 1] * xb[
                k, 0, block(0, 0, s, q), :
            ].astype(jnp.float32)

    for v in range(nu):
        total = None
        for hh in range(2):
            parts = []
            for s in range(STREAMS):
                for q in range(owners):
                    if hh == 1:
                        got = xb.at[k, v, piece(s, q, 1)]
                        if v:
                            arrived(got, s_send.at[k, v, s, q], s_recv.at[k, v, s, q], sib)
                        else:
                            arrived(got, f_send.at[k, s, q], f_recv.at[k, s, q], sib)
                    n = cell(v, hh, q)
                    at = block(v, hh, s, q)
                    parts.append(
                        x2[v, at, :]
                        + alpha3[s * rows : (s + 1) * rows, n : n + 1] * xb[k, v, at, :].astype(jnp.float32)
                    )
            final = jnp.concatenate(parts, axis=0).astype(jnp.bfloat16)
            term = jnp.dot(
                ct[v, :, hh * half : (hh + 1) * half], final, preferred_element_type=jnp.float32
            )
            total = term if total is None else total + term
        if v == 0:
            item_ref[...] = total
        elif v < nu - 1:
            item_ref[...] += total
        else:
            item_ref[...] = (item_ref[...] + total) * scale

    for cond, cp in sent:
        if cond is None:
            cp.wait_send()
        else:
            pl.when(cond)(cp.wait_send)
    spread_end(sums.at[me], p_send, p_recv)
    pl.when(is_owner)(functools.partial(spread_end, my_scal, c_send, c_recv))


def place_outputs(sol_in, item_in, sol_out, item_out):
    sol_out[...] = sol_in[...]
    item_out[...] = item_in[...]


def make_local(nu, ni):
    def local(item_factors, item_gram, tile_users, tile_items, tile_counts, tile_values):
        items, rank = item_factors.shape
        slots, side = tile_values.shape[2], tile_values.shape[-1]
        blocks = items // side
        group = USER_BLK * side
        half = group // 2
        rows = group // ni
        nz = ni // 2
        owners = nz // STREAMS
        srows = owners * rows
        cols = items // nu
        at = jnp.arange(slots, dtype=jnp.int32)
        cell = jnp.arange(USER_BLK * blocks, dtype=jnp.int32)[:, None]
        match = (
            (tile_users[0] == cell // blocks) & (tile_items[0] == cell % blocks) & (at[None, :] < tile_counts[0, 0])
        )
        inv = jnp.sum(jnp.where(match, slots - at[None, :], 0), axis=1)
        scale = float(nu * group) ** -0.5
        bf, f4 = jnp.bfloat16, jnp.float32
        dma = pltpu.SemaphoreType.DMA
        vm = pltpu.VMEM
        cells = max(8, nu * 2 * owners)
        anywhere = pl.BlockSpec(memory_space=pl.ANY)
        vmem = pl.BlockSpec(memory_space=pltpu.VMEM)
        sol, item = pl.pallas_call(
            functools.partial(kernel, nu, ni, scale),
            out_shape=(
                jax.ShapeDtypeStruct((rows, rank), f4),
                jax.ShapeDtypeStruct((cols, rank), f4),
            ),
            in_specs=[pl.BlockSpec(memory_space=pltpu.SMEM), anywhere, anywhere, anywhere],
            out_specs=(vmem, vmem),
            scratch_shapes=[
                vm((slots + 1, side, side), bf),
                vm((2, items, rank), bf),
                vm((rank, rank), f4),
                vm((group, items), bf),
                vm((half, items), bf),
                vm((nu, group, cols), bf),
                vm((nu, cols, group), bf),
                vm((ITERS, nu, group, rank), bf),
                vm((half, rank), f4),
                vm((half, rank), f4),
                vm((STREAMS, srows, rank), f4),
                vm((ITERS, STREAMS, srows, rank), bf),
                vm((ITERS, STREAMS, nz, rows, rank), bf),
                vm((STREAMS, rows, rank), f4),
                vm((STREAMS, rows, rank), f4),
                vm((STREAMS, rows, rank), f4),
                vm((STREAMS, rows, 1), f4),
                vm((STREAMS, rows, rank), f4),
                vm((2, STREAMS, rows, 1), f4),
                vm((rows, rank), f4),
                vm((nu * owners * 2, 8, LANES), f4),
                vm((nu * ni, owners, LANES), f4),
                vm((5, cells, LANES), f4),
                vm((nu, group, rank), f4),
                dma((3,)),
                dma((nu,)), dma((nu,)),
                dma((STREAMS,)), dma((STREAMS,)),
                dma((2,)), dma((2,)),
                dma((ITERS, STREAMS, owners)), dma((ITERS, STREAMS, nz)),
                dma((ITERS, STREAMS, nz)), dma((ITERS, STREAMS, owners)),
                dma((ITERS, STREAMS, owners)), dma((ITERS, STREAMS, owners)),
                dma((ITERS, nu, STREAMS, owners)), dma((ITERS, nu, STREAMS, owners)),
                dma((ITERS, nu, STREAMS, owners)), dma((ITERS, nu, STREAMS, owners)),
                dma((STREAMS,)), dma(()),
                dma((nu * ni,)), dma(()), dma((nu * ni,)), dma(()),
            ],
            compiler_params=pltpu.CompilerParams(collective_id=0, has_side_effects=True),
        )(inv, item_factors, item_gram, tile_values.reshape(slots, side, side))
        sol, item = pl.pallas_call(
            place_outputs,
            out_shape=(
                jax.ShapeDtypeStruct((rows, rank), f4),
                jax.ShapeDtypeStruct((cols, rank), f4),
            ),
            in_specs=[vmem, vmem],
            out_specs=(vmem, vmem),
        )(sol, item)
        return sol, item[None]

    return local


def solution(mesh):
    return jax.shard_map(
        make_local(mesh.shape["user"], mesh.shape["item"]),
        mesh=mesh,
        in_specs=(
            P("item", None),
            P(),
            P("user", "item", None),
            P("user", "item", None),
            P("user", "item"),
            P("user", "item", None, None, None),
        ),
        out_specs=(P(("user", "item"), None), P("item", "user", None)),
        check_vma=False,
    )
```

```python
import functools
import math

import jax
import jax.numpy as jnp
from jax import lax
from jax.experimental import pallas as pl
from jax.experimental.pallas import tpu as pltpu
from jax.sharding import PartitionSpec as P

USER_BLK = 4
ITERS = 3
CHUNK = 1024
LAST_CHUNK = 512
STREAMS = 2
LANES = 128

epsilon = 1e-06
highest = lax.Precision.HIGHEST
MESH = pl.DeviceIdType.MESH
NT = (((1,), (1,)), ((), ()))


def confidence_of(w):
    w = w.astype(jnp.float32)
    return jnp.where(w > 0, 1.0 + w, 0.0).astype(jnp.bfloat16)


def kernel(
    nu, ni, scale,
    inv_ref, y_hbm, gram_hbm, tiles_hbm,
    sol_ref, item_ref,
    tiles, yv, gram, wide, ws, turned, ct, xb, pa, ra, own, sb, rb,
    d_state, r_state, x_state, n_state, i_state, a_state, sol_in,
    scal, sums, coef, x2, kept, outgo, income,
    load_sem, w_send, w_recv, a_send, a_recv, y_send, y_recv, b_send, b_recv,
    z_send, z_recv, f_send, f_recv, u_send, u_recv, o_send, o_recv,
    c_send, c_recv, p_send, p_recv, r_send, r_recv,
):
    slots, side, _ = tiles_hbm.shape
    items, rank = y_hbm.shape
    group = wide.shape[0]
    half = group // 2
    rows = group // ni
    nz = ni // 2
    owners = nz // STREAMS
    low = (nz - owners) // 2
    srows = owners * rows
    cols = items // nu
    blocks = items // side
    devices = nu * ni
    per = STREAMS * rows
    g, o = lax.axis_index("user"), lax.axis_index("item")
    z, c = lax.div(o, 2), lax.rem(o, 2)
    other = 1 - c
    sib = {"item": z * 2 + other}
    place = lax.rem(z - low + nz, owners)
    is_owner = (z >= low) & (z < low + owners)

    line = math.isqrt(nu)
    assert line * line == nu
    gx, gy = lax.rem(g, line), lax.div(g, line)

    def grid(x, y):
        return lax.rem(x, line) + line * lax.rem(y, line)

    def unum(i, j):
        return jnp.where(c == 0, grid(gx + i, gy + j), grid(gx + j, gy + i))

    def far(j, size):
        return min(j, size - j)

    zothers = sorted(range(1, nz), key=lambda j: -far(j, nz))

    def zpeer(j):
        return {"item": lax.rem(z + (j + nz), nz) * 2 + c}

    def upeer(i, j=0):
        return {"user": unum(i, j)}

    def peer(i):
        return {"user": lax.rem(g + lax.div(i, ni), nu), "item": lax.rem(o + lax.rem(i, ni), ni)}

    def piece(s, q, hh=0):
        at = (hh * STREAMS + s) * srows
        if isinstance(q, int):
            return pl.ds(at + q * rows, rows)
        return pl.ds(pl.multiple_of(at + q * rows, rows), rows)

    sent = []

    def rcopy(src, dst, ss, rs, dev):
        return pltpu.make_async_remote_copy(
            src_ref=src, dst_ref=dst, send_sem=ss, recv_sem=rs, device_id=dev, device_id_type=MESH
        )

    def send(*args):
        cp = rcopy(*args)
        cp.start()
        sent.append((None, cp))

    def send_if(cond, *args):
        cp = rcopy(*args)
        pl.when(cond)(cp.start)
        sent.append((cond, cp))

    def arrived(dst, ss, rs, dev):
        rcopy(dst, dst, ss, rs, dev).wait_recv()

    loads = [
        pltpu.make_async_copy(tiles_hbm, tiles.at[pl.ds(0, slots)], load_sem.at[0]),
        pltpu.make_async_copy(y_hbm, yv.at[0], load_sem.at[1]),
        pltpu.make_async_copy(gram_hbm, gram, load_sem.at[2]),
    ]
    for cp in loads:
        cp.start()

    barrier = pltpu.get_barrier_semaphore()

    def greet(i, carry):
        pl.semaphore_signal(barrier, inc=1, device_id=peer(i), device_id_type=MESH)
        return carry

    lax.fori_loop(1, devices, greet, 0)

    tiles[slots] = jnp.zeros((side, side), jnp.bfloat16)
    loads[0].wait()
    for b in range(blocks):
        for q in range(owners):
            for s in range(STREAMS):
                start = (q * STREAMS + s) * 2 * rows
                u, off = start // side, start % side
                for hh in range(2):
                    to = ((hh * STREAMS + s) * owners + q) * rows
                    at = pl.ds(pl.multiple_of(off + (c if hh == 0 else other) * rows, rows), rows)
                    wide[to : to + rows, b * side : (b + 1) * side] = tiles[
                        slots - inv_ref[u * blocks + b], at, :
                    ]
    for cp in loads[1:]:
        cp.wait()

    def wcol(gg):
        return pl.ds(pl.multiple_of(gg * cols, cols), cols)

    def turn(i, j):
        to = ct.at[0, j] if i == 0 else turned.at[i - 1, j]
        to[...] = confidence_of(wide[:, wcol(unum(i, j))]).T
        if i:
            rcopy(to, ct.at[i, j], w_send, w_recv, upeer(i)).start()

    def rhs_pass(hh):
        here = slice(hh * half, (hh + 1) * half)
        acc = jnp.zeros((half, rank), jnp.float32)
        for i in range(items // CHUNK):
            at = slice(i * CHUNK, (i + 1) * CHUNK)
            acc = acc + jnp.dot(
                confidence_of(wide[here, at]), yv[0, at, :], preferred_element_type=jnp.float32
            )
        return acc

    def stream_pass(k, s):
        here = slice(s * srows, (s + 1) * srows)
        acc = jnp.zeros((srows, rank), jnp.float32)
        for side_of, w_ref in enumerate((wide, ws)):
            for i in range(items // CHUNK):
                at = slice(i * CHUNK, (i + 1) * CHUNK)
                yc = yv[side_of, at, :]
                scores = lax.dot_general(xb[k - 1, 0, here, :], yc, NT, preferred_element_type=jnp.float32)
                weighted = (scores * w_ref[here, at].astype(jnp.float32)).astype(jnp.bfloat16)
                acc = acc + jnp.dot(weighted, yc, preferred_element_type=jnp.float32)
        return acc

    def last_pass():
        acc = jnp.zeros((half, LANES), jnp.float32)
        for side_of, w_ref in enumerate((wide, ws)):
            for i in range(items // LAST_CHUNK):
                at = slice(i * LAST_CHUNK, (i + 1) * LAST_CHUNK)
                scores = lax.dot_general(
                    xb[ITERS - 1, 0, 0:half, :], yv[side_of, at, :], NT, preferred_element_type=jnp.float32
                )
                weighted = (scores * w_ref[0:half, at].astype(jnp.float32)).astype(jnp.bfloat16)
                prod = weighted.astype(jnp.float32) * scores
                for j in range(LAST_CHUNK // LANES):
                    acc = acc + prod[:, j * LANES : (j + 1) * LANES]
        for q in range(owners):
            mine = [acc[(s * owners + q) * rows : (s * owners + q + 1) * rows] for s in range(STREAMS)]
            sums[o, q : q + 1, 0:per] = jnp.sum(jnp.concatenate(mine, axis=0).T, axis=0, keepdims=True)

    def reduce_start(k, s, total):
        own[s] = total
        sb[k, s] = total.astype(jnp.bfloat16)
        for i in range(owners):
            q = jnp.where(z * 2 < nz, owners - 1 - i, i)
            zo = q + low
            j = lax.rem(zo - z + nz, nz)
            part = sb.at[k, s, pl.ds(pl.multiple_of(q * rows, rows), rows)]
            cp = rcopy(part, rb.at[k, s, j], b_send.at[s, i], b_recv.at[s], {"item": zo * 2 + c})
            pl.when(z != zo)(cp.start)

    def reduce_sent(k, s):
        for i in range(owners):
            zo = jnp.where(z * 2 < nz, owners - 1 - i, i) + low
            part = sb.at[k, s, pl.ds(0, rows)]
            pl.when(z != zo)(rcopy(part, part, b_send.at[s, i], b_recv.at[s], sib).wait_send)

    def reduce_end(k, s):
        total = own[s, pl.ds(pl.multiple_of(place * rows, rows), rows), :]
        arrived(rb.at[k, s, pl.ds(1, nz - 1)], b_send.at[s, 0], b_recv.at[s], sib)
        for j in range(1, nz):
            total = total + rb[k, s, j].astype(jnp.float32)
        return total

    def gather_send(k, s):
        mine = xb.at[k, 0, piece(s, place)]
        for j in zothers:
            rcopy(mine, mine, z_send.at[s], z_recv.at[s, place], zpeer(j)).start()

    def gather_sent(k, s):
        every = rb.at[k, s, pl.ds(1, nz - 1)]
        rcopy(every, every, z_send.at[s], z_recv.at[s, 0], sib).wait_send()

    def gather_end(k, s, pass_on):
        for q in range(owners):
            zo = q + low
            got = xb.at[k, 0, piece(s, q)]

            @pl.when(z != zo)
            def _():
                arrived(got, z_send.at[s], z_recv.at[s, q], sib)

            if pass_on:
                rcopy(got, xb.at[k, 0, piece(s, q, 1)], f_send.at[k], f_recv.at[k], sib).start()
                for i in range(1, line):
                    rcopy(got, xb.at[k, i, piece(s, q)], u_send.at[k], u_recv.at[k], upeer(i)).start()

    mine_all, theirs_all = pl.ds(0, half), pl.ds(half, half)
    away = pl.ds(1, line - 1)

    def basis_send(k):
        mine = xb.at[k, 0, mine_all]
        rcopy(mine, xb.at[k, 0, theirs_all], f_send.at[k], f_recv.at[k], sib).start()

    def basis_pass(k, which=slice(None)):
        arrived(xb.at[k, 0, theirs_all], f_send.at[k], f_recv.at[k], sib)
        for i in range(1, line):
            rcopy(xb.at[k, 0, which], xb.at[k, i, which], u_send.at[k], u_recv.at[k], upeer(i)).start()

    def basis_end(k):
        arrived(xb.at[k, away], u_send.at[k], u_recv.at[k], sib)

    def basis_sent(k):
        mine, got = xb.at[k, 0, mine_all], xb.at[k, away]
        rcopy(mine, mine, f_send.at[k], f_recv.at[k], sib).wait_send()
        rcopy(got, got, u_send.at[k], u_recv.at[k], sib).wait_send()

    def update(k, s):
        total = reduce_end(k, s)
        if k == 0:
            r_state[s] = total
            d_state[s] = total
            n_state[s] = jnp.sum(total * total, axis=1, keepdims=True)
            xb[k, 0, piece(s, place), :] = total.astype(jnp.bfloat16)
            return
        direction = d_state[s]
        image = i_state[s] + total
        norm = n_state[s]
        alpha = norm / (jnp.sum(direction * image, axis=1, keepdims=True) + epsilon)
        residual = r_state[s] - alpha * image
        norm_next = jnp.sum(residual * residual, axis=1, keepdims=True)
        direction_next = residual + norm_next / (norm + epsilon) * direction
        xb[k, 0, piece(s, place), :] = direction_next.astype(jnp.bfloat16)
        moved = alpha * direction
        x_state[s] = moved if k == 1 else x_state[s] + moved
        a_state[k - 1, s] = alpha
        r_state[s] = residual
        d_state[s] = direction_next
        n_state[s] = norm_next

    def grams():
        for s in range(STREAMS):
            i_state[s] = jnp.dot(
                d_state[s], gram[...], precision=highest, preferred_element_type=jnp.float32
            )

    def spread(slot, ss, near, far_off):
        def column(t, carry):
            dev = {"item": lax.rem(o + t, ni)}
            rcopy(slot(0), slot(0), ss, near, dev).start()
            return carry

        lax.fori_loop(1, ni, column, 0)
        for e in range(2):
            for t in range(1, line):
                gg = grid(gx + t, gy) if e == 0 else grid(gx, gy + t)

                def across(zz, carry):
                    dev = {"user": gg, "item": lax.rem(z + zz, nz) * 2 + e}
                    rcopy(slot(0), slot(t), ss, far_off, dev).start()
                    return carry

                lax.fori_loop(0, nz, across, 0)

    def spread_end(every, ss, rs):
        rcopy(every, every, ss, rs, sib).wait_send()

    told = (ni - 1) + 2 * (line - 1) * nz

    def scal_slot(t):
        return scal.at[(t * owners + place) * 2 + c]

    def sums_slot(t):
        return sums.at[(t * nz + z) * 2 + c]

    def tell():
        grams()
        lane = lax.broadcasted_iota(jnp.int32, (rows, LANES), 1)
        parts = []
        for s in range(STREAMS):
            turned = jnp.sum(d_state[s] * i_state[s], axis=1, keepdims=True)
            at = jnp.where(lane == 2, n_state[s], turned)
            at = jnp.where(lane == 1, a_state[1, s], at)
            parts.append(jnp.where(lane == 0, a_state[0, s], at))
        scal[place * 2 + c, :, 0:per] = jnp.concatenate(parts, axis=0).T[0:8]
        spread(scal_slot, c_send, c_recv, c_recv)

    def step(k, s):
        update(k, s)
        gather_send(k, s)

    pa[...] = rhs_pass(1)
    pl.semaphore_wait(barrier, devices - 1)
    send(pa, ra, a_send, a_recv, sib)
    first = rhs_pass(0)
    for s in range(STREAMS):
        own[s] = first[s * srows : (s + 1) * srows]
    send(yv.at[0], yv.at[1], y_send.at[0], y_recv.at[0], sib)
    send(wide.at[theirs_all], ws, y_send.at[1], y_recv.at[1], sib)
    arrived(ra, a_send, a_recv, sib)
    for s in range(STREAMS):
        reduce_start(0, s, own[s] + ra[s * srows : (s + 1) * srows, :])
    for i in range(1, line):
        for j in range(line):
            turn(i, j)
    for s in range(STREAMS):
        pl.when(is_owner)(functools.partial(step, 0, s))
    for j in range(line):
        turn(0, j)
    arrived(yv.at[1], y_send.at[0], y_recv.at[0], sib)
    arrived(ws, y_send.at[1], y_recv.at[1], sib)

    for k in range(1, ITERS):
        for s in range(STREAMS):
            gather_end(k - 1, s, False)
            total = stream_pass(k, s)
            reduce_sent(k - 1, s)
            reduce_start(k, s, total)
        basis_send(k - 1)
        pl.when(is_owner)(grams)
        for s in range(STREAMS):
            pl.when(is_owner)(functools.partial(gather_sent, k - 1, s))
            pl.when(is_owner)(functools.partial(step, k, s))
        basis_pass(k - 1)

    pl.when(is_owner)(tell)
    for q in range(owners):
        for s in range(STREAMS):
            target = q * STREAMS + s
            if target != q + low:
                send_if(
                    z == q + low, x_state.at[s], sol_in, o_send.at[s], o_recv, {"item": target * 2 + c}
                )
    k = ITERS - 1
    for s in range(STREAMS):
        gather_end(k, s, True)
    last_pass()
    spread(sums_slot, p_send, p_recv.at[0], p_recv.at[1])
    basis_pass(k, theirs_all)
    known = line * owners * 2

    @pl.when(is_owner)
    def _():
        arrived(scal.at[pl.ds(0, known - 1)], c_send, c_recv, sib)

    @pl.when(jnp.logical_not(is_owner))
    def _():
        arrived(scal.at[pl.ds(0, known)], c_send, c_recv, sib)

    def cell(v, hh, q):
        return (v * 2 + hh) * owners + q

    def cells(groups):
        for v in groups:
            for hh in range(2):
                for q in range(owners):
                    yield v, hh, q, (c if hh == 0 else other)

    every = range(line)

    def block(v, hh, s, q):
        at = ((hh * STREAMS + s) * owners + q) * rows
        return slice(at, at + rows)

    for v, hh, q, cc in cells(every):
        n = cell(v, hh, q)
        coef[0:4, n, :] = scal[(v * owners + q) * 2 + cc][0:4]
    alpha1, alpha2 = coef[0].T, coef[1].T
    for j in range(k):
        basis_end(j)
    for v, hh, q, cc in cells(every):
        n = cell(v, hh, q)
        for s in range(STREAMS):
            at = block(v, hh, s, q)
            r = slice(s * rows, (s + 1) * rows)
            x2[v, at, :] = alpha1[r, n : n + 1] * xb[0, v, at, :].astype(jnp.float32) + alpha2[
                r, n : n + 1
            ] * xb[1, v, at, :].astype(jnp.float32)

    def alphas(groups):
        for v, hh, q, cc in cells(groups):
            n = cell(v, hh, q)
            total = coef[3, n : n + 1, :]
            for zz in range(nz):
                total = total + sums[(v * nz + zz) * 2 + cc, q : q + 1, :]
            coef[4, n : n + 1, :] = coef[2, n : n + 1, :] / (total + epsilon)
        return coef[4].T

    def final_of(v, alpha):
        parts = []
        for hh in range(2):
            for s in range(STREAMS):
                for q in range(owners):
                    n = cell(v, hh, q)
                    at = block(v, hh, s, q)
                    parts.append(
                        x2[v, at, :]
                        + alpha[s * rows : (s + 1) * rows, n : n + 1] * xb[k, v, at, :].astype(jnp.float32)
                    )
        return jnp.concatenate(parts, axis=0).astype(jnp.bfloat16)

    arrived(sums.at[pl.ds(0, ni - 1)], p_send, p_recv.at[0], sib)
    alpha3 = alphas([0])
    final = final_of(0, alpha3)
    for j in range(line):
        kept[j] = jnp.dot(ct[0, j], final, preferred_element_type=jnp.float32)

    for target in range(nz):
        owner = target // STREAMS + low
        s, q = target % STREAMS, target // STREAMS

        @pl.when(z == target)
        def _():
            if owner == target:
                before = x_state[s]
            else:
                arrived(sol_in, o_send.at[0], o_recv, {"item": owner * 2 + c})
                before = sol_in[...]
            n = cell(0, 0, q)
            sol_ref[...] = before + alpha3[s * rows : (s + 1) * rows, n : n + 1] * xb[
                k, 0, block(0, 0, s, q), :
            ].astype(jnp.float32)

    arrived(sums.at[pl.ds(0, (line - 1) * ni)], p_send, p_recv.at[1], sib)
    alpha3 = alphas(range(1, line))
    arrived(ct.at[away], w_send, w_recv, sib)
    basis_end(k)
    finals = [final_of(v, alpha3) for v in range(1, line)]
    for j in list(range(1, line)) + [0]:
        total = kept[j]
        for v in range(1, line):
            total = total + jnp.dot(ct[v, j], finals[v - 1], preferred_element_type=jnp.float32)
        if j:
            outgo[j - 1] = total.astype(jnp.bfloat16)
            rcopy(outgo.at[j - 1], income.at[j - 1], r_send, r_recv, upeer(0, j)).start()
        else:
            item_ref[...] = total
    arrived(income, r_send, r_recv, sib)
    total = item_ref[...]
    for j in range(line - 1):
        total = total + income[j].astype(jnp.float32)
    item_ref[...] = total * scale

    for cond, cp in sent:
        if cond is None:
            cp.wait_send()
        else:
            pl.when(cond)(cp.wait_send)
    for j in range(ITERS):
        basis_sent(j)
    for s in range(STREAMS):
        reduce_sent(k, s)
        pl.when(is_owner)(functools.partial(gather_sent, k, s))
    rcopy(turned, turned, w_send, w_recv, sib).wait_send()
    spread_end(sums.at[pl.ds(0, told)], p_send, p_recv.at[0])
    pl.when(is_owner)(functools.partial(spread_end, scal.at[pl.ds(0, told)], c_send, c_recv))
    rcopy(outgo, outgo, r_send, r_recv, sib).wait_send()


def place_outputs(sol_in, item_in, sol_out, item_out):
    sol_out[...] = sol_in[...]
    item_out[...] = item_in[...]


def make_local(nu, ni):
    def local(item_factors, item_gram, tile_users, tile_items, tile_counts, tile_values):
        items, rank = item_factors.shape
        slots, side = tile_values.shape[2], tile_values.shape[-1]
        blocks = items // side
        group = USER_BLK * side
        half = group // 2
        rows = group // ni
        nz = ni // 2
        owners = nz // STREAMS
        srows = owners * rows
        cols = items // nu
        at = jnp.arange(slots, dtype=jnp.int32)
        cell = jnp.arange(USER_BLK * blocks, dtype=jnp.int32)[:, None]
        match = (
            (tile_users[0] == cell // blocks) & (tile_items[0] == cell % blocks) & (at[None, :] < tile_counts[0, 0])
        )
        inv = jnp.sum(jnp.where(match, slots - at[None, :], 0), axis=1)
        scale = float(nu * group) ** -0.5
        bf, f4 = jnp.bfloat16, jnp.float32
        dma = pltpu.SemaphoreType.DMA
        vm = pltpu.VMEM
        line = math.isqrt(nu)
        cells = max(8, line * 2 * owners)
        anywhere = pl.BlockSpec(memory_space=pl.ANY)
        vmem = pl.BlockSpec(memory_space=pltpu.VMEM)
        sol, item = pl.pallas_call(
            functools.partial(kernel, nu, ni, scale),
            out_shape=(
                jax.ShapeDtypeStruct((rows, rank), f4),
                jax.ShapeDtypeStruct((cols, rank), f4),
            ),
            in_specs=[pl.BlockSpec(memory_space=pltpu.SMEM), anywhere, anywhere, anywhere],
            out_specs=(vmem, vmem),
            scratch_shapes=[
                vm((slots + 1, side, side), bf),
                vm((2, items, rank), bf),
                vm((rank, rank), f4),
                vm((group, items), bf),
                vm((half, items), bf),
                vm((line - 1, line, cols, group), bf),
                vm((line, line, cols, group), bf),
                vm((ITERS, line, group, rank), bf),
                vm((half, rank), f4),
                vm((half, rank), f4),
                vm((STREAMS, srows, rank), f4),
                vm((ITERS, STREAMS, srows, rank), bf),
                vm((ITERS, STREAMS, nz, rows, rank), bf),
                vm((STREAMS, rows, rank), f4),
                vm((STREAMS, rows, rank), f4),
                vm((STREAMS, rows, rank), f4),
                vm((STREAMS, rows, 1), f4),
                vm((STREAMS, rows, rank), f4),
                vm((2, STREAMS, rows, 1), f4),
                vm((rows, rank), f4),
                vm((line * ni, 8, LANES), f4),
                vm((line * ni, owners, LANES), f4),
                vm((5, cells, LANES), f4),
                vm((line, group, rank), f4),
                vm((line, cols, rank), f4),
                vm((line - 1, cols, rank), bf),
                vm((line - 1, cols, rank), bf),
                dma((3,)),
                dma(()), dma(()),
                dma(()), dma(()),
                dma((2,)), dma((2,)),
                dma((STREAMS, owners)), dma((STREAMS,)),
                dma((STREAMS,)), dma((STREAMS, owners)),
                dma((ITERS,)), dma((ITERS,)),
                dma((ITERS,)), dma((ITERS,)),
                dma((STREAMS,)), dma(()),
                dma(()), dma(()), dma(()), dma((2,)),
                dma(()), dma(()),
            ],
            compiler_params=pltpu.CompilerParams(collective_id=0, has_side_effects=True),
        )(inv, item_factors, item_gram, tile_values.reshape(slots, side, side))
        sol, item = pl.pallas_call(
            place_outputs,
            out_shape=(
                jax.ShapeDtypeStruct((rows, rank), f4),
                jax.ShapeDtypeStruct((cols, rank), f4),
            ),
            in_specs=[vmem, vmem],
            out_specs=(vmem, vmem),
        )(sol, item)
        return sol, item[None]

    return local


def solution(mesh):
    return jax.shard_map(
        make_local(mesh.shape["user"], mesh.shape["item"]),
        mesh=mesh,
        in_specs=(
            P("item", None),
            P(),
            P("user", "item", None),
            P("user", "item", None),
            P("user", "item"),
            P("user", "item", None, None, None),
        ),
        out_specs=(P(("user", "item"), None), P("item", "user", None)),
        check_vma=False,
    )
```

```python
import functools
import math

import jax
import jax.numpy as jnp
from jax import lax
from jax.experimental import pallas as pl
from jax.experimental.pallas import tpu as pltpu
from jax.sharding import PartitionSpec as P

USER_BLK = 4
ITERS = 3
CHUNK = 1024
LAST_CHUNK = 512
STREAMS = 2
LANES = 128

epsilon = 1e-06
highest = lax.Precision.HIGHEST
MESH = pl.DeviceIdType.MESH
NT = (((1,), (1,)), ((), ()))


def confidence_of(w):
    w = w.astype(jnp.float32)
    return jnp.where(w > 0, 1.0 + w, 0.0).astype(jnp.bfloat16)


def kernel(
    nu, ni, scale,
    users_hbm, items_hbm, counts_hbm, y_hbm, gram_hbm, tiles_hbm,
    sol_ref, item_ref,
    users_in, items_in, count_in, slot_of, inv_ref, tiles, yv, gram, wide, ws, turned, ct, xb, pa, ra, own, sb, rb,
    d_state, r_state, x_state, n_state, i_state, a_state, sol_in,
    scal, sums, coef, x2, kept, outgo, income,
    load_sem, w_send, w_recv, a_send, a_recv, y_send, y_recv, b_send, b_recv,
    z_send, z_recv, f_send, f_recv, u_send, u_recv, o_send, o_recv,
    c_send, c_recv, p_send, p_recv, r_send, r_recv,
):
    slots, side, _ = tiles_hbm.shape
    items, rank = y_hbm.shape
    group = wide.shape[0]
    half = group // 2
    rows = group // ni
    nz = ni // 2
    owners = nz // STREAMS
    low = (nz - owners) // 2
    srows = owners * rows
    cols = items // nu
    blocks = items // side
    devices = nu * ni
    per = STREAMS * rows
    g, o = lax.axis_index("user"), lax.axis_index("item")
    z, c = lax.div(o, 2), lax.rem(o, 2)
    other = 1 - c
    sib = {"item": z * 2 + other}
    place = lax.rem(z - low + nz, owners)
    is_owner = (z >= low) & (z < low + owners)

    line = math.isqrt(nu)
    assert line * line == nu
    gx, gy = lax.rem(g, line), lax.div(g, line)

    def grid(x, y):
        return lax.rem(x, line) + line * lax.rem(y, line)

    def unum(i, j):
        return jnp.where(c == 0, grid(gx + i, gy + j), grid(gx + j, gy + i))

    def far(j, size):
        return min(j, size - j)

    zothers = sorted(range(1, nz), key=lambda j: -far(j, nz))

    def zpeer(j):
        return {"item": lax.rem(z + (j + nz), nz) * 2 + c}

    def upeer(i, j=0):
        return {"user": unum(i, j)}

    def peer(i):
        return {"user": lax.rem(g + lax.div(i, ni), nu), "item": lax.rem(o + lax.rem(i, ni), ni)}

    def piece(s, q, hh=0):
        at = (hh * STREAMS + s) * srows
        if isinstance(q, int):
            return pl.ds(at + q * rows, rows)
        return pl.ds(pl.multiple_of(at + q * rows, rows), rows)

    sent = []

    def rcopy(src, dst, ss, rs, dev):
        return pltpu.make_async_remote_copy(
            src_ref=src, dst_ref=dst, send_sem=ss, recv_sem=rs, device_id=dev, device_id_type=MESH
        )

    def send(*args):
        cp = rcopy(*args)
        cp.start()
        sent.append((None, cp))

    def send_if(cond, *args):
        cp = rcopy(*args)
        pl.when(cond)(cp.start)
        sent.append((cond, cp))

    def arrived(dst, ss, rs, dev):
        rcopy(dst, dst, ss, rs, dev).wait_recv()

    loads = [
        pltpu.make_async_copy(tiles_hbm, tiles.at[pl.ds(0, slots)], load_sem.at[0]),
        pltpu.make_async_copy(y_hbm, yv.at[0], load_sem.at[1]),
        pltpu.make_async_copy(gram_hbm, gram, load_sem.at[2]),
    ]
    index = [
        pltpu.make_async_copy(users_hbm, users_in, load_sem.at[3]),
        pltpu.make_async_copy(items_hbm, items_in, load_sem.at[4]),
        pltpu.make_async_copy(counts_hbm, count_in, load_sem.at[5]),
    ]
    for cp in index + loads:
        cp.start()

    barrier = pltpu.get_barrier_semaphore()

    def greet(i, carry):
        pl.semaphore_signal(barrier, inc=1, device_id=peer(i), device_id_type=MESH)
        return carry

    lax.fori_loop(1, devices, greet, 0)

    tiles[slots] = jnp.zeros((side, side), jnp.bfloat16)
    for cp in index:
        cp.wait()
    lane = lax.broadcasted_iota(jnp.int32, (1, slots), 1)
    key = jnp.where(lane < count_in[...], users_in[0] * blocks + items_in[0], -1)
    match = lax.broadcasted_iota(jnp.int32, (LANES, slots), 0) == key
    found = jnp.min(jnp.where(match, lane, slots), axis=1, keepdims=True)
    slot_of[...] = jnp.broadcast_to(found, (LANES, LANES)).T[0:8]
    to_scalar = pltpu.make_async_copy(slot_of, inv_ref, load_sem.at[6])
    to_scalar.start()
    to_scalar.wait()
    loads[0].wait()
    for b in range(blocks):
        for q in range(owners):
            for s in range(STREAMS):
                start = (q * STREAMS + s) * 2 * rows
                u, off = start // side, start % side
                for hh in range(2):
                    to = ((hh * STREAMS + s) * owners + q) * rows
                    at = pl.ds(pl.multiple_of(off + (c if hh == 0 else other) * rows, rows), rows)
                    wide[to : to + rows, b * side : (b + 1) * side] = tiles[
                        inv_ref[0, u * blocks + b], at, :
                    ]
    for cp in loads[1:]:
        cp.wait()

    def wcol(gg):
        return pl.ds(pl.multiple_of(gg * cols, cols), cols)

    def turn(i, j):
        to = ct.at[0, j] if i == 0 else turned.at[i - 1, j]
        to[...] = confidence_of(wide[:, wcol(unum(i, j))]).T
        if i:
            rcopy(to, ct.at[i, j], w_send, w_recv, upeer(i)).start()

    def rhs_pass(hh):
        here = slice(hh * half, (hh + 1) * half)
        acc = jnp.zeros((half, rank), jnp.float32)
        for i in range(items // CHUNK):
            at = slice(i * CHUNK, (i + 1) * CHUNK)
            acc = acc + jnp.dot(
                confidence_of(wide[here, at]), yv[0, at, :], preferred_element_type=jnp.float32
            )
        return acc

    def stream_pass(k, s):
        here = slice(s * srows, (s + 1) * srows)
        acc = jnp.zeros((srows, rank), jnp.float32)
        for side_of, w_ref in enumerate((wide, ws)):
            for i in range(items // CHUNK):
                at = slice(i * CHUNK, (i + 1) * CHUNK)
                yc = yv[side_of, at, :]
                scores = lax.dot_general(xb[k - 1, 0, here, :], yc, NT, preferred_element_type=jnp.float32)
                weighted = (scores * w_ref[here, at].astype(jnp.float32)).astype(jnp.bfloat16)
                acc = acc + jnp.dot(weighted, yc, preferred_element_type=jnp.float32)
        return acc

    def last_pass():
        acc = jnp.zeros((half, LANES), jnp.float32)
        for side_of, w_ref in enumerate((wide, ws)):
            for i in range(items // LAST_CHUNK):
                at = slice(i * LAST_CHUNK, (i + 1) * LAST_CHUNK)
                scores = lax.dot_general(
                    xb[ITERS - 1, 0, 0:half, :], yv[side_of, at, :], NT, preferred_element_type=jnp.float32
                )
                weighted = (scores * w_ref[0:half, at].astype(jnp.float32)).astype(jnp.bfloat16)
                prod = weighted.astype(jnp.float32) * scores
                for j in range(LAST_CHUNK // LANES):
                    acc = acc + prod[:, j * LANES : (j + 1) * LANES]
        for q in range(owners):
            mine = [acc[(s * owners + q) * rows : (s * owners + q + 1) * rows] for s in range(STREAMS)]
            sums[o, q : q + 1, 0:per] = jnp.sum(jnp.concatenate(mine, axis=0).T, axis=0, keepdims=True)

    def reduce_start(k, s, total):
        own[s] = total
        sb[k, s] = total.astype(jnp.bfloat16)
        for i in range(owners):
            q = jnp.where(z * 2 < nz, owners - 1 - i, i)
            zo = q + low
            j = lax.rem(zo - z + nz, nz)
            part = sb.at[k, s, pl.ds(pl.multiple_of(q * rows, rows), rows)]
            cp = rcopy(part, rb.at[k, s, j], b_send.at[s, i], b_recv.at[s], {"item": zo * 2 + c})
            pl.when(z != zo)(cp.start)

    def reduce_sent(k, s):
        for i in range(owners):
            zo = jnp.where(z * 2 < nz, owners - 1 - i, i) + low
            part = sb.at[k, s, pl.ds(0, rows)]
            pl.when(z != zo)(rcopy(part, part, b_send.at[s, i], b_recv.at[s], sib).wait_send)

    def reduce_end(k, s):
        total = own[s, pl.ds(pl.multiple_of(place * rows, rows), rows), :]
        arrived(rb.at[k, s, pl.ds(1, nz - 1)], b_send.at[s, 0], b_recv.at[s], sib)
        for j in range(1, nz):
            total = total + rb[k, s, j].astype(jnp.float32)
        return total

    def gather_send(k, s):
        mine = xb.at[k, 0, piece(s, place)]
        for j in zothers:
            rcopy(mine, mine, z_send.at[s], z_recv.at[s, place], zpeer(j)).start()

    def gather_sent(k, s):
        every = rb.at[k, s, pl.ds(1, nz - 1)]
        rcopy(every, every, z_send.at[s], z_recv.at[s, 0], sib).wait_send()

    def gather_end(k, s, pass_on):
        for q in range(owners):
            zo = q + low
            got = xb.at[k, 0, piece(s, q)]

            @pl.when(z != zo)
            def _():
                arrived(got, z_send.at[s], z_recv.at[s, q], sib)

            if pass_on:
                rcopy(got, xb.at[k, 0, piece(s, q, 1)], f_send.at[k], f_recv.at[k], sib).start()
                for i in range(1, line):
                    rcopy(got, xb.at[k, i, piece(s, q)], u_send.at[k], u_recv.at[k], upeer(i)).start()

    mine_all, theirs_all = pl.ds(0, half), pl.ds(half, half)
    away = pl.ds(1, line - 1)

    def basis_send(k):
        mine = xb.at[k, 0, mine_all]
        rcopy(mine, xb.at[k, 0, theirs_all], f_send.at[k], f_recv.at[k], sib).start()

    def basis_pass(k, which=slice(None)):
        arrived(xb.at[k, 0, theirs_all], f_send.at[k], f_recv.at[k], sib)
        for i in range(1, line):
            rcopy(xb.at[k, 0, which], xb.at[k, i, which], u_send.at[k], u_recv.at[k], upeer(i)).start()

    def basis_end(k):
        arrived(xb.at[k, away], u_send.at[k], u_recv.at[k], sib)

    def basis_sent(k):
        mine, got = xb.at[k, 0, mine_all], xb.at[k, away]
        rcopy(mine, mine, f_send.at[k], f_recv.at[k], sib).wait_send()
        rcopy(got, got, u_send.at[k], u_recv.at[k], sib).wait_send()

    def update(k, s):
        total = reduce_end(k, s)
        if k == 0:
            r_state[s] = total
            d_state[s] = total
            n_state[s] = jnp.sum(total * total, axis=1, keepdims=True)
            xb[k, 0, piece(s, place), :] = total.astype(jnp.bfloat16)
            return
        direction = d_state[s]
        image = i_state[s] + total
        norm = n_state[s]
        alpha = norm / (jnp.sum(direction * image, axis=1, keepdims=True) + epsilon)
        residual = r_state[s] - alpha * image
        norm_next = jnp.sum(residual * residual, axis=1, keepdims=True)
        direction_next = residual + norm_next / (norm + epsilon) * direction
        xb[k, 0, piece(s, place), :] = direction_next.astype(jnp.bfloat16)
        moved = alpha * direction
        x_state[s] = moved if k == 1 else x_state[s] + moved
        a_state[k - 1, s] = alpha
        r_state[s] = residual
        d_state[s] = direction_next
        n_state[s] = norm_next

    def grams():
        for s in range(STREAMS):
            i_state[s] = jnp.dot(
                d_state[s], gram[...], precision=highest, preferred_element_type=jnp.float32
            )

    def spread(slot, ss, near, far_off):
        def column(t, carry):
            dev = {"item": lax.rem(o + t, ni)}
            rcopy(slot(0), slot(0), ss, near, dev).start()
            return carry

        lax.fori_loop(1, ni, column, 0)
        for e in range(2):
            for t in range(1, line):
                gg = grid(gx + t, gy) if e == 0 else grid(gx, gy + t)

                def across(zz, carry):
                    dev = {"user": gg, "item": lax.rem(z + zz, nz) * 2 + e}
                    rcopy(slot(0), slot(t), ss, far_off, dev).start()
                    return carry

                lax.fori_loop(0, nz, across, 0)

    def spread_end(every, ss, rs):
        rcopy(every, every, ss, rs, sib).wait_send()

    told = (ni - 1) + 2 * (line - 1) * nz

    def scal_slot(t):
        return scal.at[(t * owners + place) * 2 + c]

    def sums_slot(t):
        return sums.at[(t * nz + z) * 2 + c]

    def tell():
        grams()
        lane = lax.broadcasted_iota(jnp.int32, (rows, LANES), 1)
        parts = []
        for s in range(STREAMS):
            turned = jnp.sum(d_state[s] * i_state[s], axis=1, keepdims=True)
            at = jnp.where(lane == 2, n_state[s], turned)
            at = jnp.where(lane == 1, a_state[1, s], at)
            parts.append(jnp.where(lane == 0, a_state[0, s], at))
        scal[place * 2 + c, :, 0:per] = jnp.concatenate(parts, axis=0).T[0:8]
        spread(scal_slot, c_send, c_recv, c_recv)

    def step(k, s):
        update(k, s)
        gather_send(k, s)

    pa[...] = rhs_pass(1)
    pl.semaphore_wait(barrier, devices - 1)
    send(pa, ra, a_send, a_recv, sib)
    first = rhs_pass(0)
    for s in range(STREAMS):
        own[s] = first[s * srows : (s + 1) * srows]
    send(yv.at[0], yv.at[1], y_send.at[0], y_recv.at[0], sib)
    send(wide.at[theirs_all], ws, y_send.at[1], y_recv.at[1], sib)
    arrived(ra, a_send, a_recv, sib)
    for s in range(STREAMS):
        reduce_start(0, s, own[s] + ra[s * srows : (s + 1) * srows, :])
    for i in range(1, line):
        for j in range(line):
            turn(i, j)
    for s in range(STREAMS):
        pl.when(is_owner)(functools.partial(step, 0, s))
    for j in range(line):
        turn(0, j)
    arrived(yv.at[1], y_send.at[0], y_recv.at[0], sib)
    arrived(ws, y_send.at[1], y_recv.at[1], sib)

    for k in range(1, ITERS):
        for s in range(STREAMS):
            gather_end(k - 1, s, False)
            total = stream_pass(k, s)
            reduce_sent(k - 1, s)
            reduce_start(k, s, total)
        basis_send(k - 1)
        pl.when(is_owner)(grams)
        for s in range(STREAMS):
            pl.when(is_owner)(functools.partial(gather_sent, k - 1, s))
            pl.when(is_owner)(functools.partial(step, k, s))
        basis_pass(k - 1)

    pl.when(is_owner)(tell)
    for q in range(owners):
        for s in range(STREAMS):
            target = q * STREAMS + s
            if target != q + low:
                send_if(
                    z == q + low, x_state.at[s], sol_in, o_send.at[s], o_recv, {"item": target * 2 + c}
                )
    k = ITERS - 1
    for s in range(STREAMS):
        gather_end(k, s, True)
    last_pass()
    spread(sums_slot, p_send, p_recv.at[0], p_recv.at[1])
    basis_pass(k, theirs_all)
    known = line * owners * 2

    @pl.when(is_owner)
    def _():
        arrived(scal.at[pl.ds(0, known - 1)], c_send, c_recv, sib)

    @pl.when(jnp.logical_not(is_owner))
    def _():
        arrived(scal.at[pl.ds(0, known)], c_send, c_recv, sib)

    def cell(v, hh, q):
        return (v * 2 + hh) * owners + q

    def cells(groups):
        for v in groups:
            for hh in range(2):
                for q in range(owners):
                    yield v, hh, q, (c if hh == 0 else other)

    every = range(line)

    def block(v, hh, s, q):
        at = ((hh * STREAMS + s) * owners + q) * rows
        return slice(at, at + rows)

    for v, hh, q, cc in cells(every):
        n = cell(v, hh, q)
        coef[0:4, n, :] = scal[(v * owners + q) * 2 + cc][0:4]
    alpha1, alpha2 = coef[0].T, coef[1].T
    for j in range(k):
        basis_end(j)
    for v, hh, q, cc in cells(every):
        n = cell(v, hh, q)
        for s in range(STREAMS):
            at = block(v, hh, s, q)
            r = slice(s * rows, (s + 1) * rows)
            x2[v, at, :] = alpha1[r, n : n + 1] * xb[0, v, at, :].astype(jnp.float32) + alpha2[
                r, n : n + 1
            ] * xb[1, v, at, :].astype(jnp.float32)

    def alphas(groups):
        for v, hh, q, cc in cells(groups):
            n = cell(v, hh, q)
            total = coef[3, n : n + 1, :]
            for zz in range(nz):
                total = total + sums[(v * nz + zz) * 2 + cc, q : q + 1, :]
            coef[4, n : n + 1, :] = coef[2, n : n + 1, :] / (total + epsilon)
        return coef[4].T

    def final_of(v, alpha):
        parts = []
        for hh in range(2):
            for s in range(STREAMS):
                for q in range(owners):
                    n = cell(v, hh, q)
                    at = block(v, hh, s, q)
                    parts.append(
                        x2[v, at, :]
                        + alpha[s * rows : (s + 1) * rows, n : n + 1] * xb[k, v, at, :].astype(jnp.float32)
                    )
        return jnp.concatenate(parts, axis=0).astype(jnp.bfloat16)

    arrived(sums.at[pl.ds(0, ni - 1)], p_send, p_recv.at[0], sib)
    alpha3 = alphas([0])
    final = final_of(0, alpha3)
    for j in range(line):
        kept[j] = jnp.dot(ct[0, j], final, preferred_element_type=jnp.float32)

    for target in range(nz):
        owner = target // STREAMS + low
        s, q = target % STREAMS, target // STREAMS

        @pl.when(z == target)
        def _():
            if owner == target:
                before = x_state[s]
            else:
                arrived(sol_in, o_send.at[0], o_recv, {"item": owner * 2 + c})
                before = sol_in[...]
            n = cell(0, 0, q)
            sol_ref[...] = before + alpha3[s * rows : (s + 1) * rows, n : n + 1] * xb[
                k, 0, block(0, 0, s, q), :
            ].astype(jnp.float32)

    arrived(sums.at[pl.ds(0, (line - 1) * ni)], p_send, p_recv.at[1], sib)
    alpha3 = alphas(range(1, line))
    arrived(ct.at[away], w_send, w_recv, sib)
    basis_end(k)
    finals = [final_of(v, alpha3) for v in range(1, line)]
    for j in list(range(1, line)) + [0]:
        total = kept[j]
        for v in range(1, line):
            total = total + jnp.dot(ct[v, j], finals[v - 1], preferred_element_type=jnp.float32)
        if j:
            outgo[j - 1] = total.astype(jnp.bfloat16)
            rcopy(outgo.at[j - 1], income.at[j - 1], r_send, r_recv, upeer(0, j)).start()
        else:
            item_ref[...] = total
    arrived(income, r_send, r_recv, sib)
    total = item_ref[...]
    for j in range(line - 1):
        total = total + income[j].astype(jnp.float32)
    item_ref[...] = total * scale

    for cond, cp in sent:
        if cond is None:
            cp.wait_send()
        else:
            pl.when(cond)(cp.wait_send)
    for j in range(ITERS):
        basis_sent(j)
    for s in range(STREAMS):
        reduce_sent(k, s)
        pl.when(is_owner)(functools.partial(gather_sent, k, s))
    rcopy(turned, turned, w_send, w_recv, sib).wait_send()
    spread_end(sums.at[pl.ds(0, told)], p_send, p_recv.at[0])
    pl.when(is_owner)(functools.partial(spread_end, scal.at[pl.ds(0, told)], c_send, c_recv))
    rcopy(outgo, outgo, r_send, r_recv, sib).wait_send()


def place_outputs(sol_in, item_in, sol_out, item_out, sem):
    copies = [
        pltpu.make_async_copy(item_in, item_out, sem.at[0]),
        pltpu.make_async_copy(sol_in, sol_out, sem.at[1]),
    ]
    for cp in copies:
        cp.start()
    for cp in copies:
        cp.wait()


def make_local(nu, ni):
    def local(item_factors, item_gram, tile_users, tile_items, tile_counts, tile_values):
        items, rank = item_factors.shape
        slots, side = tile_values.shape[2], tile_values.shape[-1]
        blocks = items // side
        group = USER_BLK * side
        half = group // 2
        rows = group // ni
        nz = ni // 2
        owners = nz // STREAMS
        srows = owners * rows
        cols = items // nu
        scale = float(nu * group) ** -0.5
        bf, f4 = jnp.bfloat16, jnp.float32
        dma = pltpu.SemaphoreType.DMA
        vm = pltpu.VMEM
        line = math.isqrt(nu)
        cells = max(8, line * 2 * owners)
        anywhere = pl.BlockSpec(memory_space=pl.ANY)
        vmem = pl.BlockSpec(memory_space=pltpu.VMEM)
        sol, item = pl.pallas_call(
            functools.partial(kernel, nu, ni, scale),
            out_shape=(vm((rows, rank), f4), vm((cols, rank), f4)),
            in_specs=[anywhere] * 6,
            out_specs=(vmem, vmem),
            scratch_shapes=[
                vm((1, 1, slots), jnp.int32),
                vm((1, 1, slots), jnp.int32),
                vm((1, 1), jnp.int32),
                vm((8, LANES), jnp.int32),
                pltpu.SMEM((8, LANES), jnp.int32),
                vm((slots + 1, side, side), bf),
                vm((2, items, rank), bf),
                vm((rank, rank), f4),
                vm((group, items), bf),
                vm((half, items), bf),
                vm((line - 1, line, cols, group), bf),
                vm((line, line, cols, group), bf),
                vm((ITERS, line, group, rank), bf),
                vm((half, rank), f4),
                vm((half, rank), f4),
                vm((STREAMS, srows, rank), f4),
                vm((ITERS, STREAMS, srows, rank), bf),
                vm((ITERS, STREAMS, nz, rows, rank), bf),
                vm((STREAMS, rows, rank), f4),
                vm((STREAMS, rows, rank), f4),
                vm((STREAMS, rows, rank), f4),
                vm((STREAMS, rows, 1), f4),
                vm((STREAMS, rows, rank), f4),
                vm((2, STREAMS, rows, 1), f4),
                vm((rows, rank), f4),
                vm((line * ni, 8, LANES), f4),
                vm((line * ni, owners, LANES), f4),
                vm((5, cells, LANES), f4),
                vm((line, group, rank), f4),
                vm((line, cols, rank), f4),
                vm((line - 1, cols, rank), bf),
                vm((line - 1, cols, rank), bf),
                dma((7,)),
                dma(()), dma(()),
                dma(()), dma(()),
                dma((2,)), dma((2,)),
                dma((STREAMS, owners)), dma((STREAMS,)),
                dma((STREAMS,)), dma((STREAMS, owners)),
                dma((ITERS,)), dma((ITERS,)),
                dma((ITERS,)), dma((ITERS,)),
                dma((STREAMS,)), dma(()),
                dma(()), dma(()), dma(()), dma((2,)),
                dma(()), dma(()),
            ],
            compiler_params=pltpu.CompilerParams(collective_id=0, has_side_effects=True),
        )(tile_users, tile_items, tile_counts, item_factors, item_gram, tile_values.reshape(slots, side, side))
        sol = pltpu.with_memory_space_constraint(sol, pltpu.VMEM)
        item = pltpu.with_memory_space_constraint(item, pltpu.VMEM)
        sol, item = pl.pallas_call(
            place_outputs,
            out_shape=(
                jax.ShapeDtypeStruct((rows, rank), f4),
                jax.ShapeDtypeStruct((cols, rank), f4),
            ),
            in_specs=[vmem, vmem],
            out_specs=(anywhere, anywhere),
            scratch_shapes=[dma((2,))],
        )(sol, item)
        return sol, item[None]

    return local


def solution(mesh):
    return jax.shard_map(
        make_local(mesh.shape["user"], mesh.shape["item"]),
        mesh=mesh,
        in_specs=(
            P("item", None),
            P(),
            P("user", "item", None),
            P("user", "item", None),
            P("user", "item"),
            P("user", "item", None, None, None),
        ),
        out_specs=(P(("user", "item"), None), P("item", "user", None)),
        check_vma=False,
    )
```

```python
import functools
import math

import jax
import jax.numpy as jnp
from jax import lax
from jax.experimental import pallas as pl
from jax.experimental.pallas import tpu as pltpu
from jax.sharding import PartitionSpec as P

USER_BLK = 4
ITERS = 3
CHUNK = 1024
LAST_CHUNK = 512
STREAMS = 2
LANES = 128

epsilon = 1e-06
highest = lax.Precision.HIGHEST
MESH = pl.DeviceIdType.MESH
NT = (((1,), (1,)), ((), ()))


def confidence_of(w):
    w = w.astype(jnp.float32)
    return jnp.where(w > 0, 1.0 + w, 0.0).astype(jnp.bfloat16)


def kernel(
    nu, ni, scale,
    users_hbm, items_hbm, counts_hbm, y_hbm, gram_hbm, tiles_hbm,
    sol_ref, item_ref,
    users_in, items_in, count_in, slot_of, inv_ref, tiles, yv, gram, wide, ws, turned, ct, xb, pa, ra, own, sb, rb, dn,
    d_state, r_state, x_state, n_state, i_state, a_state, sol_in,
    scal, sums, coef, x2, kept, outgo, income,
    load_sem, w_send, w_recv, a_send, a_recv, y_send, y_recv, b_send, b_recv,
    z_send, z_recv, f_send, f_recv, u_send, u_recv, o_send, o_recv,
    c_send, c_recv, p_send, p_recv, r_send, r_recv,
):
    slots, side, _ = tiles_hbm.shape
    items, rank = y_hbm.shape
    group = wide.shape[0]
    half = group // 2
    rows = group // ni
    nz = ni // 2
    owners = nz // STREAMS
    low = (nz - owners) // 2
    srows = owners * rows
    cols = items // nu
    blocks = items // side
    devices = nu * ni
    per = STREAMS * rows
    g, o = lax.axis_index("user"), lax.axis_index("item")
    z, c = lax.div(o, 2), lax.rem(o, 2)
    other = 1 - c
    sib = {"item": z * 2 + other}
    place = lax.rem(z - low + nz, owners)
    is_owner = (z >= low) & (z < low + owners)

    line = math.isqrt(nu)
    assert line * line == nu
    gx, gy = lax.rem(g, line), lax.div(g, line)

    def grid(x, y):
        return lax.rem(x, line) + line * lax.rem(y, line)

    def unum(i, j):
        return jnp.where(c == 0, grid(gx + i, gy + j), grid(gx + j, gy + i))

    def far(j, size):
        return min(j, size - j)

    zothers = sorted(range(1, nz), key=lambda j: -far(j, nz))

    def zpeer(j):
        return {"item": lax.rem(z + (j + nz), nz) * 2 + c}

    def upeer(i, j=0):
        return {"user": unum(i, j)}

    def peer(i):
        return {"user": lax.rem(g + lax.div(i, ni), nu), "item": lax.rem(o + lax.rem(i, ni), ni)}

    def piece(s, q, hh=0):
        at = (hh * STREAMS + s) * srows
        if isinstance(q, int):
            return pl.ds(at + q * rows, rows)
        return pl.ds(pl.multiple_of(at + q * rows, rows), rows)

    sent = []

    def rcopy(src, dst, ss, rs, dev):
        return pltpu.make_async_remote_copy(
            src_ref=src, dst_ref=dst, send_sem=ss, recv_sem=rs, device_id=dev, device_id_type=MESH
        )

    def send(*args):
        cp = rcopy(*args)
        cp.start()
        sent.append((None, cp))

    def send_if(cond, *args):
        cp = rcopy(*args)
        pl.when(cond)(cp.start)
        sent.append((cond, cp))

    def arrived(dst, ss, rs, dev):
        rcopy(dst, dst, ss, rs, dev).wait_recv()

    loads = [
        pltpu.make_async_copy(tiles_hbm, tiles.at[pl.ds(0, slots)], load_sem.at[0]),
        pltpu.make_async_copy(y_hbm, yv.at[0], load_sem.at[1]),
        pltpu.make_async_copy(gram_hbm, gram, load_sem.at[2]),
    ]
    index = [
        pltpu.make_async_copy(users_hbm, users_in, load_sem.at[3]),
        pltpu.make_async_copy(items_hbm, items_in, load_sem.at[4]),
        pltpu.make_async_copy(counts_hbm, count_in, load_sem.at[5]),
    ]
    for cp in index + loads:
        cp.start()

    barrier = pltpu.get_barrier_semaphore()

    def greet(i, carry):
        pl.semaphore_signal(barrier, inc=1, device_id=peer(i), device_id_type=MESH)
        return carry

    lax.fori_loop(1, devices, greet, 0)

    tiles[slots] = jnp.zeros((side, side), jnp.bfloat16)
    for cp in index:
        cp.wait()
    lane = lax.broadcasted_iota(jnp.int32, (1, slots), 1)
    key = jnp.where(lane < count_in[...], users_in[0] * blocks + items_in[0], -1)
    match = lax.broadcasted_iota(jnp.int32, (LANES, slots), 0) == key
    found = jnp.min(jnp.where(match, lane, slots), axis=1, keepdims=True)
    slot_of[...] = jnp.broadcast_to(found, (LANES, LANES)).T[0:8]
    to_scalar = pltpu.make_async_copy(slot_of, inv_ref, load_sem.at[6])
    to_scalar.start()
    to_scalar.wait()
    loads[0].wait()
    for b in range(blocks):
        for q in range(owners):
            for s in range(STREAMS):
                start = (q * STREAMS + s) * 2 * rows
                u, off = start // side, start % side
                for hh in range(2):
                    to = ((hh * STREAMS + s) * owners + q) * rows
                    at = pl.ds(pl.multiple_of(off + (c if hh == 0 else other) * rows, rows), rows)
                    wide[to : to + rows, b * side : (b + 1) * side] = tiles[
                        inv_ref[0, u * blocks + b], at, :
                    ]
    for cp in loads[1:]:
        cp.wait()

    def wcol(gg):
        return pl.ds(pl.multiple_of(gg * cols, cols), cols)

    def turn(i, j):
        to = ct.at[0, j] if i == 0 else turned.at[i - 1, j]
        to[...] = confidence_of(wide[:, wcol(unum(i, j))]).T
        if i:
            rcopy(to, ct.at[i, j], w_send, w_recv, upeer(i)).start()

    def rhs_pass(hh):
        here = slice(hh * half, (hh + 1) * half)
        acc = jnp.zeros((half, rank), jnp.float32)
        for i in range(items // CHUNK):
            at = slice(i * CHUNK, (i + 1) * CHUNK)
            acc = acc + jnp.dot(
                confidence_of(wide[here, at]), yv[0, at, :], preferred_element_type=jnp.float32
            )
        return acc

    def stream_pass(k, s):
        here = slice(s * srows, (s + 1) * srows)
        acc = jnp.zeros((srows, rank), jnp.float32)
        for side_of, w_ref in enumerate((wide, ws)):
            for i in range(items // CHUNK):
                at = slice(i * CHUNK, (i + 1) * CHUNK)
                yc = yv[side_of, at, :]
                scores = lax.dot_general(xb[k - 1, 0, here, :], yc, NT, preferred_element_type=jnp.float32)
                weighted = (scores * w_ref[here, at].astype(jnp.float32)).astype(jnp.bfloat16)
                acc = acc + jnp.dot(weighted, yc, preferred_element_type=jnp.float32)
        return acc

    def last_pass():
        acc = jnp.zeros((half, LANES), jnp.float32)
        for side_of, w_ref in enumerate((wide, ws)):
            for i in range(items // LAST_CHUNK):
                at = slice(i * LAST_CHUNK, (i + 1) * LAST_CHUNK)
                scores = lax.dot_general(
                    xb[ITERS - 1, 0, 0:half, :], yv[side_of, at, :], NT, preferred_element_type=jnp.float32
                )
                weighted = (scores * w_ref[0:half, at].astype(jnp.float32)).astype(jnp.bfloat16)
                prod = weighted.astype(jnp.float32) * scores
                for j in range(LAST_CHUNK // LANES):
                    acc = acc + prod[:, j * LANES : (j + 1) * LANES]
        for q in range(owners):
            mine = [acc[(s * owners + q) * rows : (s * owners + q + 1) * rows] for s in range(STREAMS)]
            sums[o, q : q + 1, 0:per] = jnp.sum(jnp.concatenate(mine, axis=0).T, axis=0, keepdims=True)

    def owner_device(zo):
        return {"item": zo * 2 + other}

    def reduce_start(k, s, total):
        sb[k, s] = total.astype(jnp.bfloat16)
        for i in range(owners):
            q = jnp.where(z * 2 < nz, owners - 1 - i, i)
            zo = q + low
            part = sb.at[k, s, pl.ds(pl.multiple_of(q * rows, rows), rows)]
            rcopy(part, rb.at[k, s, lax.rem(zo - z + nz, nz)], b_send.at[s], b_recv.at[s], owner_device(zo)).start()

    def reduce_sent(k, s):
        rcopy(sb.at[k, s], sb.at[k, s], b_send.at[s], b_recv.at[s], sib).wait_send()

    def reduce_end(k, s):
        arrived(rb.at[k, s], b_send.at[s], b_recv.at[s], sib)
        total = rb[k, s, 0].astype(jnp.float32)
        for j in range(1, nz):
            total = total + rb[k, s, j].astype(jnp.float32)
        return total

    def gather_send(k, s):
        for j in zothers + [0]:
            rcopy(
                dn.at[k, s], xb.at[k, 0, piece(s, place)], z_send.at[s], z_recv.at[s, place],
                owner_device(lax.rem(z + j, nz)),
            ).start()

    def gather_sent(k, s):
        rcopy(rb.at[k, s], rb.at[k, s], z_send.at[s], z_recv.at[s, 0], sib).wait_send()

    def gather_end(k, s, pass_on):
        for q in range(owners):
            got = xb.at[k, 0, piece(s, q)]
            arrived(got, z_send.at[s], z_recv.at[s, q], sib)
            if pass_on:
                rcopy(got, xb.at[k, 0, piece(s, q, 1)], f_send.at[k], f_recv.at[k], sib).start()
                for i in range(1, line):
                    rcopy(got, xb.at[k, i, piece(s, q)], u_send.at[k], u_recv.at[k], upeer(i)).start()

    mine_all, theirs_all = pl.ds(0, half), pl.ds(half, half)
    away = pl.ds(1, line - 1)

    def basis_send(k):
        mine = xb.at[k, 0, mine_all]
        rcopy(mine, xb.at[k, 0, theirs_all], f_send.at[k], f_recv.at[k], sib).start()

    def basis_pass(k, which=slice(None)):
        arrived(xb.at[k, 0, theirs_all], f_send.at[k], f_recv.at[k], sib)
        for i in range(1, line):
            rcopy(xb.at[k, 0, which], xb.at[k, i, which], u_send.at[k], u_recv.at[k], upeer(i)).start()

    def basis_end(k):
        arrived(xb.at[k, away], u_send.at[k], u_recv.at[k], sib)

    def basis_sent(k):
        mine, got = xb.at[k, 0, mine_all], xb.at[k, away]
        rcopy(mine, mine, f_send.at[k], f_recv.at[k], sib).wait_send()
        rcopy(got, got, u_send.at[k], u_recv.at[k], sib).wait_send()

    def update(k, s):
        total = reduce_end(k, s)
        if k == 0:
            r_state[s] = total
            d_state[s] = total
            n_state[s] = jnp.sum(total * total, axis=1, keepdims=True)
            dn[k, s] = total.astype(jnp.bfloat16)
            return
        direction = d_state[s]
        image = i_state[s] + total
        norm = n_state[s]
        alpha = norm / (jnp.sum(direction * image, axis=1, keepdims=True) + epsilon)
        residual = r_state[s] - alpha * image
        norm_next = jnp.sum(residual * residual, axis=1, keepdims=True)
        direction_next = residual + norm_next / (norm + epsilon) * direction
        dn[k, s] = direction_next.astype(jnp.bfloat16)
        moved = alpha * direction
        x_state[s] = moved if k == 1 else x_state[s] + moved
        a_state[k - 1, s] = alpha
        r_state[s] = residual
        d_state[s] = direction_next
        n_state[s] = norm_next

    def grams():
        for s in range(STREAMS):
            i_state[s] = jnp.dot(
                d_state[s], gram[...], precision=highest, preferred_element_type=jnp.float32
            )

    def spread(slot, ss, near, far_off):
        def column(t, carry):
            dev = {"item": lax.rem(o + t, ni)}
            rcopy(slot(0), slot(0), ss, near, dev).start()
            return carry

        lax.fori_loop(1, ni, column, 0)
        for e in range(2):
            for t in range(1, line):
                gg = grid(gx + t, gy) if e == 0 else grid(gx, gy + t)

                def across(zz, carry):
                    dev = {"user": gg, "item": lax.rem(z + zz, nz) * 2 + e}
                    rcopy(slot(0), slot(t), ss, far_off, dev).start()
                    return carry

                lax.fori_loop(0, nz, across, 0)

    def spread_end(every, ss, rs):
        rcopy(every, every, ss, rs, sib).wait_send()

    told = (ni - 1) + 2 * (line - 1) * nz

    def scal_slot(t):
        return scal.at[(t * owners + place) * 2 + other]

    def sums_slot(t):
        return sums.at[(t * nz + z) * 2 + c]

    def tell():
        grams()
        lane = lax.broadcasted_iota(jnp.int32, (rows, LANES), 1)
        parts = []
        for s in range(STREAMS):
            turned = jnp.sum(d_state[s] * i_state[s], axis=1, keepdims=True)
            at = jnp.where(lane == 2, n_state[s], turned)
            at = jnp.where(lane == 1, a_state[1, s], at)
            parts.append(jnp.where(lane == 0, a_state[0, s], at))
        scal[place * 2 + other, :, 0:per] = jnp.concatenate(parts, axis=0).T[0:8]
        spread(scal_slot, c_send, c_recv, c_recv)

    def step(k, s):
        update(k, s)
        gather_send(k, s)

    pa[...] = rhs_pass(1)
    pl.semaphore_wait(barrier, devices - 1)
    send(pa, ra, a_send, a_recv, sib)
    first = rhs_pass(0)
    for s in range(STREAMS):
        own[s] = first[s * srows : (s + 1) * srows]
    send(yv.at[0], yv.at[1], y_send.at[0], y_recv.at[0], sib)
    send(wide.at[theirs_all], ws, y_send.at[1], y_recv.at[1], sib)
    arrived(ra, a_send, a_recv, sib)
    for s in range(STREAMS):
        reduce_start(0, s, own[s] + ra[s * srows : (s + 1) * srows, :])
    for i in range(1, line):
        for j in range(line):
            turn(i, j)
    for s in range(STREAMS):
        pl.when(is_owner)(functools.partial(step, 0, s))
    for j in range(line):
        turn(0, j)
    arrived(yv.at[1], y_send.at[0], y_recv.at[0], sib)
    arrived(ws, y_send.at[1], y_recv.at[1], sib)

    for k in range(1, ITERS):
        for s in range(STREAMS):
            gather_end(k - 1, s, False)
            total = stream_pass(k, s)
            reduce_sent(k - 1, s)
            reduce_start(k, s, total)
        basis_send(k - 1)
        pl.when(is_owner)(grams)
        for s in range(STREAMS):
            pl.when(is_owner)(functools.partial(gather_sent, k - 1, s))
            pl.when(is_owner)(functools.partial(step, k, s))
        basis_pass(k - 1)

    pl.when(is_owner)(tell)
    for s in range(STREAMS):
        send_if(is_owner, x_state.at[s], sol_in, o_send.at[s], o_recv, owner_device(place * STREAMS + s))
    k = ITERS - 1
    for s in range(STREAMS):
        gather_end(k, s, True)
    last_pass()
    spread(sums_slot, p_send, p_recv.at[0], p_recv.at[1])
    basis_pass(k, theirs_all)
    known = line * owners * 2

    @pl.when(is_owner)
    def _():
        arrived(scal.at[pl.ds(0, known - 1)], c_send, c_recv, sib)

    @pl.when(jnp.logical_not(is_owner))
    def _():
        arrived(scal.at[pl.ds(0, known)], c_send, c_recv, sib)

    def cell(v, hh, q):
        return (v * 2 + hh) * owners + q

    def cells(groups):
        for v in groups:
            for hh in range(2):
                for q in range(owners):
                    yield v, hh, q, (c if hh == 0 else other)

    every = range(line)

    def block(v, hh, s, q):
        at = ((hh * STREAMS + s) * owners + q) * rows
        return slice(at, at + rows)

    for v, hh, q, cc in cells(every):
        n = cell(v, hh, q)
        coef[0:4, n, :] = scal[(v * owners + q) * 2 + cc][0:4]
    alpha1, alpha2 = coef[0].T, coef[1].T
    for j in range(k):
        basis_end(j)
    for v, hh, q, cc in cells(every):
        n = cell(v, hh, q)
        for s in range(STREAMS):
            at = block(v, hh, s, q)
            r = slice(s * rows, (s + 1) * rows)
            x2[v, at, :] = alpha1[r, n : n + 1] * xb[0, v, at, :].astype(jnp.float32) + alpha2[
                r, n : n + 1
            ] * xb[1, v, at, :].astype(jnp.float32)

    def alphas(groups):
        for v, hh, q, cc in cells(groups):
            n = cell(v, hh, q)
            total = coef[3, n : n + 1, :]
            for zz in range(nz):
                total = total + sums[(v * nz + zz) * 2 + cc, q : q + 1, :]
            coef[4, n : n + 1, :] = coef[2, n : n + 1, :] / (total + epsilon)
        return coef[4].T

    def final_of(v, alpha):
        parts = []
        for hh in range(2):
            for s in range(STREAMS):
                for q in range(owners):
                    n = cell(v, hh, q)
                    at = block(v, hh, s, q)
                    parts.append(
                        x2[v, at, :]
                        + alpha[s * rows : (s + 1) * rows, n : n + 1] * xb[k, v, at, :].astype(jnp.float32)
                    )
        return jnp.concatenate(parts, axis=0).astype(jnp.bfloat16)

    arrived(sums.at[pl.ds(0, ni - 1)], p_send, p_recv.at[0], sib)
    alpha3 = alphas([0])
    final = final_of(0, alpha3)
    for j in range(line):
        kept[j] = jnp.dot(ct[0, j], final, preferred_element_type=jnp.float32)

    arrived(sol_in, o_send.at[0], o_recv, sib)
    for target in range(nz):
        s, q = target % STREAMS, target // STREAMS

        @pl.when(z == target)
        def _():
            n = cell(0, 0, q)
            sol_ref[...] = sol_in[...] + alpha3[s * rows : (s + 1) * rows, n : n + 1] * xb[
                k, 0, block(0, 0, s, q), :
            ].astype(jnp.float32)

    arrived(sums.at[pl.ds(0, (line - 1) * ni)], p_send, p_recv.at[1], sib)
    alpha3 = alphas(range(1, line))
    arrived(ct.at[away], w_send, w_recv, sib)
    basis_end(k)
    finals = [final_of(v, alpha3) for v in range(1, line)]
    for j in list(range(1, line)) + [0]:
        total = kept[j]
        for v in range(1, line):
            total = total + jnp.dot(ct[v, j], finals[v - 1], preferred_element_type=jnp.float32)
        if j:
            outgo[j - 1] = total.astype(jnp.bfloat16)
            rcopy(outgo.at[j - 1], income.at[j - 1], r_send, r_recv, upeer(0, j)).start()
        else:
            item_ref[...] = total
    arrived(income, r_send, r_recv, sib)
    total = item_ref[...]
    for j in range(line - 1):
        total = total + income[j].astype(jnp.float32)
    item_ref[...] = total * scale

    for cond, cp in sent:
        if cond is None:
            cp.wait_send()
        else:
            pl.when(cond)(cp.wait_send)
    for j in range(ITERS):
        basis_sent(j)
    for s in range(STREAMS):
        reduce_sent(k, s)
        pl.when(is_owner)(functools.partial(gather_sent, k, s))
    rcopy(turned, turned, w_send, w_recv, sib).wait_send()
    spread_end(sums.at[pl.ds(0, told)], p_send, p_recv.at[0])
    pl.when(is_owner)(functools.partial(spread_end, scal.at[pl.ds(0, told)], c_send, c_recv))
    rcopy(outgo, outgo, r_send, r_recv, sib).wait_send()


def place_outputs(sol_in, item_in, sol_out, item_out, sem):
    copies = [
        pltpu.make_async_copy(item_in, item_out, sem.at[0]),
        pltpu.make_async_copy(sol_in, sol_out, sem.at[1]),
    ]
    for cp in copies:
        cp.start()
    for cp in copies:
        cp.wait()


def make_local(nu, ni):
    def local(item_factors, item_gram, tile_users, tile_items, tile_counts, tile_values):
        items, rank = item_factors.shape
        slots, side = tile_values.shape[2], tile_values.shape[-1]
        blocks = items // side
        group = USER_BLK * side
        half = group // 2
        rows = group // ni
        nz = ni // 2
        owners = nz // STREAMS
        srows = owners * rows
        cols = items // nu
        scale = float(nu * group) ** -0.5
        bf, f4 = jnp.bfloat16, jnp.float32
        dma = pltpu.SemaphoreType.DMA
        vm = pltpu.VMEM
        line = math.isqrt(nu)
        cells = max(8, line * 2 * owners)
        anywhere = pl.BlockSpec(memory_space=pl.ANY)
        vmem = pl.BlockSpec(memory_space=pltpu.VMEM)
        sol, item = pl.pallas_call(
            functools.partial(kernel, nu, ni, scale),
            out_shape=(vm((rows, rank), f4), vm((cols, rank), f4)),
            in_specs=[anywhere] * 6,
            out_specs=(vmem, vmem),
            scratch_shapes=[
                vm((1, 1, slots), jnp.int32),
                vm((1, 1, slots), jnp.int32),
                vm((1, 1), jnp.int32),
                vm((8, LANES), jnp.int32),
                pltpu.SMEM((8, LANES), jnp.int32),
                vm((slots + 1, side, side), bf),
                vm((2, items, rank), bf),
                vm((rank, rank), f4),
                vm((group, items), bf),
                vm((half, items), bf),
                vm((line - 1, line, cols, group), bf),
                vm((line, line, cols, group), bf),
                vm((ITERS, line, group, rank), bf),
                vm((half, rank), f4),
                vm((half, rank), f4),
                vm((STREAMS, srows, rank), f4),
                vm((ITERS, STREAMS, srows, rank), bf),
                vm((ITERS, STREAMS, nz, rows, rank), bf),
                vm((ITERS, STREAMS, rows, rank), bf),
                vm((STREAMS, rows, rank), f4),
                vm((STREAMS, rows, rank), f4),
                vm((STREAMS, rows, rank), f4),
                vm((STREAMS, rows, 1), f4),
                vm((STREAMS, rows, rank), f4),
                vm((2, STREAMS, rows, 1), f4),
                vm((rows, rank), f4),
                vm((line * ni, 8, LANES), f4),
                vm((line * ni, owners, LANES), f4),
                vm((5, cells, LANES), f4),
                vm((line, group, rank), f4),
                vm((line, cols, rank), f4),
                vm((line - 1, cols, rank), bf),
                vm((line - 1, cols, rank), bf),
                dma((7,)),
                dma(()), dma(()),
                dma(()), dma(()),
                dma((2,)), dma((2,)),
                dma((STREAMS,)), dma((STREAMS,)),
                dma((STREAMS,)), dma((STREAMS, owners)),
                dma((ITERS,)), dma((ITERS,)),
                dma((ITERS,)), dma((ITERS,)),
                dma((STREAMS,)), dma(()),
                dma(()), dma(()), dma(()), dma((2,)),
                dma(()), dma(()),
            ],
            compiler_params=pltpu.CompilerParams(collective_id=0, has_side_effects=True),
        )(tile_users, tile_items, tile_counts, item_factors, item_gram, tile_values.reshape(slots, side, side))
        sol = pltpu.with_memory_space_constraint(sol, pltpu.VMEM)
        item = pltpu.with_memory_space_constraint(item, pltpu.VMEM)
        sol, item = pl.pallas_call(
            place_outputs,
            out_shape=(
                jax.ShapeDtypeStruct((rows, rank), f4),
                jax.ShapeDtypeStruct((cols, rank), f4),
            ),
            in_specs=[vmem, vmem],
            out_specs=(anywhere, anywhere),
            scratch_shapes=[dma((2,))],
        )(sol, item)
        return sol, item[None]

    return local


def solution(mesh):
    return jax.shard_map(
        make_local(mesh.shape["user"], mesh.shape["item"]),
        mesh=mesh,
        in_specs=(
            P("item", None),
            P(),
            P("user", "item", None),
            P("user", "item", None),
            P("user", "item"),
            P("user", "item", None, None, None),
        ),
        out_specs=(P(("user", "item"), None), P("item", "user", None)),
        check_vma=False,
    )
```

```python
import functools
import math

import jax
import jax.numpy as jnp
from jax import lax
from jax.experimental import pallas as pl
from jax.experimental.pallas import tpu as pltpu
from jax.sharding import PartitionSpec as P

USER_BLK = 4
ITERS = 3
CHUNK = 512
STREAMS = 2
LANES = 128
PIECES = 4

epsilon = 1e-06
highest = lax.Precision.HIGHEST
MESH = pl.DeviceIdType.MESH


def confidence_of(w):
    return jnp.where(w > 0, 1 + w, jnp.zeros_like(w))


def kernel(
    nu, ni, scale,
    users_hbm, items_hbm, counts_hbm, y_hbm, gram_hbm, tiles_hbm,
    sol_ref, item_ref,
    users_in, items_in, count_in, slot_of, inv_ref, tiles, yv, yt, gram, wide, ws, turned, ct, xb, pa, ra, own, sb, rb, dn,
    d_state, r_state, x_state, n_state, i_state, a_state, sol_in,
    scal, sums, coef, x2, kept, outgo, income,
    load_sem, w_send, w_recv, a_send, a_recv, y_send, y_recv, b_send, b_recv,
    z_send, z_recv, f_send, f_recv, u_send, u_recv, o_send, o_recv,
    c_send, c_recv, p_send, p_recv, r_send, r_recv,
):
    slots, side, _ = tiles_hbm.shape
    items, rank = y_hbm.shape
    group = wide.shape[0]
    half = group // 2
    rows = group // ni
    nz = ni // 2
    owners = nz // STREAMS
    low = (nz - owners) // 2
    srows = owners * rows
    cols = items // nu
    blocks = items // side
    per = STREAMS * rows
    g, o = lax.axis_index("user"), lax.axis_index("item")
    z, c = lax.div(o, 2), lax.rem(o, 2)
    other = 1 - c
    sib = {"item": z * 2 + other}
    place = lax.rem(z - low + nz, owners)
    is_owner = (z >= low) & (z < low + owners)

    line = math.isqrt(nu)
    assert line * line == nu
    gx, gy = lax.rem(g, line), lax.div(g, line)

    def grid(x, y):
        return lax.rem(x, line) + line * lax.rem(y, line)

    def unum(i, j):
        return jnp.where(c == 0, grid(gx + i, gy + j), grid(gx + j, gy + i))

    def far(j, size):
        return min(j, size - j)

    zothers = sorted(range(1, nz), key=lambda j: -far(j, nz))

    def zpeer(j):
        return {"item": lax.rem(z + (j + nz), nz) * 2 + c}

    def upeer(i, j=0):
        return {"user": unum(i, j)}

    def piece(s, q, hh=0):
        at = (hh * STREAMS + s) * srows
        if isinstance(q, int):
            return pl.ds(at + q * rows, rows)
        return pl.ds(pl.multiple_of(at + q * rows, rows), rows)

    sent = []

    def rcopy(src, dst, ss, rs, dev):
        return pltpu.make_async_remote_copy(
            src_ref=src, dst_ref=dst, send_sem=ss, recv_sem=rs, device_id=dev, device_id_type=MESH
        )

    def send(*args):
        cp = rcopy(*args)
        cp.start()
        sent.append((None, cp))

    def send_if(cond, *args):
        cp = rcopy(*args)
        pl.when(cond)(cp.start)
        sent.append((cond, cp))

    def arrived(dst, ss, rs, dev):
        rcopy(dst, dst, ss, rs, dev).wait_recv()

    loads = [
        pltpu.make_async_copy(tiles_hbm, tiles.at[pl.ds(0, slots)], load_sem.at[0]),
        pltpu.make_async_copy(y_hbm, yv.at[0], load_sem.at[1]),
        pltpu.make_async_copy(gram_hbm, gram, load_sem.at[2]),
    ]
    index = [
        pltpu.make_async_copy(users_hbm, users_in, load_sem.at[3]),
        pltpu.make_async_copy(items_hbm, items_in, load_sem.at[4]),
        pltpu.make_async_copy(counts_hbm, count_in, load_sem.at[5]),
    ]
    for cp in index + loads:
        cp.start()

    barrier = pltpu.get_barrier_semaphore()

    def signal(dev):
        pl.semaphore_signal(barrier, inc=1, device_id=dev, device_id_type=MESH)

    def greet(t, carry):
        signal({"item": lax.rem(o + t, ni)})
        return carry

    def greet_line(i, t, carry):
        signal({"user": unum(i, 0), "item": t})
        return carry

    def greet_cross(i, t, carry):
        signal({"user": unum(0, i), "item": t * 2 + other})
        return carry

    lax.fori_loop(1, ni, greet, 0)
    for i in range(1, line):
        lax.fori_loop(0, ni, functools.partial(greet_line, i), 0)
        lax.fori_loop(0, nz, functools.partial(greet_cross, i), 0)
        signal(upeer(0, i))
    greeted = (ni - 1) + (line - 1) * (ni + nz + 1)
    tiles[slots] = jnp.zeros((side, side), jnp.bfloat16)
    for cp in index:
        cp.wait()
    lane = lax.broadcasted_iota(jnp.int32, (1, slots), 1)
    key = jnp.where(lane < count_in[...], users_in[0] * blocks + items_in[0], -1)
    match = lax.broadcasted_iota(jnp.int32, (LANES, slots), 0) == key
    found = jnp.min(jnp.where(match, lane, slots), axis=1, keepdims=True)
    slot_of[...] = jnp.broadcast_to(found, (LANES, LANES)).T[0:8]
    to_scalar = pltpu.make_async_copy(slot_of, inv_ref, load_sem.at[6])
    to_scalar.start()
    to_scalar.wait()
    loads[0].wait()
    def scatter(hh):
        for b in range(blocks):
            for q in range(owners):
                for s in range(STREAMS):
                    start = (q * STREAMS + s) * 2 * rows
                    u, off = start // side, start % side
                    to = ((hh * STREAMS + s) * owners + q) * rows
                    at = pl.ds(pl.multiple_of(off + (c if hh == 0 else other) * rows, rows), rows)
                    wide[to : to + rows, b * side : (b + 1) * side] = tiles[
                        inv_ref[0, u * blocks + b], at, :
                    ]

    scatter(1)
    loads[1].wait()

    def wcol(gg):
        return pl.ds(pl.multiple_of(gg * cols, cols), cols)

    def turn(i, j):
        to = ct.at[0, j] if i == 0 else turned.at[i - 1, j]
        to[...] = confidence_of(wide[:, wcol(unum(i, j))]).T
        if i:
            rcopy(to, ct.at[i, j], w_send, w_recv, upeer(i)).start()

    def rhs_pass(hh):
        here = slice(hh * half, (hh + 1) * half)
        return jnp.dot(confidence_of(wide[here, :]), yv[0], preferred_element_type=jnp.float32)

    def stream_pass(k, s):
        here = slice(s * srows, (s + 1) * srows)
        acc = jnp.zeros((srows, rank), jnp.float32)
        for side_of, w_ref in enumerate((wide, ws)):
            for i in range(items // CHUNK):
                at = slice(i * CHUNK, (i + 1) * CHUNK)
                yc = yv[side_of, at, :]
                scores = jnp.dot(xb[k - 1, 0, here, :], yt[side_of, :, at], preferred_element_type=jnp.float32)
                weighted = (scores * w_ref[here, at].astype(jnp.float32)).astype(jnp.bfloat16)
                acc = acc + jnp.dot(weighted, yc, preferred_element_type=jnp.float32)
        return acc

    def last_pass(s):
        here = slice(s * srows, (s + 1) * srows)
        acc = jnp.zeros((srows, LANES), jnp.float32)
        for side_of, w_ref in enumerate((wide, ws)):
            for i in range(items // CHUNK):
                at = slice(i * CHUNK, (i + 1) * CHUNK)
                scores = jnp.dot(
                    xb[ITERS - 1, 0, here, :], yt[side_of, :, at], preferred_element_type=jnp.float32
                )
                weighted = (scores * w_ref[here, at].astype(jnp.float32)).astype(jnp.bfloat16)
                prod = weighted.astype(jnp.float32) * scores
                for j in range(CHUNK // LANES):
                    acc = acc + prod[:, j * LANES : (j + 1) * LANES]
        return acc

    def sums_store(accs):
        for q in range(owners):
            mine = jnp.concatenate([acc[q * rows : (q + 1) * rows] for acc in accs], axis=0)
            sums[o, q : q + 1, 0:per] = jnp.sum(mine.T, axis=0, keepdims=True)

    def flip(which):
        for i in range(items // rank):
            at = slice(i * rank, (i + 1) * rank)
            yt[which, :, at] = yv[which, at, :].T

    def owner_device(zo):
        return {"item": zo * 2 + other}

    def reduce_start(k, s, total):
        sb[k, s] = total.astype(jnp.bfloat16)
        for i in range(owners):
            q = jnp.where(z * 2 < nz, owners - 1 - i, i)
            zo = q + low
            part = sb.at[k, s, pl.ds(pl.multiple_of(q * rows, rows), rows)]
            rcopy(part, rb.at[k, s, lax.rem(zo - z + nz, nz)], b_send.at[s], b_recv.at[s], owner_device(zo)).start()

    def reduce_sent(k, s):
        rcopy(sb.at[k, s], sb.at[k, s], b_send.at[s], b_recv.at[s], sib).wait_send()

    def reduce_end(k, s):
        arrived(rb.at[k, s], b_send.at[s], b_recv.at[s], sib)
        total = rb[k, s, 0].astype(jnp.float32)
        for j in range(1, nz):
            total = total + rb[k, s, j].astype(jnp.float32)
        return total

    def gather_send(k, s):
        for j in zothers + [0]:
            rcopy(
                dn.at[k, s], xb.at[k, 0, piece(s, place)], z_send.at[s], z_recv.at[s, place],
                owner_device(lax.rem(z + j, nz)),
            ).start()

    def gather_sent(k, s):
        rcopy(rb.at[k, s], rb.at[k, s], z_send.at[s], z_recv.at[s, 0], sib).wait_send()

    def gather_end(k, s, pass_on):
        for q in range(owners):
            got = xb.at[k, 0, piece(s, q)]
            arrived(got, z_send.at[s], z_recv.at[s, q], sib)
            if pass_on:
                rcopy(got, xb.at[k, 0, piece(s, q, 1)], f_send.at[k], f_recv.at[k + s], sib).start()
                for i in range(1, line):
                    rcopy(got, xb.at[k, i, piece(s, q)], u_send.at[k], u_recv.at[k], upeer(i)).start()

    mine_all, theirs_all = pl.ds(0, half), pl.ds(half, half)
    away = pl.ds(1, line - 1)

    def basis_send(k):
        mine = xb.at[k, 0, mine_all]
        rcopy(mine, xb.at[k, 0, theirs_all], f_send.at[k], f_recv.at[k], sib).start()

    def basis_pass(k):
        arrived(xb.at[k, 0, theirs_all], f_send.at[k], f_recv.at[k], sib)
        for i in range(1, line):
            rcopy(xb.at[k, 0], xb.at[k, i], u_send.at[k], u_recv.at[k], upeer(i)).start()

    def basis_end(k):
        arrived(xb.at[k, away], u_send.at[k], u_recv.at[k], sib)

    def basis_sent(k):
        mine, got = xb.at[k, 0, mine_all], xb.at[k, away]
        rcopy(mine, mine, f_send.at[k], f_recv.at[k], sib).wait_send()
        rcopy(got, got, u_send.at[k], u_recv.at[k], sib).wait_send()

    def update(k, s):
        total = reduce_end(k, s)
        if k == 0:
            r_state[s] = total
            d_state[s] = total
            n_state[s] = jnp.sum(total * total, axis=1, keepdims=True)
            dn[k, s] = total.astype(jnp.bfloat16)
            return
        direction = d_state[s]
        image = i_state[s] + total
        norm = n_state[s]
        alpha = norm / (jnp.sum(direction * image, axis=1, keepdims=True) + epsilon)
        residual = r_state[s] - alpha * image
        norm_next = jnp.sum(residual * residual, axis=1, keepdims=True)
        direction_next = residual + norm_next / (norm + epsilon) * direction
        dn[k, s] = direction_next.astype(jnp.bfloat16)
        moved = alpha * direction
        x_state[s] = moved if k == 1 else x_state[s] + moved
        a_state[k - 1, s] = alpha
        r_state[s] = residual
        d_state[s] = direction_next
        n_state[s] = norm_next

    def grams():
        for s in range(STREAMS):
            i_state[s] = jnp.dot(
                d_state[s], gram[...], precision=highest, preferred_element_type=jnp.float32
            )

    def spread(slot, ss, near, far_off):
        def column(t, carry):
            dev = {"item": lax.rem(o + t, ni)}
            rcopy(slot(0), slot(0), ss, near, dev).start()
            return carry

        for e in range(2):
            for t in range(1, line):
                gg = grid(gx + t, gy) if e == 0 else grid(gx, gy + t)

                def across(zz, carry):
                    dev = {"user": gg, "item": lax.rem(z + zz, nz) * 2 + e}
                    rcopy(slot(0), slot(t), ss, far_off, dev).start()
                    return carry

                lax.fori_loop(0, nz, across, 0)
        lax.fori_loop(1, ni, column, 0)

    def spread_end(every, ss, rs):
        rcopy(every, every, ss, rs, sib).wait_send()

    told = (ni - 1) + 2 * (line - 1) * nz

    def scal_slot(t):
        return scal.at[(t * owners + place) * 2 + other]

    def sums_slot(t):
        return sums.at[(t * nz + z) * 2 + c]

    def tell():
        grams()
        lane = lax.broadcasted_iota(jnp.int32, (rows, LANES), 1)
        parts = []
        for s in range(STREAMS):
            turned = jnp.sum(d_state[s] * i_state[s], axis=1, keepdims=True)
            at = jnp.where(lane == 2, n_state[s], turned)
            at = jnp.where(lane == 1, a_state[1, s], at)
            parts.append(jnp.where(lane == 0, a_state[0, s], at))
        scal[place * 2 + other, :, 0:per] = jnp.concatenate(parts, axis=0).T[0:8]
        spread(scal_slot, c_send, c_recv, c_recv)

    def step(k, s):
        update(k, s)
        gather_send(k, s)

    pa[...] = rhs_pass(1)
    pl.semaphore_wait(barrier, greeted)
    send(pa, ra, a_send, a_recv, sib)
    scatter(0)
    first = rhs_pass(0)
    for s in range(STREAMS):
        own[s] = first[s * srows : (s + 1) * srows]
    send(yv.at[0], yv.at[1], y_send.at[0], y_recv.at[0], sib)
    send(wide.at[theirs_all], ws, y_send.at[1], y_recv.at[1], sib)
    arrived(ra, a_send, a_recv, sib)
    for s in range(STREAMS):
        reduce_start(0, s, own[s] + ra[s * srows : (s + 1) * srows, :])
    for i in range(1, line):
        for j in range(line):
            turn(i, j)
    for j in range(line):
        turn(0, j)
    flip(0)
    loads[2].wait()
    arrived(yv.at[1], y_send.at[0], y_recv.at[0], sib)
    flip(1)
    for s in range(STREAMS):
        pl.when(is_owner)(functools.partial(step, 0, s))
    arrived(ws, y_send.at[1], y_recv.at[1], sib)

    for k in range(1, ITERS):
        for s in range(STREAMS):
            gather_end(k - 1, s, False)
            total = stream_pass(k, s)
            reduce_sent(k - 1, s)
            reduce_start(k, s, total)
        basis_send(k - 1)
        pl.when(is_owner)(grams)
        for s in range(STREAMS):
            pl.when(is_owner)(functools.partial(gather_sent, k - 1, s))
            pl.when(is_owner)(functools.partial(step, k, s))
        basis_pass(k - 1)

    pl.when(is_owner)(tell)
    for s in range(STREAMS):
        send_if(is_owner, x_state.at[s], sol_in, o_send.at[s], o_recv, owner_device(place * STREAMS + s))
    k = ITERS - 1

    def last_forward(s):
        got = xb.at[k, 0, pl.ds(half + s * srows, srows)]
        arrived(got, f_send.at[k], f_recv.at[k + s], sib)
        for i in range(1, line):
            rcopy(got, xb.at[k, i, pl.ds(half + s * srows, srows)], u_send.at[k], u_recv.at[k], upeer(i)).start()

    rowsums = []
    for s in range(STREAMS):
        gather_end(k, s, True)
        if s:
            last_forward(s - 1)
        rowsums.append(last_pass(s))
    sums_store(rowsums)
    spread(sums_slot, p_send, p_recv.at[0], p_recv.at[1])
    last_forward(STREAMS - 1)
    known = line * owners * 2

    @pl.when(is_owner)
    def _():
        arrived(scal.at[pl.ds(0, known - 1)], c_send, c_recv, sib)

    @pl.when(jnp.logical_not(is_owner))
    def _():
        arrived(scal.at[pl.ds(0, known)], c_send, c_recv, sib)

    def cell(v, hh, q):
        return (v * 2 + hh) * owners + q

    def cells(groups):
        for v in groups:
            for hh in range(2):
                for q in range(owners):
                    yield v, hh, q, (c if hh == 0 else other)

    every = range(line)

    def block(v, hh, s, q):
        at = ((hh * STREAMS + s) * owners + q) * rows
        return slice(at, at + rows)

    for v, hh, q, cc in cells(every):
        n = cell(v, hh, q)
        coef[0:4, n, :] = scal[(v * owners + q) * 2 + cc][0:4]
    alpha1, alpha2 = coef[0].T, coef[1].T
    for j in range(k):
        basis_end(j)
    for v, hh, q, cc in cells(every):
        n = cell(v, hh, q)
        for s in range(STREAMS):
            at = block(v, hh, s, q)
            r = slice(s * rows, (s + 1) * rows)
            x2[v, at, :] = alpha1[r, n : n + 1] * xb[0, v, at, :].astype(jnp.float32) + alpha2[
                r, n : n + 1
            ] * xb[1, v, at, :].astype(jnp.float32)

    def alphas(groups):
        for v, hh, q, cc in cells(groups):
            n = cell(v, hh, q)
            total = coef[3, n : n + 1, :]
            for zz in range(nz):
                total = total + sums[(v * nz + zz) * 2 + cc, q : q + 1, :]
            coef[4, n : n + 1, :] = coef[2, n : n + 1, :] / (total + epsilon)
        return coef[4].T

    def final_of(v, alpha):
        parts = []
        for hh in range(2):
            for s in range(STREAMS):
                for q in range(owners):
                    n = cell(v, hh, q)
                    at = block(v, hh, s, q)
                    parts.append(
                        x2[v, at, :]
                        + alpha[s * rows : (s + 1) * rows, n : n + 1] * xb[k, v, at, :].astype(jnp.float32)
                    )
        return jnp.concatenate(parts, axis=0).astype(jnp.bfloat16)

    arrived(sums.at[pl.ds(0, ni - 1)], p_send, p_recv.at[0], sib)
    alpha3 = alphas([0])
    final = final_of(0, alpha3)
    for j in range(line):
        kept[j] = jnp.dot(ct[0, j], final, preferred_element_type=jnp.float32)

    arrived(sol_in, o_send.at[0], o_recv, sib)
    for target in range(nz):
        s, q = target % STREAMS, target // STREAMS

        @pl.when(z == target)
        def _():
            n = cell(0, 0, q)
            sol_ref[...] = sol_in[...] + alpha3[s * rows : (s + 1) * rows, n : n + 1] * xb[
                k, 0, block(0, 0, s, q), :
            ].astype(jnp.float32)

    arrived(sums.at[pl.ds(0, (line - 1) * ni)], p_send, p_recv.at[1], sib)
    alpha3 = alphas(range(1, line))
    arrived(ct.at[away], w_send, w_recv, sib)
    basis_end(k)
    finals = [final_of(v, alpha3) for v in range(1, line)]
    for j in list(range(1, line)) + [0]:
        for i in range(PIECES):
            at = slice(i * cols // PIECES, (i + 1) * cols // PIECES)
            total = kept[j, at, :]
            for v in range(1, line):
                total = total + jnp.dot(ct[v, j, at, :], finals[v - 1], preferred_element_type=jnp.float32)
            if j:
                outgo[j - 1, at, :] = total.astype(jnp.bfloat16)
                part = pl.ds(i * cols // PIECES, cols // PIECES)
                rcopy(
                    outgo.at[j - 1, part], income.at[j - 1, part], r_send, r_recv, upeer(0, j)
                ).start()
            else:
                item_ref[at, :] = total
    arrived(income, r_send, r_recv, sib)
    total = item_ref[...]
    for j in range(line - 1):
        total = total + income[j].astype(jnp.float32)
    item_ref[...] = total * scale

    for cond, cp in sent:
        if cond is None:
            cp.wait_send()
        else:
            pl.when(cond)(cp.wait_send)
    for j in range(ITERS):
        basis_sent(j)
    for s in range(STREAMS):
        reduce_sent(k, s)
        pl.when(is_owner)(functools.partial(gather_sent, k, s))
    rcopy(turned, turned, w_send, w_recv, sib).wait_send()
    spread_end(sums.at[pl.ds(0, told)], p_send, p_recv.at[0])
    pl.when(is_owner)(functools.partial(spread_end, scal.at[pl.ds(0, told)], c_send, c_recv))
    rcopy(outgo, outgo, r_send, r_recv, sib).wait_send()


def place_outputs(sol_in, item_in, sol_out, item_out, sem):
    copies = [
        pltpu.make_async_copy(item_in, item_out, sem.at[0]),
        pltpu.make_async_copy(sol_in, sol_out, sem.at[1]),
    ]
    for cp in copies:
        cp.start()
    for cp in copies:
        cp.wait()


def make_local(nu, ni):
    def local(item_factors, item_gram, tile_users, tile_items, tile_counts, tile_values):
        items, rank = item_factors.shape
        slots, side = tile_values.shape[2], tile_values.shape[-1]
        blocks = items // side
        group = USER_BLK * side
        half = group // 2
        rows = group // ni
        nz = ni // 2
        owners = nz // STREAMS
        srows = owners * rows
        cols = items // nu
        scale = float(nu * group) ** -0.5
        bf, f4 = jnp.bfloat16, jnp.float32
        dma = pltpu.SemaphoreType.DMA
        vm = pltpu.VMEM
        line = math.isqrt(nu)
        cells = max(8, line * 2 * owners)
        anywhere = pl.BlockSpec(memory_space=pl.ANY)
        vmem = pl.BlockSpec(memory_space=pltpu.VMEM)
        sol, item = pl.pallas_call(
            functools.partial(kernel, nu, ni, scale),
            out_shape=(vm((rows, rank), f4), vm((cols, rank), f4)),
            in_specs=[anywhere] * 6,
            out_specs=(vmem, vmem),
            scratch_shapes=[
                vm((1, 1, slots), jnp.int32),
                vm((1, 1, slots), jnp.int32),
                vm((1, 1), jnp.int32),
                vm((8, LANES), jnp.int32),
                pltpu.SMEM((8, LANES), jnp.int32),
                vm((slots + 1, side, side), bf),
                vm((2, items, rank), bf),
                vm((2, rank, items), bf),
                vm((rank, rank), f4),
                vm((group, items), bf),
                vm((half, items), bf),
                vm((line - 1, line, cols, group), bf),
                vm((line, line, cols, group), bf),
                vm((ITERS, line, group, rank), bf),
                vm((half, rank), f4),
                vm((half, rank), f4),
                vm((STREAMS, srows, rank), f4),
                vm((ITERS, STREAMS, srows, rank), bf),
                vm((ITERS, STREAMS, nz, rows, rank), bf),
                vm((ITERS, STREAMS, rows, rank), bf),
                vm((STREAMS, rows, rank), f4),
                vm((STREAMS, rows, rank), f4),
                vm((STREAMS, rows, rank), f4),
                vm((STREAMS, rows, 1), f4),
                vm((STREAMS, rows, rank), f4),
                vm((2, STREAMS, rows, 1), f4),
                vm((rows, rank), f4),
                vm((line * ni, 8, LANES), f4),
                vm((line * ni, owners, LANES), f4),
                vm((5, cells, LANES), f4),
                vm((line, group, rank), f4),
                vm((line, cols, rank), f4),
                vm((line - 1, cols, rank), bf),
                vm((line - 1, cols, rank), bf),
                dma((7,)),
                dma(()), dma(()),
                dma(()), dma(()),
                dma((2,)), dma((2,)),
                dma((STREAMS,)), dma((STREAMS,)),
                dma((STREAMS,)), dma((STREAMS, owners)),
                dma((ITERS,)), dma((ITERS - 1 + STREAMS,)),
                dma((ITERS,)), dma((ITERS,)),
                dma((STREAMS,)), dma(()),
                dma(()), dma(()), dma(()), dma((2,)),
                dma(()), dma(()),
            ],
            compiler_params=pltpu.CompilerParams(collective_id=0, has_side_effects=True),
        )(tile_users, tile_items, tile_counts, item_factors, item_gram, tile_values.reshape(slots, side, side))
        sol = pltpu.with_memory_space_constraint(sol, pltpu.VMEM)
        item = pltpu.with_memory_space_constraint(item, pltpu.VMEM)
        sol, item = pl.pallas_call(
            place_outputs,
            out_shape=(
                jax.ShapeDtypeStruct((rows, rank), f4),
                jax.ShapeDtypeStruct((cols, rank), f4),
            ),
            in_specs=[vmem, vmem],
            out_specs=(anywhere, anywhere),
            scratch_shapes=[dma((2,))],
        )(sol, item)
        return sol, item[None]

    return local


def solution(mesh):
    return jax.shard_map(
        make_local(mesh.shape["user"], mesh.shape["item"]),
        mesh=mesh,
        in_specs=(
            P("item", None),
            P(),
            P("user", "item", None),
            P("user", "item", None),
            P("user", "item"),
            P("user", "item", None, None, None),
        ),
        out_specs=(P(("user", "item"), None), P("item", "user", None)),
        check_vma=False,
    )
```

```python
import functools
import math

import jax
import jax.numpy as jnp
from jax import lax
from jax.experimental import pallas as pl
from jax.experimental.pallas import tpu as pltpu
from jax.sharding import PartitionSpec as P

USER_BLK = 4
ITERS = 3
CHUNK = 512
STREAMS = 2
PARTS = 2
LANES = 128
PIECES = 4

epsilon = 1e-06
highest = lax.Precision.HIGHEST
MESH = pl.DeviceIdType.MESH


def confidence_of(w):
    return jnp.where(w > 0, 1 + w, jnp.zeros_like(w))


def kernel(
    nu, ni, scale,
    users_hbm, items_hbm, counts_hbm, y_hbm, gram_hbm, tiles_hbm,
    sol_ref, item_ref,
    users_in, items_in, count_in, slot_of, inv_ref, tiles, yv, yt, gram, wide, ws, turned, ct, xb, pa, ra, own, sb, rb, dn,
    d_state, r_state, x_state, n_state, i_state, a_state, sol_in,
    scal, sums, coef, x2, kept, outgo, income,
    load_sem, w_send, w_recv, a_send, a_recv, y_send, y_recv, b_send, b_recv,
    z_send, z_recv, f_send, f_recv, u_send, u_recv, o_send, o_recv,
    c_send, c_recv, p_send, p_recv, r_send, r_recv,
):
    slots, side, _ = tiles_hbm.shape
    items, rank = y_hbm.shape
    group = wide.shape[0]
    half = group // 2
    rows = group // ni
    nz = ni // 2
    owners = nz // STREAMS
    low = (nz - owners) // 2
    srows = owners * rows
    cols = items // nu
    blocks = items // side
    per = STREAMS * rows
    g, o = lax.axis_index("user"), lax.axis_index("item")
    z, c = lax.div(o, 2), lax.rem(o, 2)
    other = 1 - c
    sib = {"item": z * 2 + other}
    place = lax.rem(z - low + nz, owners)
    is_owner = (z >= low) & (z < low + owners)

    line = math.isqrt(nu)
    assert line * line == nu
    gx, gy = lax.rem(g, line), lax.div(g, line)

    def grid(x, y):
        return lax.rem(x, line) + line * lax.rem(y, line)

    def unum(i, j):
        return jnp.where(c == 0, grid(gx + i, gy + j), grid(gx + j, gy + i))

    def far(j, size):
        return min(j, size - j)

    zothers = sorted(range(1, nz), key=lambda j: -far(j, nz))

    def zpeer(j):
        return {"item": lax.rem(z + (j + nz), nz) * 2 + c}

    def upeer(i, j=0):
        return {"user": unum(i, j)}

    def piece(s, q, hh=0):
        at = (hh * STREAMS + s) * srows
        if isinstance(q, int):
            return pl.ds(at + q * rows, rows)
        return pl.ds(pl.multiple_of(at + q * rows, rows), rows)

    sent = []

    def rcopy(src, dst, ss, rs, dev):
        return pltpu.make_async_remote_copy(
            src_ref=src, dst_ref=dst, send_sem=ss, recv_sem=rs, device_id=dev, device_id_type=MESH
        )

    def send(*args):
        cp = rcopy(*args)
        cp.start()
        sent.append((None, cp))

    def send_if(cond, *args):
        cp = rcopy(*args)
        pl.when(cond)(cp.start)
        sent.append((cond, cp))

    def arrived(dst, ss, rs, dev):
        rcopy(dst, dst, ss, rs, dev).wait_recv()

    loads = [
        pltpu.make_async_copy(tiles_hbm, tiles.at[pl.ds(0, slots)], load_sem.at[0]),
        pltpu.make_async_copy(y_hbm, yv.at[0], load_sem.at[1]),
        pltpu.make_async_copy(gram_hbm, gram, load_sem.at[2]),
    ]
    index = [
        pltpu.make_async_copy(users_hbm, users_in, load_sem.at[3]),
        pltpu.make_async_copy(items_hbm, items_in, load_sem.at[4]),
        pltpu.make_async_copy(counts_hbm, count_in, load_sem.at[5]),
    ]
    for cp in index + loads:
        cp.start()

    barrier = pltpu.get_barrier_semaphore()

    def signal(dev):
        pl.semaphore_signal(barrier, inc=1, device_id=dev, device_id_type=MESH)

    def greet(t, carry):
        signal({"item": lax.rem(o + t, ni)})
        return carry

    def greet_line(i, t, carry):
        signal({"user": unum(i, 0), "item": t})
        return carry

    def greet_cross(i, t, carry):
        signal({"user": unum(0, i), "item": t * 2 + other})
        return carry

    lax.fori_loop(1, ni, greet, 0)
    for i in range(1, line):
        lax.fori_loop(0, ni, functools.partial(greet_line, i), 0)
        lax.fori_loop(0, nz, functools.partial(greet_cross, i), 0)
        signal(upeer(0, i))
    greeted = (ni - 1) + (line - 1) * (ni + nz + 1)
    tiles[slots] = jnp.zeros((side, side), jnp.bfloat16)
    for cp in index:
        cp.wait()
    lane = lax.broadcasted_iota(jnp.int32, (1, slots), 1)
    key = jnp.where(lane < count_in[...], users_in[0] * blocks + items_in[0], -1)
    match = lax.broadcasted_iota(jnp.int32, (LANES, slots), 0) == key
    found = jnp.min(jnp.where(match, lane, slots), axis=1, keepdims=True)
    slot_of[...] = jnp.broadcast_to(found, (LANES, LANES)).T[0:8]
    to_scalar = pltpu.make_async_copy(slot_of, inv_ref, load_sem.at[6])
    to_scalar.start()
    to_scalar.wait()
    loads[0].wait()
    def scatter(hh):
        for b in range(blocks):
            for q in range(owners):
                for s in range(STREAMS):
                    start = (q * STREAMS + s) * 2 * rows
                    u, off = start // side, start % side
                    to = ((hh * STREAMS + s) * owners + q) * rows
                    at = pl.ds(pl.multiple_of(off + (c if hh == 0 else other) * rows, rows), rows)
                    wide[to : to + rows, b * side : (b + 1) * side] = tiles[
                        inv_ref[0, u * blocks + b], at, :
                    ]

    scatter(1)
    loads[1].wait()

    def wcol(gg):
        return pl.ds(pl.multiple_of(gg * cols, cols), cols)

    def turn(i, j):
        to = ct.at[0, j] if i == 0 else turned.at[i - 1, j]
        to[...] = confidence_of(wide[:, wcol(unum(i, j))]).T
        if i:
            rcopy(to, ct.at[i, j], w_send, w_recv, upeer(i)).start()

    def rhs_pass(hh):
        here = slice(hh * half, (hh + 1) * half)
        return jnp.dot(confidence_of(wide[here, :]), yv[0], preferred_element_type=jnp.float32)

    def stream_pass(k, s):
        here = slice(s * srows, (s + 1) * srows)
        acc = jnp.zeros((srows, rank), jnp.float32)
        for side_of, w_ref in enumerate((wide, ws)):
            for i in range(items // CHUNK):
                at = slice(i * CHUNK, (i + 1) * CHUNK)
                yc = yv[side_of, at, :]
                scores = jnp.dot(xb[k - 1, 0, here, :], yt[side_of, :, at], preferred_element_type=jnp.float32)
                weighted = (scores * w_ref[here, at].astype(jnp.float32)).astype(jnp.bfloat16)
                acc = acc + jnp.dot(weighted, yc, preferred_element_type=jnp.float32)
        return acc

    def last_pass(s):
        here = slice(s * srows, (s + 1) * srows)
        acc = jnp.zeros((srows, LANES), jnp.float32)
        for side_of, w_ref in enumerate((wide, ws)):
            for i in range(items // CHUNK):
                at = slice(i * CHUNK, (i + 1) * CHUNK)
                scores = jnp.dot(
                    xb[ITERS - 1, 0, here, :], yt[side_of, :, at], preferred_element_type=jnp.float32
                )
                weighted = (scores * w_ref[here, at].astype(jnp.float32)).astype(jnp.bfloat16)
                prod = weighted.astype(jnp.float32) * scores
                for j in range(CHUNK // LANES):
                    acc = acc + prod[:, j * LANES : (j + 1) * LANES]
        return acc

    def sums_store(accs):
        for q in range(owners):
            mine = jnp.concatenate([acc[q * rows : (q + 1) * rows] for acc in accs], axis=0)
            sums[o, q : q + 1, 0:per] = jnp.sum(mine.T, axis=0, keepdims=True)

    def flip(which):
        for i in range(items // rank):
            at = slice(i * rank, (i + 1) * rank)
            yt[which, :, at] = yv[which, at, :].T

    def owner_device(zo):
        return {"item": zo * 2 + other}

    parts = rb.shape[2]
    prows = rows // parts

    def reduce_start(k, s, total):
        sb[k, s] = total.astype(jnp.bfloat16)
        for t in range(parts):
            for i in range(owners):
                q = jnp.where(z * 2 < nz, owners - 1 - i, i)
                zo = q + low
                part = sb.at[k, s, pl.ds(pl.multiple_of(q * rows + t * prows, prows), prows)]
                to = rb.at[k, s, t, lax.rem(zo - z + nz, nz)]
                rcopy(part, to, b_send.at[s], b_recv.at[s, t], owner_device(zo)).start()

    def reduce_sent(k, s):
        rcopy(sb.at[k, s], sb.at[k, s], b_send.at[s], b_recv.at[s, 0], sib).wait_send()

    def reduce_end(k, s, t):
        arrived(rb.at[k, s, t], b_send.at[s], b_recv.at[s, t], sib)
        total = rb[k, s, t, 0].astype(jnp.float32)
        for j in range(1, nz):
            total = total + rb[k, s, t, j].astype(jnp.float32)
        return total

    def gather_send(k, s, t):
        part = pl.ds(t * prows, prows)
        at = pl.ds(pl.multiple_of(s * srows + place * rows + t * prows, prows), prows)
        for j in zothers + [0]:
            rcopy(
                dn.at[k, s, part], xb.at[k, 0, at], z_send.at[s], z_recv.at[s, place],
                owner_device(lax.rem(z + j, nz)),
            ).start()

    def gather_sent(k, s):
        rcopy(rb.at[k, s], rb.at[k, s], z_send.at[s], z_recv.at[s, 0], sib).wait_send()

    def gather_end(k, s, pass_on):
        for q in range(owners):
            got = xb.at[k, 0, piece(s, q)]
            arrived(got, z_send.at[s], z_recv.at[s, q], sib)
            if pass_on:
                rcopy(got, xb.at[k, 0, piece(s, q, 1)], f_send.at[k], f_recv.at[k + s], sib).start()
                for i in range(1, line):
                    rcopy(got, xb.at[k, i, piece(s, q)], u_send.at[k], u_recv.at[k], upeer(i)).start()

    mine_all, theirs_all = pl.ds(0, half), pl.ds(half, half)
    away = pl.ds(1, line - 1)

    def basis_send(k):
        mine = xb.at[k, 0, mine_all]
        rcopy(mine, xb.at[k, 0, theirs_all], f_send.at[k], f_recv.at[k], sib).start()

    def basis_pass(k):
        arrived(xb.at[k, 0, theirs_all], f_send.at[k], f_recv.at[k], sib)
        for i in range(1, line):
            rcopy(xb.at[k, 0], xb.at[k, i], u_send.at[k], u_recv.at[k], upeer(i)).start()

    def basis_end(k):
        arrived(xb.at[k, away], u_send.at[k], u_recv.at[k], sib)

    def basis_sent(k):
        mine, got = xb.at[k, 0, mine_all], xb.at[k, away]
        rcopy(mine, mine, f_send.at[k], f_recv.at[k], sib).wait_send()
        rcopy(got, got, u_send.at[k], u_recv.at[k], sib).wait_send()

    def update(k, s, t):
        at = slice(t * prows, (t + 1) * prows)
        total = reduce_end(k, s, t)
        if k == 0:
            r_state[s, at] = total
            d_state[s, at] = total
            n_state[s, at] = jnp.sum(total * total, axis=1, keepdims=True)
            dn[k, s, at] = total.astype(jnp.bfloat16)
            return
        direction = d_state[s, at]
        image = i_state[s, at] + total
        norm = n_state[s, at]
        alpha = norm / (jnp.sum(direction * image, axis=1, keepdims=True) + epsilon)
        residual = r_state[s, at] - alpha * image
        norm_next = jnp.sum(residual * residual, axis=1, keepdims=True)
        direction_next = residual + norm_next / (norm + epsilon) * direction
        dn[k, s, at] = direction_next.astype(jnp.bfloat16)
        gather_send(k, s, t)
        moved = alpha * direction
        x_state[s, at] = moved if k == 1 else x_state[s, at] + moved
        a_state[k - 1, s, at] = alpha
        r_state[s, at] = residual
        d_state[s, at] = direction_next
        n_state[s, at] = norm_next

    def grams():
        for s in range(STREAMS):
            i_state[s] = jnp.dot(
                d_state[s], gram[...], precision=highest, preferred_element_type=jnp.float32
            )

    def spread(slot, ss, near, far_off):
        def column(t, carry):
            dev = {"item": lax.rem(o + t, ni)}
            rcopy(slot(0), slot(0), ss, near, dev).start()
            return carry

        for e in range(2):
            for t in range(1, line):
                gg = grid(gx + t, gy) if e == 0 else grid(gx, gy + t)

                def across(zz, carry):
                    dev = {"user": gg, "item": lax.rem(z + zz, nz) * 2 + e}
                    rcopy(slot(0), slot(t), ss, far_off, dev).start()
                    return carry

                lax.fori_loop(0, nz, across, 0)
        lax.fori_loop(1, ni, column, 0)

    def spread_end(every, ss, rs):
        rcopy(every, every, ss, rs, sib).wait_send()

    told = (ni - 1) + 2 * (line - 1) * nz

    def scal_slot(t):
        return scal.at[(t * owners + place) * 2 + other]

    def sums_slot(t):
        return sums.at[(t * nz + z) * 2 + c]

    def tell():
        grams()
        lane = lax.broadcasted_iota(jnp.int32, (rows, LANES), 1)
        parts = []
        for s in range(STREAMS):
            turned = jnp.sum(d_state[s] * i_state[s], axis=1, keepdims=True)
            at = jnp.where(lane == 2, n_state[s], turned)
            at = jnp.where(lane == 1, a_state[1, s], at)
            parts.append(jnp.where(lane == 0, a_state[0, s], at))
        scal[place * 2 + other, :, 0:per] = jnp.concatenate(parts, axis=0).T[0:8]
        spread(scal_slot, c_send, c_recv, c_recv)

    def step(k, s):
        for t in range(parts):
            update(k, s, t)
            if k == 0:
                gather_send(k, s, t)

    pa[...] = rhs_pass(1)
    pl.semaphore_wait(barrier, greeted)
    send(pa, ra, a_send, a_recv, sib)
    scatter(0)
    first = rhs_pass(0)
    for s in range(STREAMS):
        own[s] = first[s * srows : (s + 1) * srows]
    send(yv.at[0], yv.at[1], y_send.at[0], y_recv.at[0], sib)
    send(wide.at[theirs_all], ws, y_send.at[1], y_recv.at[1], sib)
    arrived(ra, a_send, a_recv, sib)
    for s in range(STREAMS):
        reduce_start(0, s, own[s] + ra[s * srows : (s + 1) * srows, :])
    for i in range(1, line):
        for j in range(line):
            turn(i, j)
    for j in range(line):
        turn(0, j)
    flip(0)
    loads[2].wait()
    arrived(yv.at[1], y_send.at[0], y_recv.at[0], sib)
    flip(1)
    for s in range(STREAMS):
        pl.when(is_owner)(functools.partial(step, 0, s))
    arrived(ws, y_send.at[1], y_recv.at[1], sib)

    for k in range(1, ITERS):
        for s in range(STREAMS):
            gather_end(k - 1, s, False)
            total = stream_pass(k, s)
            reduce_sent(k - 1, s)
            reduce_start(k, s, total)
        basis_send(k - 1)
        pl.when(is_owner)(grams)
        for s in range(STREAMS):
            pl.when(is_owner)(functools.partial(gather_sent, k - 1, s))
            pl.when(is_owner)(functools.partial(step, k, s))
        basis_pass(k - 1)

    pl.when(is_owner)(tell)
    for s in range(STREAMS):
        send_if(is_owner, x_state.at[s], sol_in, o_send.at[s], o_recv, owner_device(place * STREAMS + s))
    k = ITERS - 1

    def last_forward(s):
        got = xb.at[k, 0, pl.ds(half + s * srows, srows)]
        arrived(got, f_send.at[k], f_recv.at[k + s], sib)
        for i in range(1, line):
            rcopy(got, xb.at[k, i, pl.ds(half + s * srows, srows)], u_send.at[k], u_recv.at[k], upeer(i)).start()

    rowsums = []
    for s in range(STREAMS):
        gather_end(k, s, True)
        if s:
            last_forward(s - 1)
        rowsums.append(last_pass(s))
    sums_store(rowsums)
    spread(sums_slot, p_send, p_recv.at[0], p_recv.at[1])
    last_forward(STREAMS - 1)
    known = line * owners * 2

    @pl.when(is_owner)
    def _():
        arrived(scal.at[pl.ds(0, known - 1)], c_send, c_recv, sib)

    @pl.when(jnp.logical_not(is_owner))
    def _():
        arrived(scal.at[pl.ds(0, known)], c_send, c_recv, sib)

    def cell(v, hh, q):
        return (v * 2 + hh) * owners + q

    def cells(groups):
        for v in groups:
            for hh in range(2):
                for q in range(owners):
                    yield v, hh, q, (c if hh == 0 else other)

    every = range(line)

    def block(v, hh, s, q):
        at = ((hh * STREAMS + s) * owners + q) * rows
        return slice(at, at + rows)

    for v, hh, q, cc in cells(every):
        n = cell(v, hh, q)
        coef[0:4, n, :] = scal[(v * owners + q) * 2 + cc][0:4]
    alpha1, alpha2 = coef[0].T, coef[1].T
    for j in range(k):
        basis_end(j)
    for v, hh, q, cc in cells(every):
        n = cell(v, hh, q)
        for s in range(STREAMS):
            at = block(v, hh, s, q)
            r = slice(s * rows, (s + 1) * rows)
            x2[v, at, :] = alpha1[r, n : n + 1] * xb[0, v, at, :].astype(jnp.float32) + alpha2[
                r, n : n + 1
            ] * xb[1, v, at, :].astype(jnp.float32)

    def alphas(groups):
        for v, hh, q, cc in cells(groups):
            n = cell(v, hh, q)
            total = coef[3, n : n + 1, :]
            for zz in range(nz):
                total = total + sums[(v * nz + zz) * 2 + cc, q : q + 1, :]
            coef[4, n : n + 1, :] = coef[2, n : n + 1, :] / (total + epsilon)
        return coef[4].T

    def final_of(v, alpha):
        parts = []
        for hh in range(2):
            for s in range(STREAMS):
                for q in range(owners):
                    n = cell(v, hh, q)
                    at = block(v, hh, s, q)
                    parts.append(
                        x2[v, at, :]
                        + alpha[s * rows : (s + 1) * rows, n : n + 1] * xb[k, v, at, :].astype(jnp.float32)
                    )
        return jnp.concatenate(parts, axis=0).astype(jnp.bfloat16)

    arrived(sums.at[pl.ds(0, ni - 1)], p_send, p_recv.at[0], sib)
    alpha3 = alphas([0])
    final = final_of(0, alpha3)
    for j in range(line):
        kept[j] = jnp.dot(ct[0, j], final, preferred_element_type=jnp.float32)

    arrived(sol_in, o_send.at[0], o_recv, sib)
    for target in range(nz):
        s, q = target % STREAMS, target // STREAMS

        @pl.when(z == target)
        def _():
            n = cell(0, 0, q)
            sol_ref[...] = sol_in[...] + alpha3[s * rows : (s + 1) * rows, n : n + 1] * xb[
                k, 0, block(0, 0, s, q), :
            ].astype(jnp.float32)

    arrived(sums.at[pl.ds(0, (line - 1) * ni)], p_send, p_recv.at[1], sib)
    alpha3 = alphas(range(1, line))
    arrived(ct.at[away], w_send, w_recv, sib)
    basis_end(k)
    finals = [final_of(v, alpha3) for v in range(1, line)]
    for j in list(range(1, line)) + [0]:
        for i in range(PIECES):
            at = slice(i * cols // PIECES, (i + 1) * cols // PIECES)
            total = kept[j, at, :]
            for v in range(1, line):
                total = total + jnp.dot(ct[v, j, at, :], finals[v - 1], preferred_element_type=jnp.float32)
            if j:
                outgo[j - 1, at, :] = total.astype(jnp.bfloat16)
                part = pl.ds(i * cols // PIECES, cols // PIECES)
                rcopy(
                    outgo.at[j - 1, part], income.at[j - 1, part], r_send, r_recv, upeer(0, j)
                ).start()
            else:
                item_ref[at, :] = total
    arrived(income, r_send, r_recv, sib)
    total = item_ref[...]
    for j in range(line - 1):
        total = total + income[j].astype(jnp.float32)
    item_ref[...] = total * scale

    for cond, cp in sent:
        if cond is None:
            cp.wait_send()
        else:
            pl.when(cond)(cp.wait_send)
    for j in range(ITERS):
        basis_sent(j)
    for s in range(STREAMS):
        reduce_sent(k, s)
        pl.when(is_owner)(functools.partial(gather_sent, k, s))
    rcopy(turned, turned, w_send, w_recv, sib).wait_send()
    spread_end(sums.at[pl.ds(0, told)], p_send, p_recv.at[0])
    pl.when(is_owner)(functools.partial(spread_end, scal.at[pl.ds(0, told)], c_send, c_recv))
    rcopy(outgo, outgo, r_send, r_recv, sib).wait_send()


def place_outputs(sol_in, item_in, sol_out, item_out, sem):
    copies = [
        pltpu.make_async_copy(item_in, item_out, sem.at[0]),
        pltpu.make_async_copy(sol_in, sol_out, sem.at[1]),
    ]
    for cp in copies:
        cp.start()
    for cp in copies:
        cp.wait()


def make_local(nu, ni):
    def local(item_factors, item_gram, tile_users, tile_items, tile_counts, tile_values):
        items, rank = item_factors.shape
        slots, side = tile_values.shape[2], tile_values.shape[-1]
        blocks = items // side
        group = USER_BLK * side
        half = group // 2
        rows = group // ni
        nz = ni // 2
        owners = nz // STREAMS
        srows = owners * rows
        cols = items // nu
        scale = float(nu * group) ** -0.5
        bf, f4 = jnp.bfloat16, jnp.float32
        dma = pltpu.SemaphoreType.DMA
        vm = pltpu.VMEM
        line = math.isqrt(nu)
        parts = min(PARTS, rows // 16)
        cells = max(8, line * 2 * owners)
        anywhere = pl.BlockSpec(memory_space=pl.ANY)
        vmem = pl.BlockSpec(memory_space=pltpu.VMEM)
        sol, item = pl.pallas_call(
            functools.partial(kernel, nu, ni, scale),
            out_shape=(vm((rows, rank), f4), vm((cols, rank), f4)),
            in_specs=[anywhere] * 6,
            out_specs=(vmem, vmem),
            scratch_shapes=[
                vm((1, 1, slots), jnp.int32),
                vm((1, 1, slots), jnp.int32),
                vm((1, 1), jnp.int32),
                vm((8, LANES), jnp.int32),
                pltpu.SMEM((8, LANES), jnp.int32),
                vm((slots + 1, side, side), bf),
                vm((2, items, rank), bf),
                vm((2, rank, items), bf),
                vm((rank, rank), f4),
                vm((group, items), bf),
                vm((half, items), bf),
                vm((line - 1, line, cols, group), bf),
                vm((line, line, cols, group), bf),
                vm((ITERS, line, group, rank), bf),
                vm((half, rank), f4),
                vm((half, rank), f4),
                vm((STREAMS, srows, rank), f4),
                vm((ITERS, STREAMS, srows, rank), bf),
                vm((ITERS, STREAMS, parts, nz, rows // parts, rank), bf),
                vm((ITERS, STREAMS, rows, rank), bf),
                vm((STREAMS, rows, rank), f4),
                vm((STREAMS, rows, rank), f4),
                vm((STREAMS, rows, rank), f4),
                vm((STREAMS, rows, 1), f4),
                vm((STREAMS, rows, rank), f4),
                vm((2, STREAMS, rows, 1), f4),
                vm((rows, rank), f4),
                vm((line * ni, 8, LANES), f4),
                vm((line * ni, owners, LANES), f4),
                vm((5, cells, LANES), f4),
                vm((line, group, rank), f4),
                vm((line, cols, rank), f4),
                vm((line - 1, cols, rank), bf),
                vm((line - 1, cols, rank), bf),
                dma((7,)),
                dma(()), dma(()),
                dma(()), dma(()),
                dma((2,)), dma((2,)),
                dma((STREAMS,)), dma((STREAMS, parts)),
                dma((STREAMS,)), dma((STREAMS, owners)),
                dma((ITERS,)), dma((ITERS - 1 + STREAMS,)),
                dma((ITERS,)), dma((ITERS,)),
                dma((STREAMS,)), dma(()),
                dma(()), dma(()), dma(()), dma((2,)),
                dma(()), dma(()),
            ],
            compiler_params=pltpu.CompilerParams(collective_id=0, has_side_effects=True),
        )(tile_users, tile_items, tile_counts, item_factors, item_gram, tile_values.reshape(slots, side, side))
        sol = pltpu.with_memory_space_constraint(sol, pltpu.VMEM)
        item = pltpu.with_memory_space_constraint(item, pltpu.VMEM)
        sol, item = pl.pallas_call(
            place_outputs,
            out_shape=(
                jax.ShapeDtypeStruct((rows, rank), f4),
                jax.ShapeDtypeStruct((cols, rank), f4),
            ),
            in_specs=[vmem, vmem],
            out_specs=(anywhere, anywhere),
            scratch_shapes=[dma((2,))],
        )(sol, item)
        return sol, item[None]

    return local


def solution(mesh):
    return jax.shard_map(
        make_local(mesh.shape["user"], mesh.shape["item"]),
        mesh=mesh,
        in_specs=(
            P("item", None),
            P(),
            P("user", "item", None),
            P("user", "item", None),
            P("user", "item"),
            P("user", "item", None, None, None),
        ),
        out_specs=(P(("user", "item"), None), P("item", "user", None)),
        check_vma=False,
    )
```

```python
import functools
import math

import jax
import jax.numpy as jnp
from jax import lax
from jax.experimental import pallas as pl
from jax.experimental.pallas import tpu as pltpu
from jax.sharding import PartitionSpec as P

USER_BLK = 4
ITERS = 3
CHUNK = 512
STREAMS = 2
PARTS = 2
LANES = 128
PIECES = 4

epsilon = 1e-06
highest = lax.Precision.HIGHEST
MESH = pl.DeviceIdType.MESH


def confidence_of(w):
    return jnp.where(w > 0, 1 + w, jnp.zeros_like(w))


def kernel(
    nu, ni, scale,
    users_hbm, items_hbm, counts_hbm, y_hbm, gram_hbm, tiles_hbm,
    sol_ref, item_ref,
    users_in, items_in, count_in, slot_of, inv_ref, tiles, yv, yt, gram, wide, ws, turned, ct, xb, pa, ra, own, sb, rb, dn,
    d_state, r_state, x_state, n_state, i_state, a_state, sol_in,
    scal, sums, coef, x2, kept, outgo, income,
    load_sem, w_send, w_recv, a_send, a_recv, y_send, y_recv, b_send, b_recv,
    z_send, z_recv, f_send, f_recv, u_send, u_recv, o_send, o_recv,
    c_send, c_recv, p_send, p_recv, r_send, r_recv,
):
    slots, side, _ = tiles_hbm.shape
    items, rank = y_hbm.shape
    group = wide.shape[0]
    half = group // 2
    rows = group // ni
    nz = ni // 2
    owners = nz // STREAMS
    low = (nz - owners) // 2
    srows = owners * rows
    cols = items // nu
    blocks = items // side
    per = STREAMS * rows
    g, o = lax.axis_index("user"), lax.axis_index("item")
    z, c = lax.div(o, 2), lax.rem(o, 2)
    other = 1 - c
    sib = {"item": z * 2 + other}
    place = lax.rem(z - low + nz, owners)
    is_owner = (z >= low) & (z < low + owners)

    line = math.isqrt(nu)
    assert line * line == nu
    gx, gy = lax.rem(g, line), lax.div(g, line)

    def grid(x, y):
        return lax.rem(x, line) + line * lax.rem(y, line)

    def unum(i, j):
        return jnp.where(c == 0, grid(gx + i, gy + j), grid(gx + j, gy + i))

    def far(j, size):
        return min(j, size - j)

    zothers = sorted(range(1, nz), key=lambda j: -far(j, nz))

    def zpeer(j):
        return {"item": lax.rem(z + (j + nz), nz) * 2 + c}

    def upeer(i, j=0):
        return {"user": unum(i, j)}

    def cross(i):
        return {"user": unum(0, i), "item": z * 2 + other}

    def piece(s, q, hh=0):
        at = (hh * STREAMS + s) * srows
        if isinstance(q, int):
            return pl.ds(at + q * rows, rows)
        return pl.ds(pl.multiple_of(at + q * rows, rows), rows)

    sent = []

    def rcopy(src, dst, ss, rs, dev):
        return pltpu.make_async_remote_copy(
            src_ref=src, dst_ref=dst, send_sem=ss, recv_sem=rs, device_id=dev, device_id_type=MESH
        )

    def send(*args):
        cp = rcopy(*args)
        cp.start()
        sent.append((None, cp))

    def send_if(cond, *args):
        cp = rcopy(*args)
        pl.when(cond)(cp.start)
        sent.append((cond, cp))

    def arrived(dst, ss, rs, dev):
        rcopy(dst, dst, ss, rs, dev).wait_recv()

    loads = [
        pltpu.make_async_copy(tiles_hbm, tiles.at[pl.ds(0, slots)], load_sem.at[0]),
        pltpu.make_async_copy(y_hbm, yv.at[0], load_sem.at[1]),
        pltpu.make_async_copy(gram_hbm, gram, load_sem.at[2]),
    ]
    index = [
        pltpu.make_async_copy(users_hbm, users_in, load_sem.at[3]),
        pltpu.make_async_copy(items_hbm, items_in, load_sem.at[4]),
        pltpu.make_async_copy(counts_hbm, count_in, load_sem.at[5]),
    ]
    for cp in index + loads:
        cp.start()

    barrier = pltpu.get_barrier_semaphore()

    def signal(dev):
        pl.semaphore_signal(barrier, inc=1, device_id=dev, device_id_type=MESH)

    def greet(t, carry):
        signal({"item": lax.rem(o + t, ni)})
        return carry

    def greet_line(i, t, carry):
        signal({"user": unum(i, 0), "item": t})
        return carry

    def greet_cross(i, t, carry):
        signal({"user": unum(0, i), "item": t * 2 + other})
        return carry

    lax.fori_loop(1, ni, greet, 0)
    for i in range(1, line):
        lax.fori_loop(0, ni, functools.partial(greet_line, i), 0)
        lax.fori_loop(0, nz, functools.partial(greet_cross, i), 0)
        signal(upeer(0, i))
    greeted = (ni - 1) + (line - 1) * (ni + nz + 1)
    tiles[slots] = jnp.zeros((side, side), jnp.bfloat16)
    for cp in index:
        cp.wait()
    lane = lax.broadcasted_iota(jnp.int32, (1, slots), 1)
    key = jnp.where(lane < count_in[...], users_in[0] * blocks + items_in[0], -1)
    match = lax.broadcasted_iota(jnp.int32, (LANES, slots), 0) == key
    found = jnp.min(jnp.where(match, lane, slots), axis=1, keepdims=True)
    slot_of[...] = jnp.broadcast_to(found, (LANES, LANES)).T[0:8]
    to_scalar = pltpu.make_async_copy(slot_of, inv_ref, load_sem.at[6])
    to_scalar.start()
    to_scalar.wait()
    loads[0].wait()
    def scatter(hh):
        for b in range(blocks):
            for q in range(owners):
                for s in range(STREAMS):
                    start = (q * STREAMS + s) * 2 * rows
                    u, off = start // side, start % side
                    to = ((hh * STREAMS + s) * owners + q) * rows
                    at = pl.ds(pl.multiple_of(off + (c if hh == 0 else other) * rows, rows), rows)
                    wide[to : to + rows, b * side : (b + 1) * side] = tiles[
                        inv_ref[0, u * blocks + b], at, :
                    ]

    scatter(1)
    loads[1].wait()

    def wcol(gg):
        return pl.ds(pl.multiple_of(gg * cols, cols), cols)

    def turn(i, j):
        to = ct.at[0, j] if i == 0 else turned.at[i - 1, j]
        to[...] = confidence_of(wide[:, wcol(unum(i, j))]).T
        if i:
            rcopy(to, ct.at[i, j], w_send, w_recv, upeer(i)).start()

    def rhs_pass(hh):
        here = slice(hh * half, (hh + 1) * half)
        return jnp.dot(confidence_of(wide[here, :]), yv[0], preferred_element_type=jnp.float32)

    def stream_pass(k, s):
        here = slice(s * srows, (s + 1) * srows)
        acc = jnp.zeros((srows, rank), jnp.float32)
        for side_of, w_ref in enumerate((wide, ws)):
            for i in range(items // CHUNK):
                at = slice(i * CHUNK, (i + 1) * CHUNK)
                yc = yv[side_of, at, :]
                scores = jnp.dot(xb[k - 1, 0, here, :], yt[side_of, :, at], preferred_element_type=jnp.float32)
                weighted = (scores * w_ref[here, at].astype(jnp.float32)).astype(jnp.bfloat16)
                acc = acc + jnp.dot(weighted, yc, preferred_element_type=jnp.float32)
        return acc

    def last_pass(s):
        here = slice(s * srows, (s + 1) * srows)
        acc = jnp.zeros((srows, LANES), jnp.float32)
        for side_of, w_ref in enumerate((wide, ws)):
            for i in range(items // CHUNK):
                at = slice(i * CHUNK, (i + 1) * CHUNK)
                scores = jnp.dot(
                    xb[ITERS - 1, 0, here, :], yt[side_of, :, at], preferred_element_type=jnp.float32
                )
                prod = scores * (scores * w_ref[here, at].astype(jnp.float32))
                for j in range(CHUNK // LANES):
                    acc = acc + prod[:, j * LANES : (j + 1) * LANES]
        return acc

    def sums_store(accs):
        for q in range(owners):
            mine = jnp.concatenate([acc[q * rows : (q + 1) * rows] for acc in accs], axis=0)
            sums[o, q : q + 1, 0:per] = jnp.sum(mine.T, axis=0, keepdims=True)

    def flip(which):
        for i in range(items // rank):
            at = slice(i * rank, (i + 1) * rank)
            yt[which, :, at] = yv[which, at, :].T

    def owner_device(zo):
        return {"item": zo * 2 + other}

    parts = rb.shape[2]
    prows = rows // parts

    def reduce_start(k, s, total):
        sb[k, s] = total.astype(jnp.bfloat16)
        for t in range(parts):
            for i in range(owners):
                q = jnp.where(z * 2 < nz, owners - 1 - i, i)
                zo = q + low
                part = sb.at[k, s, pl.ds(pl.multiple_of(q * rows + t * prows, prows), prows)]
                to = rb.at[k, s, t, lax.rem(zo - z + nz, nz)]
                rcopy(part, to, b_send.at[s], b_recv.at[s, t], owner_device(zo)).start()

    def reduce_sent(k, s):
        rcopy(sb.at[k, s], sb.at[k, s], b_send.at[s], b_recv.at[s, 0], sib).wait_send()

    def reduce_end(k, s, t):
        arrived(rb.at[k, s, t], b_send.at[s], b_recv.at[s, t], sib)
        total = rb[k, s, t, 0].astype(jnp.float32)
        for j in range(1, nz):
            total = total + rb[k, s, t, j].astype(jnp.float32)
        return total

    def gather_send(k, s, t):
        part = pl.ds(t * prows, prows)
        at = pl.ds(pl.multiple_of(s * srows + place * rows + t * prows, prows), prows)
        for j in zothers + [0]:
            rcopy(
                dn.at[k, s, part], xb.at[k, 0, at], z_send.at[s], z_recv.at[s, place],
                owner_device(lax.rem(z + j, nz)),
            ).start()

    def gather_sent(k, s):
        rcopy(rb.at[k, s], rb.at[k, s], z_send.at[s], z_recv.at[s, 0], sib).wait_send()

    def gather_end(k, s, pass_on):
        for q in range(owners):
            got = xb.at[k, 0, piece(s, q)]
            arrived(got, z_send.at[s], z_recv.at[s, q], sib)
            if pass_on:
                rcopy(got, xb.at[k, 0, piece(s, q, 1)], f_send.at[k], f_recv.at[k + s], sib).start()
                for i in range(1, line):
                    rcopy(got, xb.at[k, i, piece(s, q)], u_send.at[k], u_recv.at[k], upeer(i)).start()
                    rcopy(got, xb.at[k, i, piece(s, q, 1)], u_send.at[k], u_recv.at[k], cross(i)).start()

    mine_all, theirs_all = pl.ds(0, half), pl.ds(half, half)
    away = pl.ds(1, line - 1)

    def basis_send(k):
        mine = xb.at[k, 0, mine_all]
        rcopy(mine, xb.at[k, 0, theirs_all], f_send.at[k], f_recv.at[k], sib).start()
        for i in range(1, line):
            rcopy(mine, xb.at[k, i, mine_all], u_send.at[k], u_recv.at[k], upeer(i)).start()
            rcopy(mine, xb.at[k, i, theirs_all], u_send.at[k], u_recv.at[k], cross(i)).start()

    def basis_end(k):
        arrived(xb.at[k, away], u_send.at[k], u_recv.at[k], sib)

    def basis_sent(k):
        mine, got = xb.at[k, 0, mine_all], xb.at[k, away]
        rcopy(mine, mine, f_send.at[k], f_recv.at[k], sib).wait_send()
        rcopy(got, got, u_send.at[k], u_recv.at[k], sib).wait_send()

    def update(k, s, t):
        at = slice(t * prows, (t + 1) * prows)
        total = reduce_end(k, s, t)
        if k == 0:
            r_state[s, at] = total
            d_state[s, at] = total
            n_state[s, at] = jnp.sum(total * total, axis=1, keepdims=True)
            dn[k, s, at] = total.astype(jnp.bfloat16)
            return
        direction = d_state[s, at]
        image = i_state[s, at] + total
        norm = n_state[s, at]
        alpha = norm / (jnp.sum(direction * image, axis=1, keepdims=True) + epsilon)
        residual = r_state[s, at] - alpha * image
        norm_next = jnp.sum(residual * residual, axis=1, keepdims=True)
        direction_next = residual + norm_next / (norm + epsilon) * direction
        dn[k, s, at] = direction_next.astype(jnp.bfloat16)
        gather_send(k, s, t)
        moved = alpha * direction
        x_state[s, at] = moved if k == 1 else x_state[s, at] + moved
        a_state[k - 1, s, at] = alpha
        r_state[s, at] = residual
        d_state[s, at] = direction_next
        n_state[s, at] = norm_next

    def grams():
        for s in range(STREAMS):
            i_state[s] = jnp.dot(
                d_state[s], gram[...], precision=highest, preferred_element_type=jnp.float32
            )

    def spread(slot, ss, near, far_off):
        def column(t, carry):
            dev = {"item": lax.rem(o + t, ni)}
            rcopy(slot(0), slot(0), ss, near, dev).start()
            return carry

        for e in range(2):
            for t in range(1, line):
                gg = grid(gx + t, gy) if e == 0 else grid(gx, gy + t)

                def across(zz, carry):
                    dev = {"user": gg, "item": lax.rem(z + zz, nz) * 2 + e}
                    rcopy(slot(0), slot(t), ss, far_off, dev).start()
                    return carry

                lax.fori_loop(0, nz, across, 0)
        lax.fori_loop(1, ni, column, 0)

    def spread_end(every, ss, rs):
        rcopy(every, every, ss, rs, sib).wait_send()

    told = (ni - 1) + 2 * (line - 1) * nz

    def scal_slot(t):
        return scal.at[(t * owners + place) * 2 + other]

    def sums_slot(t):
        return sums.at[(t * nz + z) * 2 + c]

    def tell():
        grams()
        lane = lax.broadcasted_iota(jnp.int32, (rows, LANES), 1)
        parts = []
        for s in range(STREAMS):
            turned = jnp.sum(d_state[s] * i_state[s], axis=1, keepdims=True)
            at = jnp.where(lane == 2, n_state[s], turned)
            at = jnp.where(lane == 1, a_state[1, s], at)
            parts.append(jnp.where(lane == 0, a_state[0, s], at))
        scal[place * 2 + other, :, 0:per] = jnp.concatenate(parts, axis=0).T[0:8]
        spread(scal_slot, c_send, c_recv, c_recv)

    def step(k, s):
        for t in range(parts):
            update(k, s, t)
            if k == 0:
                gather_send(k, s, t)

    pa[...] = rhs_pass(1)
    pl.semaphore_wait(barrier, greeted)
    send(pa, ra, a_send, a_recv, sib)
    scatter(0)
    first = rhs_pass(0)
    for s in range(STREAMS):
        own[s] = first[s * srows : (s + 1) * srows]
    send(yv.at[0], yv.at[1], y_send.at[0], y_recv.at[0], sib)
    send(wide.at[theirs_all], ws, y_send.at[1], y_recv.at[1], sib)
    arrived(ra, a_send, a_recv, sib)
    for s in range(STREAMS):
        reduce_start(0, s, own[s] + ra[s * srows : (s + 1) * srows, :])
    for i in range(1, line):
        for j in range(line):
            turn(i, j)
    for j in range(line):
        turn(0, j)
    flip(0)
    loads[2].wait()
    arrived(yv.at[1], y_send.at[0], y_recv.at[0], sib)
    flip(1)
    for s in range(STREAMS):
        pl.when(is_owner)(functools.partial(step, 0, s))
    arrived(ws, y_send.at[1], y_recv.at[1], sib)

    for k in range(1, ITERS):
        for s in range(STREAMS):
            gather_end(k - 1, s, False)
            total = stream_pass(k, s)
            reduce_sent(k - 1, s)
            reduce_start(k, s, total)
        basis_send(k - 1)
        pl.when(is_owner)(grams)
        for s in range(STREAMS):
            pl.when(is_owner)(functools.partial(gather_sent, k - 1, s))
            pl.when(is_owner)(functools.partial(step, k, s))

    pl.when(is_owner)(tell)
    for s in range(STREAMS):
        send_if(is_owner, x_state.at[s], sol_in, o_send.at[s], o_recv, owner_device(place * STREAMS + s))
    k = ITERS - 1

    def last_theirs(s):
        got = xb.at[k, 0, pl.ds(half + s * srows, srows)]
        arrived(got, f_send.at[k], f_recv.at[k + s], sib)

    rowsums = []
    for s in range(STREAMS):
        gather_end(k, s, True)
        rowsums.append(last_pass(s))
    sums_store(rowsums)
    spread(sums_slot, p_send, p_recv.at[0], p_recv.at[1])
    known = line * owners * 2

    @pl.when(is_owner)
    def _():
        arrived(scal.at[pl.ds(0, known - 1)], c_send, c_recv, sib)

    @pl.when(jnp.logical_not(is_owner))
    def _():
        arrived(scal.at[pl.ds(0, known)], c_send, c_recv, sib)

    def cell(v, hh, q):
        return (v * 2 + hh) * owners + q

    def cells(groups):
        for v in groups:
            for hh in range(2):
                for q in range(owners):
                    yield v, hh, q, (c if hh == 0 else other)

    every = range(line)

    def block(v, hh, s, q):
        at = ((hh * STREAMS + s) * owners + q) * rows
        return slice(at, at + rows)

    for v, hh, q, cc in cells(every):
        n = cell(v, hh, q)
        coef[0:4, n, :] = scal[(v * owners + q) * 2 + cc][0:4]
    alpha1, alpha2 = coef[0].T, coef[1].T
    for j in range(k):
        arrived(xb.at[j, 0, theirs_all], f_send.at[j], f_recv.at[j], sib)
        basis_end(j)
    for v, hh, q, cc in cells(every):
        n = cell(v, hh, q)
        for s in range(STREAMS):
            at = block(v, hh, s, q)
            r = slice(s * rows, (s + 1) * rows)
            x2[v, at, :] = alpha1[r, n : n + 1] * xb[0, v, at, :].astype(jnp.float32) + alpha2[
                r, n : n + 1
            ] * xb[1, v, at, :].astype(jnp.float32)

    def alphas(groups):
        for v, hh, q, cc in cells(groups):
            n = cell(v, hh, q)
            total = coef[3, n : n + 1, :]
            for zz in range(nz):
                total = total + sums[(v * nz + zz) * 2 + cc, q : q + 1, :]
            coef[4, n : n + 1, :] = coef[2, n : n + 1, :] / (total + epsilon)
        return coef[4].T

    def final_of(v, alpha):
        parts = []
        for hh in range(2):
            for s in range(STREAMS):
                for q in range(owners):
                    n = cell(v, hh, q)
                    at = block(v, hh, s, q)
                    parts.append(
                        x2[v, at, :]
                        + alpha[s * rows : (s + 1) * rows, n : n + 1] * xb[k, v, at, :].astype(jnp.float32)
                    )
        return jnp.concatenate(parts, axis=0).astype(jnp.bfloat16)

    arrived(sums.at[pl.ds(0, ni - 1)], p_send, p_recv.at[0], sib)
    alpha3 = alphas([0])
    for s in range(STREAMS):
        last_theirs(s)
    final = final_of(0, alpha3)
    for j in range(line):
        kept[j] = jnp.dot(ct[0, j], final, preferred_element_type=jnp.float32)

    arrived(sol_in, o_send.at[0], o_recv, sib)
    for target in range(nz):
        s, q = target % STREAMS, target // STREAMS

        @pl.when(z == target)
        def _():
            n = cell(0, 0, q)
            sol_ref[...] = sol_in[...] + alpha3[s * rows : (s + 1) * rows, n : n + 1] * xb[
                k, 0, block(0, 0, s, q), :
            ].astype(jnp.float32)

    arrived(sums.at[pl.ds(0, (line - 1) * ni)], p_send, p_recv.at[1], sib)
    alpha3 = alphas(range(1, line))
    arrived(ct.at[away], w_send, w_recv, sib)
    basis_end(k)
    finals = [final_of(v, alpha3) for v in range(1, line)]
    for j in list(range(1, line)) + [0]:
        for i in range(PIECES):
            at = slice(i * cols // PIECES, (i + 1) * cols // PIECES)
            total = kept[j, at, :]
            for v in range(1, line):
                total = total + jnp.dot(ct[v, j, at, :], finals[v - 1], preferred_element_type=jnp.float32)
            if j:
                outgo[j - 1, at, :] = total.astype(jnp.bfloat16)
                part = pl.ds(i * cols // PIECES, cols // PIECES)
                rcopy(
                    outgo.at[j - 1, part], income.at[j - 1, part], r_send, r_recv, upeer(0, j)
                ).start()
            else:
                item_ref[at, :] = total
    arrived(income, r_send, r_recv, sib)
    total = item_ref[...]
    for j in range(line - 1):
        total = total + income[j].astype(jnp.float32)
    item_ref[...] = total * scale

    for cond, cp in sent:
        if cond is None:
            cp.wait_send()
        else:
            pl.when(cond)(cp.wait_send)
    for j in range(ITERS):
        basis_sent(j)
    for s in range(STREAMS):
        reduce_sent(k, s)
        pl.when(is_owner)(functools.partial(gather_sent, k, s))
    rcopy(turned, turned, w_send, w_recv, sib).wait_send()
    spread_end(sums.at[pl.ds(0, told)], p_send, p_recv.at[0])
    pl.when(is_owner)(functools.partial(spread_end, scal.at[pl.ds(0, told)], c_send, c_recv))
    rcopy(outgo, outgo, r_send, r_recv, sib).wait_send()


def place_outputs(sol_in, item_in, sol_out, item_out, sem):
    copies = [
        pltpu.make_async_copy(item_in, item_out, sem.at[0]),
        pltpu.make_async_copy(sol_in, sol_out, sem.at[1]),
    ]
    for cp in copies:
        cp.start()
    for cp in copies:
        cp.wait()


def make_local(nu, ni):
    def local(item_factors, item_gram, tile_users, tile_items, tile_counts, tile_values):
        items, rank = item_factors.shape
        slots, side = tile_values.shape[2], tile_values.shape[-1]
        blocks = items // side
        group = USER_BLK * side
        half = group // 2
        rows = group // ni
        nz = ni // 2
        owners = nz // STREAMS
        srows = owners * rows
        cols = items // nu
        scale = float(nu * group) ** -0.5
        bf, f4 = jnp.bfloat16, jnp.float32
        dma = pltpu.SemaphoreType.DMA
        vm = pltpu.VMEM
        line = math.isqrt(nu)
        parts = min(PARTS, rows // 16)
        cells = max(8, line * 2 * owners)
        anywhere = pl.BlockSpec(memory_space=pl.ANY)
        vmem = pl.BlockSpec(memory_space=pltpu.VMEM)
        sol, item = pl.pallas_call(
            functools.partial(kernel, nu, ni, scale),
            out_shape=(vm((rows, rank), f4), vm((cols, rank), f4)),
            in_specs=[anywhere] * 6,
            out_specs=(vmem, vmem),
            scratch_shapes=[
                vm((1, 1, slots), jnp.int32),
                vm((1, 1, slots), jnp.int32),
                vm((1, 1), jnp.int32),
                vm((8, LANES), jnp.int32),
                pltpu.SMEM((8, LANES), jnp.int32),
                vm((slots + 1, side, side), bf),
                vm((2, items, rank), bf),
                vm((2, rank, items), bf),
                vm((rank, rank), f4),
                vm((group, items), bf),
                vm((half, items), bf),
                vm((line - 1, line, cols, group), bf),
                vm((line, line, cols, group), bf),
                vm((ITERS, line, group, rank), bf),
                vm((half, rank), f4),
                vm((half, rank), f4),
                vm((STREAMS, srows, rank), f4),
                vm((ITERS, STREAMS, srows, rank), bf),
                vm((ITERS, STREAMS, parts, nz, rows // parts, rank), bf),
                vm((ITERS, STREAMS, rows, rank), bf),
                vm((STREAMS, rows, rank), f4),
                vm((STREAMS, rows, rank), f4),
                vm((STREAMS, rows, rank), f4),
                vm((STREAMS, rows, 1), f4),
                vm((STREAMS, rows, rank), f4),
                vm((2, STREAMS, rows, 1), f4),
                vm((rows, rank), f4),
                vm((line * ni, 8, LANES), f4),
                vm((line * ni, owners, LANES), f4),
                vm((5, cells, LANES), f4),
                vm((line, group, rank), f4),
                vm((line, cols, rank), f4),
                vm((line - 1, cols, rank), bf),
                vm((line - 1, cols, rank), bf),
                dma((7,)),
                dma(()), dma(()),
                dma(()), dma(()),
                dma((2,)), dma((2,)),
                dma((STREAMS,)), dma((STREAMS, parts)),
                dma((STREAMS,)), dma((STREAMS, owners)),
                dma((ITERS,)), dma((ITERS - 1 + STREAMS,)),
                dma((ITERS,)), dma((ITERS,)),
                dma((STREAMS,)), dma(()),
                dma(()), dma(()), dma(()), dma((2,)),
                dma(()), dma(()),
            ],
            compiler_params=pltpu.CompilerParams(collective_id=0, has_side_effects=True),
        )(tile_users, tile_items, tile_counts, item_factors, item_gram, tile_values.reshape(slots, side, side))
        sol = pltpu.with_memory_space_constraint(sol, pltpu.VMEM)
        item = pltpu.with_memory_space_constraint(item, pltpu.VMEM)
        sol, item = pl.pallas_call(
            place_outputs,
            out_shape=(
                jax.ShapeDtypeStruct((rows, rank), f4),
                jax.ShapeDtypeStruct((cols, rank), f4),
            ),
            in_specs=[vmem, vmem],
            out_specs=(anywhere, anywhere),
            scratch_shapes=[dma((2,))],
        )(sol, item)
        return sol, item[None]

    return local


def solution(mesh):
    return jax.shard_map(
        make_local(mesh.shape["user"], mesh.shape["item"]),
        mesh=mesh,
        in_specs=(
            P("item", None),
            P(),
            P("user", "item", None),
            P("user", "item", None),
            P("user", "item"),
            P("user", "item", None, None, None),
        ),
        out_specs=(P(("user", "item"), None), P("item", "user", None)),
        check_vma=False,
    )
```

```python
import functools
import math

import jax
import jax.numpy as jnp
from jax import lax
from jax.experimental import pallas as pl
from jax.experimental.pallas import tpu as pltpu
from jax.sharding import PartitionSpec as P

USER_BLK = 4
ITERS = 3
CHUNK = 512
STREAMS = 2
PARTS = 2
LANES = 128
PIECES = 4

epsilon = 1e-06
highest = lax.Precision.HIGHEST
MESH = pl.DeviceIdType.MESH


def confidence_of(w):
    return jnp.where(w > 0, 1 + w, jnp.zeros_like(w))


def kernel(
    nu, ni, scale,
    users_hbm, items_hbm, counts_hbm, y_hbm, gram_hbm, tiles_hbm,
    sol_ref, item_ref,
    users_in, items_in, count_in, slot_of, inv_ref, tiles, yv, yt, gram, wide, ws, turned, ct, xb, pa, ra, own, sb, rb, dn,
    d_state, r_state, x_state, n_state, i_state, a_state, sol_in,
    scal, sums, coef, x2, kept, outgo, income,
    load_sem, w_send, w_recv, a_send, a_recv, y_send, y_recv, b_send, b_recv,
    z_send, z_recv, f_send, f_recv, u_send, u_recv, o_send, o_recv,
    c_send, c_recv, p_send, p_recv, r_send, r_recv,
):
    slots, side, _ = tiles_hbm.shape
    items, rank = y_hbm.shape
    group = wide.shape[0]
    half = group // 2
    rows = group // ni
    nz = ni // 2
    owners = nz // STREAMS
    low = (nz - owners) // 2
    srows = owners * rows
    cols = items // nu
    blocks = items // side
    per = STREAMS * rows
    g, o = lax.axis_index("user"), lax.axis_index("item")
    z, c = lax.div(o, 2), lax.rem(o, 2)
    other = 1 - c
    sib = {"item": z * 2 + other}
    place = lax.rem(z - low + nz, owners)
    is_owner = (z >= low) & (z < low + owners)

    line = math.isqrt(nu)
    assert line * line == nu
    gx, gy = lax.rem(g, line), lax.div(g, line)

    def grid(x, y):
        return lax.rem(x, line) + line * lax.rem(y, line)

    def unum(i, j):
        return jnp.where(c == 0, grid(gx + i, gy + j), grid(gx + j, gy + i))

    def far(j, size):
        return min(j, size - j)

    zothers = sorted(range(1, nz), key=lambda j: -far(j, nz))

    def zpeer(j):
        return {"item": lax.rem(z + (j + nz), nz) * 2 + c}

    def upeer(i, j=0):
        return {"user": unum(i, j)}

    def cross(i):
        return {"user": unum(0, i), "item": z * 2 + other}

    def piece(s, q, hh=0):
        at = (hh * STREAMS + s) * srows
        if isinstance(q, int):
            return pl.ds(at + q * rows, rows)
        return pl.ds(pl.multiple_of(at + q * rows, rows), rows)

    sent = []

    def rcopy(src, dst, ss, rs, dev):
        return pltpu.make_async_remote_copy(
            src_ref=src, dst_ref=dst, send_sem=ss, recv_sem=rs, device_id=dev, device_id_type=MESH
        )

    def send(*args):
        cp = rcopy(*args)
        cp.start()
        sent.append((None, cp))

    def send_if(cond, *args):
        cp = rcopy(*args)
        pl.when(cond)(cp.start)
        sent.append((cond, cp))

    def arrived(dst, ss, rs, dev):
        rcopy(dst, dst, ss, rs, dev).wait_recv()

    loads = [
        pltpu.make_async_copy(tiles_hbm, tiles.at[pl.ds(0, slots)], load_sem.at[0]),
        pltpu.make_async_copy(y_hbm, yv.at[0], load_sem.at[1]),
        pltpu.make_async_copy(gram_hbm, gram, load_sem.at[2]),
    ]
    index = [
        pltpu.make_async_copy(users_hbm, users_in, load_sem.at[3]),
        pltpu.make_async_copy(items_hbm, items_in, load_sem.at[4]),
        pltpu.make_async_copy(counts_hbm, count_in, load_sem.at[5]),
    ]
    for cp in index + loads:
        cp.start()

    barrier = pltpu.get_barrier_semaphore()

    def signal(dev):
        pl.semaphore_signal(barrier, inc=1, device_id=dev, device_id_type=MESH)

    def greet(t, carry):
        signal({"item": lax.rem(o + t, ni)})
        return carry

    def greet_line(i, t, carry):
        signal({"user": unum(i, 0), "item": t})
        return carry

    def greet_cross(i, t, carry):
        signal({"user": unum(0, i), "item": t * 2 + other})
        return carry

    lax.fori_loop(1, ni, greet, 0)
    for i in range(1, line):
        lax.fori_loop(0, ni, functools.partial(greet_line, i), 0)
        lax.fori_loop(0, nz, functools.partial(greet_cross, i), 0)
        signal(upeer(0, i))
    greeted = (ni - 1) + (line - 1) * (ni + nz + 1)
    tiles[slots] = jnp.zeros((side, side), jnp.bfloat16)
    for cp in index:
        cp.wait()
    lane = lax.broadcasted_iota(jnp.int32, (1, slots), 1)
    key = jnp.where(lane < count_in[...], users_in[0] * blocks + items_in[0], -1)
    match = lax.broadcasted_iota(jnp.int32, (LANES, slots), 0) == key
    found = jnp.min(jnp.where(match, lane, slots), axis=1, keepdims=True)
    slot_of[...] = jnp.broadcast_to(found, (LANES, LANES)).T[0:8]
    to_scalar = pltpu.make_async_copy(slot_of, inv_ref, load_sem.at[6])
    to_scalar.start()
    to_scalar.wait()
    loads[0].wait()
    def scatter(hh):
        for b in range(blocks):
            for q in range(owners):
                for s in range(STREAMS):
                    start = (q * STREAMS + s) * 2 * rows
                    u, off = start // side, start % side
                    to = ((hh * STREAMS + s) * owners + q) * rows
                    at = pl.ds(pl.multiple_of(off + (c if hh == 0 else other) * rows, rows), rows)
                    wide[to : to + rows, b * side : (b + 1) * side] = tiles[
                        inv_ref[0, u * blocks + b], at, :
                    ]

    scatter(1)
    loads[1].wait()

    def wcol(gg):
        return pl.ds(pl.multiple_of(gg * cols, cols), cols)

    def turn(i, j):
        to = ct.at[0, j] if i == 0 else turned.at[i - 1, j]
        to[...] = confidence_of(wide[:, wcol(unum(i, j))]).T
        if i:
            rcopy(to, ct.at[i, j], w_send, w_recv, upeer(i)).start()

    def rhs_pass(hh):
        here = slice(hh * half, (hh + 1) * half)
        return jnp.dot(confidence_of(wide[here, :]), yv[0], preferred_element_type=jnp.float32)

    def stream_pass(k, s):
        here = slice(s * srows, (s + 1) * srows)
        acc = jnp.zeros((srows, rank), jnp.float32)
        for side_of, w_ref in enumerate((wide, ws)):
            for i in range(items // CHUNK):
                at = slice(i * CHUNK, (i + 1) * CHUNK)
                yc = yv[side_of, at, :]
                scores = jnp.dot(xb[k - 1, 0, here, :], yt[side_of, :, at], preferred_element_type=jnp.float32)
                weighted = (scores * w_ref[here, at].astype(jnp.float32)).astype(jnp.bfloat16)
                acc = acc + jnp.dot(weighted, yc, preferred_element_type=jnp.float32)
        return acc

    def last_pass(s):
        here = slice(s * srows, (s + 1) * srows)
        acc = jnp.zeros((srows, LANES), jnp.float32)
        for side_of, w_ref in enumerate((wide, ws)):
            for i in range(items // CHUNK):
                at = slice(i * CHUNK, (i + 1) * CHUNK)
                scores = jnp.dot(
                    xb[ITERS - 1, 0, here, :], yt[side_of, :, at], preferred_element_type=jnp.float32
                )
                prod = scores * (scores * w_ref[here, at].astype(jnp.float32))
                for j in range(CHUNK // LANES):
                    acc = acc + prod[:, j * LANES : (j + 1) * LANES]
        return acc

    def sums_store(accs):
        for q in range(owners):
            mine = jnp.concatenate([acc[q * rows : (q + 1) * rows] for acc in accs], axis=0)
            sums[o, q : q + 1, 0:per] = jnp.sum(mine.T, axis=0, keepdims=True)

    def flip(which):
        for i in range(items // rank):
            at = slice(i * rank, (i + 1) * rank)
            yt[which, :, at] = yv[which, at, :].T

    def owner_device(zo):
        return {"item": zo * 2 + other}

    parts = rb.shape[2]
    prows = rows // parts

    def reduce_start(k, s, total):
        sb[k, s] = total.astype(jnp.bfloat16)
        for t in range(parts):
            for i in range(owners):
                q = jnp.where(z * 2 < nz, owners - 1 - i, i)
                zo = q + low
                part = sb.at[k, s, pl.ds(pl.multiple_of(q * rows + t * prows, prows), prows)]
                to = rb.at[k, s, t, lax.rem(zo - z + nz, nz)]
                rcopy(part, to, b_send.at[s], b_recv.at[s, t], owner_device(zo)).start()

    def reduce_sent(k, s):
        rcopy(sb.at[k, s], sb.at[k, s], b_send.at[s], b_recv.at[s, 0], sib).wait_send()

    def reduce_end(k, s, t):
        arrived(rb.at[k, s, t], b_send.at[s], b_recv.at[s, t], sib)
        total = rb[k, s, t, 0].astype(jnp.float32)
        for j in range(1, nz):
            total = total + rb[k, s, t, j].astype(jnp.float32)
        return total

    def gather_send(k, s, t):
        part = pl.ds(t * prows, prows)
        at = pl.ds(pl.multiple_of(s * srows + place * rows + t * prows, prows), prows)
        for j in zothers + [0]:
            rcopy(
                dn.at[k, s, part], xb.at[k, 0, at], z_send.at[s], z_recv.at[s, place],
                owner_device(lax.rem(z + j, nz)),
            ).start()

    def gather_sent(k, s):
        rcopy(rb.at[k, s], rb.at[k, s], z_send.at[s], z_recv.at[s, 0], sib).wait_send()

    def gather_end(k, s, pass_on):
        for q in range(owners):
            got = xb.at[k, 0, piece(s, q)]
            arrived(got, z_send.at[s], z_recv.at[s, q], sib)
            if pass_on:
                rcopy(got, xb.at[k, 0, piece(s, q, 1)], f_send.at[k], f_recv.at[k + s], sib).start()
                for i in range(1, line):
                    rcopy(got, xb.at[k, i, piece(s, q)], u_send.at[k], u_recv.at[k], upeer(i)).start()
                    rcopy(got, xb.at[k, i, piece(s, q, 1)], u_send.at[k], u_recv.at[k], cross(i)).start()

    mine_all, theirs_all = pl.ds(0, half), pl.ds(half, half)
    away = pl.ds(1, line - 1)

    def basis_send(k):
        mine = xb.at[k, 0, mine_all]
        rcopy(mine, xb.at[k, 0, theirs_all], f_send.at[k], f_recv.at[k], sib).start()
        for i in range(1, line):
            rcopy(mine, xb.at[k, i, mine_all], u_send.at[k], u_recv.at[k], upeer(i)).start()
            rcopy(mine, xb.at[k, i, theirs_all], u_send.at[k], u_recv.at[k], cross(i)).start()

    def basis_end(k):
        arrived(xb.at[k, away], u_send.at[k], u_recv.at[k], sib)

    def basis_sent(k):
        mine, got = xb.at[k, 0, mine_all], xb.at[k, away]
        rcopy(mine, mine, f_send.at[k], f_recv.at[k], sib).wait_send()
        rcopy(got, got, u_send.at[k], u_recv.at[k], sib).wait_send()

    def update(k, s, t):
        at = slice(t * prows, (t + 1) * prows)
        total = reduce_end(k, s, t)
        if k == 0:
            r_state[s, at] = total
            d_state[s, at] = total
            n_state[s, at] = jnp.sum(total * total, axis=1, keepdims=True)
            dn[k, s, at] = total.astype(jnp.bfloat16)
            return
        direction = d_state[s, at]
        image = i_state[s, at] + total
        norm = n_state[s, at]
        alpha = norm / (jnp.sum(direction * image, axis=1, keepdims=True) + epsilon)
        residual = r_state[s, at] - alpha * image
        norm_next = jnp.sum(residual * residual, axis=1, keepdims=True)
        direction_next = residual + norm_next / (norm + epsilon) * direction
        dn[k, s, at] = direction_next.astype(jnp.bfloat16)
        gather_send(k, s, t)
        moved = alpha * direction
        x_state[s, at] = moved if k == 1 else x_state[s, at] + moved
        a_state[k - 1, s, at] = alpha
        r_state[s, at] = residual
        d_state[s, at] = direction_next
        n_state[s, at] = norm_next

    def grams():
        for s in range(STREAMS):
            i_state[s] = jnp.dot(
                d_state[s], gram[...], precision=highest, preferred_element_type=jnp.float32
            )

    def spread(slot, ss, near, far_off):
        def column(t, carry):
            dev = {"item": lax.rem(o + t, ni)}
            rcopy(slot(0), slot(0), ss, near, dev).start()
            return carry

        for e in range(2):
            for t in range(1, line):
                gg = grid(gx + t, gy) if e == 0 else grid(gx, gy + t)

                def across(zz, carry):
                    dev = {"user": gg, "item": lax.rem(z + zz, nz) * 2 + e}
                    rcopy(slot(0), slot(t), ss, far_off, dev).start()
                    return carry

                lax.fori_loop(0, nz, across, 0)
        lax.fori_loop(1, ni, column, 0)

    def spread_end(every, ss, rs):
        rcopy(every, every, ss, rs, sib).wait_send()

    told = (ni - 1) + 2 * (line - 1) * nz

    def scal_slot(t):
        return scal.at[(t * owners + place) * 2 + other]

    def sums_slot(t):
        return sums.at[(t * nz + z) * 2 + c]

    def tell():
        grams()
        lane = lax.broadcasted_iota(jnp.int32, (rows, LANES), 1)
        parts = []
        for s in range(STREAMS):
            turned = jnp.sum(d_state[s] * i_state[s], axis=1, keepdims=True)
            at = jnp.where(lane == 2, n_state[s], turned)
            at = jnp.where(lane == 1, a_state[1, s], at)
            parts.append(jnp.where(lane == 0, a_state[0, s], at))
        scal[place * 2 + other, :, 0:per] = jnp.concatenate(parts, axis=0).T[0:8]
        spread(scal_slot, c_send, c_recv, c_recv)

    def step(k, s):
        for t in range(parts):
            update(k, s, t)
            if k == 0:
                gather_send(k, s, t)

    pa[...] = rhs_pass(1)
    pl.semaphore_wait(barrier, greeted)
    for s in range(STREAMS):
        here = pl.ds(s * srows, srows)
        send(pa.at[here], ra.at[here], a_send.at[s], a_recv.at[s], sib)
    scatter(0)
    first = rhs_pass(0)
    for s in range(STREAMS):
        own[s] = first[s * srows : (s + 1) * srows]
    send(yv.at[0], yv.at[1], y_send.at[0], y_recv.at[0], sib)
    send(wide.at[theirs_all], ws, y_send.at[1], y_recv.at[1], sib)
    for s in range(STREAMS):
        arrived(ra.at[pl.ds(s * srows, srows)], a_send.at[s], a_recv.at[s], sib)
        reduce_start(0, s, own[s] + ra[s * srows : (s + 1) * srows, :])
    for i in range(1, line):
        for j in range(line):
            turn(i, j)
    for j in range(line):
        turn(0, j)
    flip(0)
    loads[2].wait()
    arrived(yv.at[1], y_send.at[0], y_recv.at[0], sib)
    flip(1)
    for s in range(STREAMS):
        pl.when(is_owner)(functools.partial(step, 0, s))
    arrived(ws, y_send.at[1], y_recv.at[1], sib)

    for k in range(1, ITERS):
        for s in range(STREAMS):
            gather_end(k - 1, s, False)
            total = stream_pass(k, s)
            reduce_sent(k - 1, s)
            reduce_start(k, s, total)
        basis_send(k - 1)
        pl.when(is_owner)(grams)
        for s in range(STREAMS):
            pl.when(is_owner)(functools.partial(gather_sent, k - 1, s))
            pl.when(is_owner)(functools.partial(step, k, s))

    pl.when(is_owner)(tell)
    for s in range(STREAMS):
        send_if(is_owner, x_state.at[s], sol_in, o_send.at[s], o_recv, owner_device(place * STREAMS + s))
    k = ITERS - 1

    def last_theirs(s):
        got = xb.at[k, 0, pl.ds(half + s * srows, srows)]
        arrived(got, f_send.at[k], f_recv.at[k + s], sib)

    rowsums = []
    for s in range(STREAMS):
        gather_end(k, s, True)
        rowsums.append(last_pass(s))
    sums_store(rowsums)
    spread(sums_slot, p_send, p_recv.at[0], p_recv.at[1])
    known = line * owners * 2

    @pl.when(is_owner)
    def _():
        arrived(scal.at[pl.ds(0, known - 1)], c_send, c_recv, sib)

    @pl.when(jnp.logical_not(is_owner))
    def _():
        arrived(scal.at[pl.ds(0, known)], c_send, c_recv, sib)

    def cell(v, hh, q):
        return (v * 2 + hh) * owners + q

    def cells(groups):
        for v in groups:
            for hh in range(2):
                for q in range(owners):
                    yield v, hh, q, (c if hh == 0 else other)

    every = range(line)

    def block(v, hh, s, q):
        at = ((hh * STREAMS + s) * owners + q) * rows
        return slice(at, at + rows)

    for v, hh, q, cc in cells(every):
        n = cell(v, hh, q)
        coef[0:4, n, :] = scal[(v * owners + q) * 2 + cc][0:4]
    alpha1, alpha2 = coef[0].T, coef[1].T
    for j in range(k):
        arrived(xb.at[j, 0, theirs_all], f_send.at[j], f_recv.at[j], sib)
        basis_end(j)
    for v, hh, q, cc in cells(every):
        n = cell(v, hh, q)
        for s in range(STREAMS):
            at = block(v, hh, s, q)
            r = slice(s * rows, (s + 1) * rows)
            x2[v, at, :] = alpha1[r, n : n + 1] * xb[0, v, at, :].astype(jnp.float32) + alpha2[
                r, n : n + 1
            ] * xb[1, v, at, :].astype(jnp.float32)

    def alphas(groups):
        for v, hh, q, cc in cells(groups):
            n = cell(v, hh, q)
            total = coef[3, n : n + 1, :]
            for zz in range(nz):
                total = total + sums[(v * nz + zz) * 2 + cc, q : q + 1, :]
            coef[4, n : n + 1, :] = coef[2, n : n + 1, :] / (total + epsilon)
        return coef[4].T

    def final_of(v, alpha):
        parts = []
        for hh in range(2):
            for s in range(STREAMS):
                for q in range(owners):
                    n = cell(v, hh, q)
                    at = block(v, hh, s, q)
                    parts.append(
                        x2[v, at, :]
                        + alpha[s * rows : (s + 1) * rows, n : n + 1] * xb[k, v, at, :].astype(jnp.float32)
                    )
        return jnp.concatenate(parts, axis=0).astype(jnp.bfloat16)

    arrived(sums.at[pl.ds(0, ni - 1)], p_send, p_recv.at[0], sib)
    alpha3 = alphas([0])
    for s in range(STREAMS):
        last_theirs(s)
    final = final_of(0, alpha3)
    for j in range(line):
        kept[j] = jnp.dot(ct[0, j], final, preferred_element_type=jnp.float32)

    arrived(sol_in, o_send.at[0], o_recv, sib)
    for target in range(nz):
        s, q = target % STREAMS, target // STREAMS

        @pl.when(z == target)
        def _():
            n = cell(0, 0, q)
            sol_ref[...] = sol_in[...] + alpha3[s * rows : (s + 1) * rows, n : n + 1] * xb[
                k, 0, block(0, 0, s, q), :
            ].astype(jnp.float32)

    arrived(sums.at[pl.ds(0, (line - 1) * ni)], p_send, p_recv.at[1], sib)
    alpha3 = alphas(range(1, line))
    arrived(ct.at[away], w_send, w_recv, sib)
    basis_end(k)
    finals = [final_of(v, alpha3) for v in range(1, line)]
    for j in list(range(1, line)) + [0]:
        for i in range(PIECES):
            at = slice(i * cols // PIECES, (i + 1) * cols // PIECES)
            total = kept[j, at, :]
            for v in range(1, line):
                total = total + jnp.dot(ct[v, j, at, :], finals[v - 1], preferred_element_type=jnp.float32)
            if j:
                outgo[j - 1, at, :] = total.astype(jnp.bfloat16)
                part = pl.ds(i * cols // PIECES, cols // PIECES)
                rcopy(
                    outgo.at[j - 1, part], income.at[j - 1, part], r_send, r_recv, upeer(0, j)
                ).start()
            else:
                item_ref[at, :] = total
    arrived(income, r_send, r_recv, sib)
    total = item_ref[...]
    for j in range(line - 1):
        total = total + income[j].astype(jnp.float32)
    item_ref[...] = total * scale

    for cond, cp in sent:
        if cond is None:
            cp.wait_send()
        else:
            pl.when(cond)(cp.wait_send)
    for j in range(ITERS):
        basis_sent(j)
    for s in range(STREAMS):
        reduce_sent(k, s)
        pl.when(is_owner)(functools.partial(gather_sent, k, s))
    rcopy(turned, turned, w_send, w_recv, sib).wait_send()
    spread_end(sums.at[pl.ds(0, told)], p_send, p_recv.at[0])
    pl.when(is_owner)(functools.partial(spread_end, scal.at[pl.ds(0, told)], c_send, c_recv))
    rcopy(outgo, outgo, r_send, r_recv, sib).wait_send()


def place_outputs(sol_in, item_in, sol_out, item_out, sem):
    copies = [
        pltpu.make_async_copy(item_in, item_out, sem.at[0]),
        pltpu.make_async_copy(sol_in, sol_out, sem.at[1]),
    ]
    for cp in copies:
        cp.start()
    for cp in copies:
        cp.wait()


def make_local(nu, ni):
    def local(item_factors, item_gram, tile_users, tile_items, tile_counts, tile_values):
        items, rank = item_factors.shape
        slots, side = tile_values.shape[2], tile_values.shape[-1]
        blocks = items // side
        group = USER_BLK * side
        half = group // 2
        rows = group // ni
        nz = ni // 2
        owners = nz // STREAMS
        srows = owners * rows
        cols = items // nu
        scale = float(nu * group) ** -0.5
        bf, f4 = jnp.bfloat16, jnp.float32
        dma = pltpu.SemaphoreType.DMA
        vm = pltpu.VMEM
        line = math.isqrt(nu)
        parts = min(PARTS, rows // 16)
        cells = max(8, line * 2 * owners)
        anywhere = pl.BlockSpec(memory_space=pl.ANY)
        vmem = pl.BlockSpec(memory_space=pltpu.VMEM)
        sol, item = pl.pallas_call(
            functools.partial(kernel, nu, ni, scale),
            out_shape=(vm((rows, rank), f4), vm((cols, rank), f4)),
            in_specs=[anywhere] * 6,
            out_specs=(vmem, vmem),
            scratch_shapes=[
                vm((1, 1, slots), jnp.int32),
                vm((1, 1, slots), jnp.int32),
                vm((1, 1), jnp.int32),
                vm((8, LANES), jnp.int32),
                pltpu.SMEM((8, LANES), jnp.int32),
                vm((slots + 1, side, side), bf),
                vm((2, items, rank), bf),
                vm((2, rank, items), bf),
                vm((rank, rank), f4),
                vm((group, items), bf),
                vm((half, items), bf),
                vm((line - 1, line, cols, group), bf),
                vm((line, line, cols, group), bf),
                vm((ITERS, line, group, rank), bf),
                vm((half, rank), f4),
                vm((half, rank), f4),
                vm((STREAMS, srows, rank), f4),
                vm((ITERS, STREAMS, srows, rank), bf),
                vm((ITERS, STREAMS, parts, nz, rows // parts, rank), bf),
                vm((ITERS, STREAMS, rows, rank), bf),
                vm((STREAMS, rows, rank), f4),
                vm((STREAMS, rows, rank), f4),
                vm((STREAMS, rows, rank), f4),
                vm((STREAMS, rows, 1), f4),
                vm((STREAMS, rows, rank), f4),
                vm((2, STREAMS, rows, 1), f4),
                vm((rows, rank), f4),
                vm((line * ni, 8, LANES), f4),
                vm((line * ni, owners, LANES), f4),
                vm((5, cells, LANES), f4),
                vm((line, group, rank), f4),
                vm((line, cols, rank), f4),
                vm((line - 1, cols, rank), bf),
                vm((line - 1, cols, rank), bf),
                dma((7,)),
                dma(()), dma(()),
                dma((STREAMS,)), dma((STREAMS,)),
                dma((2,)), dma((2,)),
                dma((STREAMS,)), dma((STREAMS, parts)),
                dma((STREAMS,)), dma((STREAMS, owners)),
                dma((ITERS,)), dma((ITERS - 1 + STREAMS,)),
                dma((ITERS,)), dma((ITERS,)),
                dma((STREAMS,)), dma(()),
                dma(()), dma(()), dma(()), dma((2,)),
                dma(()), dma(()),
            ],
            compiler_params=pltpu.CompilerParams(collective_id=0, has_side_effects=True),
        )(tile_users, tile_items, tile_counts, item_factors, item_gram, tile_values.reshape(slots, side, side))
        sol = pltpu.with_memory_space_constraint(sol, pltpu.VMEM)
        item = pltpu.with_memory_space_constraint(item, pltpu.VMEM)
        sol, item = pl.pallas_call(
            place_outputs,
            out_shape=(
                jax.ShapeDtypeStruct((rows, rank), f4),
                jax.ShapeDtypeStruct((cols, rank), f4),
            ),
            in_specs=[vmem, vmem],
            out_specs=(anywhere, anywhere),
            scratch_shapes=[dma((2,))],
        )(sol, item)
        return sol, item[None]

    return local


def solution(mesh):
    return jax.shard_map(
        make_local(mesh.shape["user"], mesh.shape["item"]),
        mesh=mesh,
        in_specs=(
            P("item", None),
            P(),
            P("user", "item", None),
            P("user", "item", None),
            P("user", "item"),
            P("user", "item", None, None, None),
        ),
        out_specs=(P(("user", "item"), None), P("item", "user", None)),
        check_vma=False,
    )
```
